32 devices in a mesh: zx: 2 (over x), zy: 16 (over z, y, core).
Axes of the slice: x: 2, y: 2, z: 4, core: 2. Of those that a mesh axis runs over, the one named last changes fastest.
Arguments:
- frac: float32 [8, 128, 4096], P(None, 'zx', 'zy'), may hold values from 0 to 1, as said below
- density: float32 [8, 128, 4096], P(None, 'zx', 'zy'), may hold values from 0.5 to 4
- energy: float32 [8, 128, 4096], P(None, 'zx', 'zy'), may hold values from 0.5 to 2
- node_shift: float32 [2, 128, 4096], P(None, 'zx', 'zy'), may hold values from -0.15 to 0.15
- node_speed: float32 [2, 128, 4096], P(None, 'zx', 'zy'), may hold values from -1 to 1
- dest_tile: int32 [2, 16, 256, 1], P('zx', 'zy'), may hold values from 0 to 31; in each aligned block of 256 rows (0 to 255, 256 to 511, ..., all dimensions but the last counted through in order) at most 16 rows name the same one
- src_block: int32 [2, 16, 256], P('zx', 'zy'), may hold values from 0 to 127
- dest_block: int32 [2, 16, 256], P('zx', 'zy'), may hold values from 0 to 127
- crossing: float32 [2, 16, 256], P('zx', 'zy'), may hold values from 0.1 to 0.6
- keep: float32 [2, 16, 128], P('zx', 'zy'), may hold values from 0.3 to 0.9
Outputs:
- remapped: float32 [3, 8, 128, 4096], P(None, None, 'zx', 'zy')
- speed_after: float32 [2, 128, 4096], P(None, 'zx', 'zy')
- shift_after: float32 [2, 128, 4096], P(None, 'zx', 'zy')
The draws below stay inside these ranges and needn't reach their ends.
Inputs may be any that keep to these rules, and one draw needn't show every extreme that they name: `frac`: at each zone the 8 fractions are positive and sum to one. `dest_tile`: devices are numbered a 16 + b; among the entries of one device at most 16 name the same destination device.
All inputs are finite; a program needn't handle non-finite values.
Results may differ from the reference program's by a relative error of at most 0.00002.
Values sent between devices are 32-bit elements; how exact they have to be, the bound alone decides.
No kernel may reach another device: no remote copies, remote signals or barrier semaphores. Data moves between devices by JAX's collectives and lax.ppermute only.
A program may use at most 64 MiB of HBM per device.

```python
import math
import jax
import jax.numpy as jnp
import numpy as np
from jax import lax

CX = 64
CY = 256
M = 8
BLOCK = 128
NB = 128
ENTRIES = 256
CAP = 16
NX = 128
NY = 4096
N_ZX = 2
N_ZY = 16
DEVICES = 32


def draw_frac(key, part):
    raw_values = jax.random.uniform(jax.random.fold_in(key, 11), (M, NX, NY), jnp.float32, 0.02, 1.0)
    shaped = raw_values * raw_values * raw_values
    return shaped / jnp.sum(shaped, axis=0, keepdims=True)


def plant(drawn, stream_key, smallest, top_value):
    shape = drawn.shape
    index_at = [jax.random.randint(jax.random.fold_in(stream_key, axis), (), 0, shape[axis]) for axis in range(len(shape))]
    drawn = drawn.at[tuple(index_at)].set(smallest)
    longest = shape.index(max(shape))
    index_at[longest] = (index_at[longest] + 1) % shape[longest]
    return drawn.at[tuple(index_at)].set(top_value)


def steps_of(own_key, dims, cuts, low, top_value):
    def one(dim, shards_of):
        steps = jax.random.uniform(jax.random.fold_in(jax.random.fold_in(own_key, 6), dim), (shards_of,), jnp.float32, low / len(cuts), top_value / len(cuts))
        return jnp.repeat(jnp.exp(steps), dims[dim] // shards_of).reshape((-1,) + (1,) * (len(dims) - dim - 1))

    gain = one(*cuts[0])
    for cut in cuts[1:]:
        gain = gain * one(*cut)
    return gain


def deal_out(rng, own, number, rows, amount, top, reach, skew):
    order = jax.random.permutation(rng, amount)
    packed, ordinary = portions_of(amount, rows * top, reach, skew, True), portions_of(amount, rows * top, reach, skew, False)
    places = jnp.arange(amount)

    def named(tallies, turn):
        used = int((tallies > 0).sum())
        fixed = max(1, used // 4)
        passed = fixed + (places - fixed + turn * (used - fixed)) % max(1, amount - fixed)
        return jnp.zeros((amount,), jnp.int32).at[order[jnp.where(places < fixed, places, passed)]].set(jnp.asarray(tallies, jnp.int32))

    tallies = jnp.where(number % 4 == 0, named(packed, number // 4), named(ordinary, number - number // 4 - 1))
    mixed = jax.random.permutation(jax.random.fold_in(own, 3), amount)
    donor, taker = mixed[0:amount // 2 * 2:2], mixed[1:amount // 2 * 2:2]
    room = jnp.minimum(tallies[donor] - 1, reach - tallies[taker]) // 2
    room = jnp.where((donor == order[0]) | (taker == order[0]) | (tallies[taker] == 0), 0, jnp.maximum(room, 0))
    passed = jax.random.randint(jax.random.fold_in(own, 4), (amount // 2,), 0, 1 << 20) % (room + 1)
    tallies = tallies.at[donor].add(-passed).at[taker].add(passed)
    labels = jnp.searchsorted(jnp.cumsum(tallies), jnp.arange(rows * top), side="right").astype(jnp.int32)
    grid = labels.reshape(top, rows).T
    grid = grid[jax.random.permutation(jax.random.fold_in(own, 1), rows)]
    turn = jax.random.randint(jax.random.fold_in(own, 2), (rows, 1), 0, top)
    return jnp.take_along_axis(grid, (jnp.arange(top)[None, :] + turn) % top, axis=1)


def portions_of(number_of, total, bound, lean, full):
    loads = [(1 << 20) // math.isqrt(rank ** lean) + 1 for rank in range(1, number_of + 1)]
    largest = bound if full else min(bound, max(-(-total // number_of), total * loads[0] // sum(loads)))
    least = 1 if total - largest >= number_of - 1 else 0
    given, spare = [largest] + [least] * (number_of - 1), total - largest - least * (number_of - 1)
    while spare > 0:
        free = [i for i in range(1, number_of) if given[i] < largest] or [i for i in range(1, number_of) if given[i] < bound]
        whole, left = sum([loads[i] for i in free]), spare
        for i in free:
            addition = min(bound - given[i], max(1, left * loads[i] // whole), spare)
            given[i] = given[i] + addition
            spare = spare - addition
    return np.array(given)


def setup_inputs(seed: int = 0) -> dict:
    seeds = jax.random.split(jax.random.key(seed), 11)
    frac = draw_frac(jax.random.fold_in(seeds[10], 71), 0)
    density = jnp.clip(jnp.exp(math.log(4.0) - 2.0794415 * jax.random.uniform(seeds[1], (M, NX, NY), jnp.float32) ** steps_of(seeds[1], (M, NX, NY), ((1, 2), (2, 16)), -0.2, 0.2)), 0.5, 4.0)
    energy = jnp.clip(jnp.exp(math.log(2.0) - 1.3862944 * jax.random.uniform(seeds[2], (M, NX, NY), jnp.float32) ** steps_of(seeds[2], (M, NX, NY), ((1, 2), (2, 16)), -0.2, 0.2)), 0.5, 2.0)
    node_shift = jnp.clip(jax.random.uniform(seeds[3], (2, NX, NY), jnp.float32, -0.15, 0.15) * steps_of(seeds[3], (2, NX, NY), ((1, 2), (2, 16)), -0.4, 0.0), -0.15, 0.15)
    node_speed = jnp.clip(jax.random.uniform(seeds[4], (2, NX, NY), jnp.float32, -1.0, 1.0) * steps_of(seeds[4], (2, NX, NY), ((1, 2), (2, 16)), -0.4, 0.0), -1.0, 1.0)
    dest_tile_keys = jax.random.split(jax.random.fold_in(seeds[5], 1), N_ZX * N_ZY * ENTRIES // ENTRIES)
    dest_tile_turns = jax.random.permutation(jax.random.fold_in(seeds[5], 3), N_ZX * N_ZY * ENTRIES // ENTRIES)
    dest_tile = jax.vmap(lambda own, number: deal_out(jax.random.fold_in(seeds[5], 2), own, number, ENTRIES, DEVICES, 1, CAP, 2))(dest_tile_keys, dest_tile_turns).reshape((N_ZX, N_ZY, ENTRIES, 1))
    src_block = plant(jax.random.randint(seeds[6], (N_ZX, N_ZY, ENTRIES), 0, NB), jax.random.fold_in(seeds[6], 1), 0, NB - 1).astype(jnp.int32)
    dest_block = plant(jax.random.randint(seeds[7], (N_ZX, N_ZY, ENTRIES), 0, NB), jax.random.fold_in(seeds[7], 1), 0, NB - 1).astype(jnp.int32)
    crossing = jnp.clip(0.1 + 0.5 * jax.random.uniform(seeds[8], (N_ZX, N_ZY, ENTRIES), jnp.float32) ** steps_of(seeds[8], (N_ZX, N_ZY, ENTRIES), ((0, 2), (1, 16)), -0.2, 0.2), 0.1, 0.6)
    keep = jnp.clip(0.3 + 0.59999996 * jax.random.uniform(seeds[9], (N_ZX, N_ZY, NB), jnp.float32) ** steps_of(seeds[9], (N_ZX, N_ZY, NB), ((0, 2), (1, 16)), -0.2, 0.2), 0.3, 0.9)
    return {"frac": frac, "density": density, "energy": energy, "node_shift": node_shift, "node_speed": node_speed, "dest_tile": dest_tile, "src_block": src_block, "dest_block": dest_block, "crossing": crossing, "keep": keep}


TIME_STEP = 0.02
VISC_COEF = 0.25


def corner_geometry(corners):
    corner_one, corner_two, corner_three, corner_four = corners
    rise_x = 1.0 + corner_three[0] - corner_one[0]
    rise_y = 1.0 + corner_three[1] - corner_one[1]
    cross_x = -1.0 + corner_four[0] - corner_two[0]
    cross_y = 1.0 + corner_four[1] - corner_two[1]
    return rise_x, rise_y, cross_x, cross_y


def zone_area(corners):
    rise_x, rise_y, cross_x, cross_y = corner_geometry(corners)
    return 0.5 * (rise_x * cross_y - cross_x * rise_y)


def zone_phase(frac, density, energy, shifts, speeds):
    rise_x, rise_y, cross_x, cross_y = corner_geometry(shifts)
    area_now = 0.5 * (rise_x * cross_y - cross_x * rise_y)
    speed_one, speed_two, speed_three, speed_four = speeds
    area_rate = 0.5 * ((speed_three[0] - speed_one[0]) * cross_y + rise_x * (speed_four[1] - speed_two[1])
                       - (speed_four[0] - speed_two[0]) * rise_y - cross_x * (speed_three[1] - speed_one[1]))
    squeeze = jnp.minimum(area_rate / area_now, 0.0)
    gammas = (1.3 + 0.05 * jnp.arange(frac.shape[0], dtype=jnp.int32).astype(jnp.float32))[:, None, None]
    mat_pressure = (gammas - 1.0) * density * energy
    zone_density = jnp.sum(frac * density, axis=0)
    viscous = VISC_COEF * zone_density * area_now * squeeze * squeeze
    total_pressure = jnp.sum(frac * mat_pressure, axis=0) + viscous
    half_press = 0.5 * total_pressure
    quarter_mass = 0.25 * zone_density * area_now
    term_one = jnp.stack([-half_press * cross_y, half_press * cross_x, quarter_mass])
    term_two = jnp.stack([half_press * rise_y, -half_press * rise_x, quarter_mass])
    term_three = jnp.stack([half_press * cross_y, -half_press * cross_x, quarter_mass])
    term_four = jnp.stack([-half_press * rise_y, half_press * rise_x, quarter_mass])
    return area_now, mat_pressure, viscous, (term_one, term_two, term_three, term_four)


def node_update(totals, node_shift, node_speed):
    accel_xy = totals[0:2] / totals[2:3]
    speed_after = node_speed + TIME_STEP * accel_xy
    shift_after = node_shift + TIME_STEP * speed_after
    return speed_after, shift_after


def material_state(frac, density, energy, area_now, area_after, mat_pressure, viscous):
    energy_after = energy - (mat_pressure + viscous) * (area_after - area_now) / (density * area_now)
    volume = frac * area_after
    mass_now = frac * density * area_now
    return jnp.stack([volume, mass_now, mass_now * energy_after])


def rolled_corners(values):
    return (values, jnp.roll(values, -1, 1), jnp.roll(values, (-1, -1), (1, 2)), jnp.roll(values, -1, 2))


def reference(frac, density, energy, node_shift, node_speed, dest_tile, src_block, dest_block, crossing, keep):
    area_now, mat_pressure, viscous, terms = zone_phase(frac, density, energy, rolled_corners(node_shift), rolled_corners(node_speed))
    term_one, term_two, term_three, term_four = terms
    totals = term_one + jnp.roll(term_two, 1, 1) + jnp.roll(term_three, (1, 1), (1, 2)) + jnp.roll(term_four, 1, 2)
    speed_after, shift_after = node_update(totals, node_shift, node_speed)
    area_after = zone_area(rolled_corners(shift_after))
    conserved = material_state(frac, density, energy, area_now, area_after, mat_pressure, viscous)
    fields = 3 * M
    blocks = conserved.reshape(fields, N_ZX, CX, N_ZY, CY).transpose(0, 1, 3, 2, 4).reshape(fields, N_ZX * N_ZY * NB, BLOCK)
    start = blocks * keep.reshape(N_ZX * N_ZY * NB)[None, :, None]

    def accumulate(carry, inputs):
        row_index, targets, sources, places, weights = inputs
        device_ids = row_index * N_ZY + jnp.arange(N_ZY, dtype=jnp.int32)
        global_src = (device_ids[:, None] * NB + sources).reshape(-1)
        global_dst = (targets * NB + places).reshape(-1)
        contrib = blocks[:, global_src, :] * weights.reshape(-1)[None, :, None]
        return carry.at[:, global_dst, :].add(contrib), None

    result, unused = lax.scan(accumulate, start, (jnp.arange(N_ZX, dtype=jnp.int32), dest_tile[..., 0], src_block, dest_block, crossing))
    remapped = result.reshape(fields, N_ZX, N_ZY, CX, CY).transpose(0, 1, 3, 2, 4).reshape(3, M, NX, NY)
    return remapped, speed_after, shift_after
```

```python
import jax
import jax.numpy as jnp
import numpy as np
from jax import lax
from jax.experimental import pallas as pl
from jax.experimental.pallas import tpu as pltpu
from jax.sharding import PartitionSpec as P

TIME_STEP = 0.02
VISC_COEF = 0.25


def shifted(value, axis, by):
    peers = lax.axis_size(axis)
    return lax.ppermute(value, axis, [(i, (i + by) % peers) for i in range(peers)])


def corner_geometry(corners):
    corner_one, corner_two, corner_three, corner_four = corners
    rise_x = 1.0 + corner_three[0] - corner_one[0]
    rise_y = 1.0 + corner_three[1] - corner_one[1]
    cross_x = -1.0 + corner_four[0] - corner_two[0]
    cross_y = 1.0 + corner_four[1] - corner_two[1]
    return (rise_x, rise_y, cross_x, cross_y)


def zone_area(corners):
    rise_x, rise_y, cross_x, cross_y = corner_geometry(corners)
    return 0.5 * (rise_x * cross_y - cross_x * rise_y)


def zone_phase(frac, density, energy, shifts, speeds):
    rise_x, rise_y, cross_x, cross_y = corner_geometry(shifts)
    area_now = 0.5 * (rise_x * cross_y - cross_x * rise_y)
    speed_one, speed_two, speed_three, speed_four = speeds
    area_rate = 0.5 * (
        (speed_three[0] - speed_one[0]) * cross_y
        + rise_x * (speed_four[1] - speed_two[1])
        - (speed_four[0] - speed_two[0]) * rise_y
        - cross_x * (speed_three[1] - speed_one[1])
    )
    squeeze = jnp.minimum(area_rate / area_now, 0.0)
    gammas = (1.3 + 0.05 * jnp.arange(frac.shape[0], dtype=jnp.int32).astype(jnp.float32))[
        :, None, None
    ]
    mat_pressure = (gammas - 1.0) * density * energy
    zone_density = jnp.sum(frac * density, axis=0)
    viscous = VISC_COEF * zone_density * area_now * squeeze * squeeze
    total_pressure = jnp.sum(frac * mat_pressure, axis=0) + viscous
    half_press = 0.5 * total_pressure
    quarter_mass = 0.25 * zone_density * area_now
    term_one = jnp.stack([-half_press * cross_y, half_press * cross_x, quarter_mass])
    term_two = jnp.stack([half_press * rise_y, -half_press * rise_x, quarter_mass])
    term_three = jnp.stack([half_press * cross_y, -half_press * cross_x, quarter_mass])
    term_four = jnp.stack([-half_press * rise_y, half_press * rise_x, quarter_mass])
    return (area_now, mat_pressure, viscous, (term_one, term_two, term_three, term_four))


def node_update(totals, node_shift, node_speed):
    accel_xy = totals[0:2] / totals[2:3]
    speed_after = node_speed + TIME_STEP * accel_xy
    shift_after = node_shift + TIME_STEP * speed_after
    return (speed_after, shift_after)


def material_state(frac, density, energy, area_now, area_after, mat_pressure, viscous):
    energy_after = energy - (mat_pressure + viscous) * (area_after - area_now) / (
        density * area_now
    )
    volume = frac * area_after
    mass_now = frac * density * area_now
    return jnp.stack([volume, mass_now, mass_now * energy_after])


def upper_along_x(values):
    received = shifted(values[:, 0:1, :], "zx", -1)
    return jnp.concatenate([values, received], axis=1)


def upper_along_y(values):
    received = shifted(values[:, :, 0:1], "zy", -1)
    return jnp.concatenate([values, received], axis=2)


def upper_rim(values):
    return upper_along_y(upper_along_x(values))


def spill_along_x(values):
    received = shifted(values[:, -1:, :], "zx", 1)
    return jnp.concatenate([values[:, 0:1, :] + received, values[:, 1:-1, :]], axis=1)


def spill_along_y(values):
    received = shifted(values[:, :, -1:], "zy", 1)
    return jnp.concatenate([values[:, :, 0:1] + received, values[:, :, 1:-1]], axis=2)


def spill_rim(values):
    return spill_along_y(spill_along_x(values))


def slice_corners(extended):
    return (extended[:, :-1, :-1], extended[:, 1:, :-1], extended[:, 1:, 1:], extended[:, :-1, 1:])


SUB = 8
LANES = 128
QUAD = 4


def lower_half(shape):
    return lax.broadcasted_iota(jnp.int32, shape, len(shape) - 2) % SUB < QUAD


def zones_first(field):
    return jnp.concatenate([field[:, :LANES], field[:, LANES:]], axis=0).T


def pair_to_pieces(first, second, low):
    even = jnp.where(low, first, pltpu.roll(second, QUAD, 0))
    odd = jnp.where(low, pltpu.roll(first, QUAD, 0), second)
    return even, odd


def pack_kernel(frac_ref, density_ref, energy_ref, out_ref):
    low = lower_half((SUB, LANES))
    for group, ref in enumerate((frac_ref, density_ref, energy_ref)):
        for pair in range(ref.shape[0] // 2):
            first, second = zones_first(ref[2 * pair]), zones_first(ref[2 * pair + 1])
            row = SUB * (group * (ref.shape[0] // 2) + pair)
            for octet in range(LANES // SUB):
                at = slice(SUB * octet, SUB * octet + SUB)
                even, odd = pair_to_pieces(first[at], second[at], low)
                out_ref[2 * octet, row : row + SUB, :] = even
                out_ref[2 * octet + 1, row : row + SUB, :] = odd


def split3(value):
    high = value.astype(jnp.bfloat16)
    left = value - high.astype(jnp.float32)
    middle = left.astype(jnp.bfloat16)
    low = (left - middle.astype(jnp.float32)).astype(jnp.bfloat16)
    return high, middle, low


def table_kernel(me_ref, target_ref, source_ref, place_ref, weight_ref, out_ref):
    entries = target_ref.shape[0]
    capacity = LANES // SUB
    me = me_ref[0, 0]
    target = target_ref[...]
    down = lax.broadcasted_iota(jnp.int32, (entries, entries), 0)
    across = lax.broadcasted_iota(jnp.int32, (entries, entries), 1)
    column = target.astype(jnp.float32)
    row = jnp.sum(jnp.where(down == across, column, 0.0), axis=0, keepdims=True)
    earlier = (row == column) & (across < down)
    rank = jnp.sum(jnp.where(earlier, 1.0, 0.0), axis=1, keepdims=True).astype(jnp.int32)
    slot = (target >> 3) * LANES + ((target & 7) ^ (me & 7)) * capacity + rank
    slots = 4 * LANES
    hot = jnp.where(lax.broadcasted_iota(jnp.int32, (entries, slots), 1) == slot, 1.0, 0.0)
    weight = weight_ref[...]
    source, place = source_ref[...], place_ref[...]
    source = ((source & 1) * 64 + (source >> 1)).astype(jnp.float32).astype(jnp.bfloat16)
    place = ((place & 1) * 64 + (place >> 1)).astype(jnp.float32).astype(jnp.bfloat16)
    parts = [part.astype(jnp.float32) for part in (*split3(weight), source, place)]
    values = jnp.concatenate(parts + [jnp.zeros((SUB - len(parts), entries), jnp.float32)], axis=0)
    tables = jnp.dot(
        values.astype(jnp.bfloat16), hot.astype(jnp.bfloat16), preferred_element_type=jnp.float32
    )
    weights = tables[0:1] + tables[1:2] + tables[2:3]
    for octet in range(4):
        at = slice(LANES * octet, LANES * octet + LANES)
        out_ref[octet : octet + 1, :] = jnp.zeros((1, LANES), jnp.float32)
        out_ref[4 + octet : 5 + octet, :] = tables[3:4, at]
        out_ref[8 + octet : 9 + octet, :] = weights[:, at]
        out_ref[12 + octet : 13 + octet, :] = tables[4:5, at]


def extras_kernel(area_ref, after_ref, viscous_ref, tables_ref, out_ref):
    low = lower_half((SUB, LANES))
    area, after = zones_first(area_ref[...]), zones_first(after_ref[...])
    viscous = zones_first(viscous_ref[...])
    first, second = tables_ref[0:8], tables_ref[8:16]
    for octet in range(LANES // SUB):
        at = slice(SUB * octet, SUB * octet + SUB)
        even, odd = pair_to_pieces(area[at], after[at], low)
        out_ref[2 * octet, 0:8, :] = even
        out_ref[2 * octet + 1, 0:8, :] = odd
        out_ref[2 * octet, 8:16, :] = jnp.where(low, viscous[at], first)
        out_ref[2 * octet + 1, 8:16, :] = jnp.where(low, pltpu.roll(viscous[at], QUAD, 0), first)
        out_ref[2 * octet, 16:24, :] = second
        out_ref[2 * octet + 1, 16:24, :] = second


def crossing_kernel(raw_ref, extra_ref, out_ref, state_ref, slots_ref, places_ref):
    devices, rows, lanes = raw_ref.shape
    tiles = rows // SUB
    pairs = tiles // 3
    low = lower_half((SUB, LANES))
    gammas = (np.float32(1.3) + np.float32(0.05) * np.arange(2 * pairs, dtype=np.float32)) - np.float32(1.0)

    def conserve(source, carry):
        area_pair, viscous_pair = extra_ref[source, 0:8], extra_ref[source, 8:16]
        area_swap = pltpu.roll(area_pair, QUAD, 0)
        area, after = jnp.where(low, area_pair, area_swap), jnp.where(low, area_swap, area_pair)
        viscous = jnp.where(low, viscous_pair, pltpu.roll(viscous_pair, QUAD, 0))
        change = after - area
        for pair in range(pairs):
            at = [slice(SUB * (pair + pairs * group), SUB * (pair + pairs * group) + SUB) for group in range(3)]
            frac, density, energy = raw_ref[source, at[0]], raw_ref[source, at[1]], raw_ref[source, at[2]]
            stiff = jnp.where(low, gammas[2 * pair], gammas[2 * pair + 1])
            mass = frac * density * area
            pressure = stiff * density * energy
            state_ref[source, at[0]] = frac * after
            state_ref[source, at[1]] = mass
            state_ref[source, at[2]] = mass * energy - frac * (pressure + viscous) * change
        return carry

    lax.fori_loop(0, devices, conserve, 0)
    piece = lax.broadcasted_iota(jnp.int32, (SUB, LANES), 1) // (LANES // SUB)
    odd = [(piece >> bit) & 1 == 1 for bit in range(3)]

    def regroup(values):
        for bit in range(3):
            values = [
                jnp.where(odd[bit], values[i | (1 << bit)], values[i & ~(1 << bit)])
                if not (i >> bit) & 1
                else jnp.where(odd[bit], values[i & ~(1 << bit)], values[i | (1 << bit)])
                for i in range(SUB)
            ]
        return values

    def gather(a, carry):
        for octet in range(devices // SUB):
            index, weight, place = [], [], []
            for sigma in range(SUB):
                source = a * SUB + sigma
                spread = (SUB, LANES)
                index.append(
                    jnp.broadcast_to(extra_ref[source, 12 + octet : 13 + octet], spread).astype(jnp.int32)
                )
                weight.append(jnp.broadcast_to(extra_ref[source, 16 + octet : 17 + octet], spread))
                place.append(jnp.broadcast_to(extra_ref[source, 20 + octet : 21 + octet], spread))
            for delta, value in enumerate(regroup(place)):
                places_ref[SUB * octet + delta, a] = value
            for tile in range(tiles):
                at = slice(SUB * tile, SUB * tile + SUB)
                values = [
                    jnp.take_along_axis(
                        state_ref[a * SUB + sigma, at], index[sigma], axis=1, mode="promise_in_bounds"
                    )
                    * weight[sigma]
                    for sigma in range(SUB)
                ]
                for delta, value in enumerate(regroup(values)):
                    slots_ref[SUB * octet + delta, a, at] = value
        return carry

    lax.fori_loop(0, devices // SUB, gather, 0)

    def scatter(target, carry):
        groups = devices // SUB
        value = jnp.concatenate([slots_ref[target, a] for a in range(groups)], axis=1)
        parts = jnp.concatenate(split3(value), axis=0)
        place = [places_ref[target, a] for a in range(groups)]
        block = lax.broadcasted_iota(jnp.int32, (SUB, LANES), 0).astype(jnp.float32)
        hot = jnp.concatenate(
            [
                jnp.concatenate(
                    [
                        jnp.where(place[a] == block + float(SUB * tile), 1.0, 0.0)
                        for tile in range(LANES // SUB)
                    ],
                    axis=0,
                )
                for a in range(groups)
            ],
            axis=1,
        ).astype(jnp.bfloat16)
        total = lax.dot_general(
            parts, hot, (((1,), (1,)), ((), ())), preferred_element_type=jnp.float32
        )
        out_ref[target] = total[0:rows] + total[rows : 2 * rows] + total[2 * rows : 3 * rows]
        return carry

    lax.fori_loop(0, devices, scatter, 0)


def unpack_kernel(sums_ref, own_ref, out_ref):
    low = lower_half((SUB, LANES))
    half = LANES // 2
    for pair in range(sums_ref.shape[1] // SUB):
        at = slice(SUB * pair, SUB * pair + SUB)
        first, second = [], []
        for octet in range(LANES // SUB):
            even, odd = pair_to_pieces(sums_ref[2 * octet, at], sums_ref[2 * octet + 1, at], low)
            first.append(even)
            second.append(odd)
        for field, tiles in ((2 * pair, first), (2 * pair + 1, second)):
            blocks = jnp.concatenate(tiles, axis=0).T
            out_ref[field, :, :LANES] = own_ref[field, :, :LANES] + blocks[:half]
            out_ref[field, :, LANES:] = own_ref[field, :, LANES:] + blocks[half:]


def whole(count):
    return [pl.BlockSpec(memory_space=pltpu.VMEM)] * count


def exchange(value):
    return lax.all_to_all(value, ("zx", "zy"), 0, 0, tiled=True)


def remap_by_zones(
    frac, density, energy, area_now, area_after, viscous, dest_tile, src_block, dest_block, crossing
):
    devices = lax.axis_size("zx") * lax.axis_size("zy")
    fields = 3 * frac.shape[0]
    rows = fields * QUAD
    f32 = jnp.float32
    raw = pl.pallas_call(
        pack_kernel,
        out_shape=jax.ShapeDtypeStruct((devices, rows, LANES), f32),
        in_specs=whole(3),
        out_specs=whole(1)[0],
        name="pack",
    )(frac, density, energy)
    raw = exchange(raw)
    me = (lax.axis_index("zx") * lax.axis_size("zy") + lax.axis_index("zy")).astype(jnp.int32)
    tables = pl.pallas_call(
        table_kernel,
        out_shape=jax.ShapeDtypeStruct((16, LANES), f32),
        in_specs=[pl.BlockSpec(memory_space=pltpu.SMEM)] + whole(4),
        out_specs=whole(1)[0],
        name="tables",
    )(me.reshape(1, 1), dest_tile[0, 0], src_block[0], dest_block[0], crossing[0])
    extras = pl.pallas_call(
        extras_kernel,
        out_shape=jax.ShapeDtypeStruct((devices, 24, LANES), f32),
        in_specs=whole(4),
        out_specs=whole(1)[0],
        name="extras",
    )(area_now, area_after, viscous, tables)
    extras = exchange(extras)
    sums = pl.pallas_call(
        crossing_kernel,
        out_shape=jax.ShapeDtypeStruct((devices, rows, LANES), f32),
        in_specs=whole(2),
        out_specs=whole(1)[0],
        scratch_shapes=[
            pltpu.VMEM((devices, rows, LANES), f32),
            pltpu.VMEM((devices, devices // SUB, rows, LANES), f32),
            pltpu.VMEM((devices, devices // SUB, SUB, LANES), f32),
        ],
        name="crossings",
    )(raw, extras)
    return exchange(sums)


def lagrange(frac, density, energy, node_shift, node_speed):
    node_fields = jnp.concatenate([node_shift, node_speed], axis=0)
    extended = upper_rim(node_fields)
    area_now, mat_pressure, viscous, terms = zone_phase(
        frac, density, energy, slice_corners(extended[0:2]), slice_corners(extended[2:4])
    )
    term_one, term_two, term_three, term_four = terms
    gathered = (
        jnp.pad(term_one, ((0, 0), (0, 1), (0, 1)))
        + jnp.pad(term_two, ((0, 0), (1, 0), (0, 1)))
        + jnp.pad(term_three, ((0, 0), (1, 0), (1, 0)))
        + jnp.pad(term_four, ((0, 0), (0, 1), (1, 0)))
    )
    totals = spill_rim(gathered)
    speed_after, shift_after = node_update(totals, node_shift, node_speed)
    moved_rim = upper_rim(shift_after)
    area_after = zone_area(slice_corners(moved_rim))
    return area_now, area_after, viscous, mat_pressure, speed_after, shift_after


def local(*arguments):
    materials, rows_x, rows_y = arguments[0].shape
    devices = lax.axis_size("zx") * lax.axis_size("zy")
    entries, nblocks = arguments[6].shape[2], arguments[9].shape[2]
    fits = (rows_x, rows_y, nblocks) == (64, 256, LANES) and materials == 8
    if fits and devices == LANES // QUAD and entries <= 2 * LANES:
        return local_by_zones(*arguments)
    return local_by_entries(*arguments)


def local_by_zones(
    frac, density, energy, node_shift, node_speed, dest_tile, src_block, dest_block, crossing, keep
):
    materials, rows_x, rows_y = frac.shape
    area_now, area_after, viscous, mat_pressure, speed_after, shift_after = lagrange(
        frac, density, energy, node_shift, node_speed
    )
    sums = remap_by_zones(
        frac, density, energy, area_now, area_after, viscous, dest_tile, src_block, dest_block, crossing
    )
    conserved = material_state(frac, density, energy, area_now, area_after, mat_pressure, viscous)
    share = keep[0, 0].reshape(rows_x, 2)
    share = jnp.concatenate(
        [jnp.broadcast_to(share[:, h : h + 1], (rows_x, LANES)) for h in range(2)], axis=1
    )
    own = (conserved * share).reshape(3 * materials, rows_x, rows_y)
    remapped = pl.pallas_call(
        unpack_kernel,
        out_shape=jax.ShapeDtypeStruct(own.shape, jnp.float32),
        in_specs=whole(2),
        out_specs=whole(1)[0],
        name="unpack",
    )(sums, own)
    return (remapped.reshape(3, materials, rows_x, rows_y), speed_after, shift_after)


def local_by_entries(
    frac, density, energy, node_shift, node_speed, dest_tile, src_block, dest_block, crossing, keep
):
    materials, rows_x, rows_y = frac.shape
    node_fields = jnp.concatenate([node_shift, node_speed], axis=0)
    extended = upper_rim(node_fields)
    area_now, mat_pressure, viscous, terms = zone_phase(
        frac, density, energy, slice_corners(extended[0:2]), slice_corners(extended[2:4])
    )
    term_one, term_two, term_three, term_four = terms
    gathered = (
        jnp.pad(term_one, ((0, 0), (0, 1), (0, 1)))
        + jnp.pad(term_two, ((0, 0), (1, 0), (0, 1)))
        + jnp.pad(term_three, ((0, 0), (1, 0), (1, 0)))
        + jnp.pad(term_four, ((0, 0), (0, 1), (1, 0)))
    )
    totals = spill_rim(gathered)
    speed_after, shift_after = node_update(totals, node_shift, node_speed)
    moved_rim = upper_rim(shift_after)
    area_after = zone_area(slice_corners(moved_rim))
    conserved = material_state(frac, density, energy, area_now, area_after, mat_pressure, viscous)
    nblocks = keep.shape[2]
    block_len = rows_x * rows_y // nblocks
    fields = 3 * materials
    blocks = conserved.reshape(fields, nblocks, block_len)
    size_x = lax.axis_size("zx")
    size_y = lax.axis_size("zy")
    devices = size_x * size_y
    targets = dest_tile[0, 0, :, 0]
    sources = src_block[0, 0]
    places = dest_block[0, 0]
    weights = crossing[0, 0]
    entry_count = targets.shape[0]
    capacity = max(2, 2 * entry_count // devices)
    member = (targets[:, None] == jnp.arange(devices, dtype=jnp.int32)[None, :]).astype(jnp.int32)
    before = jnp.cumsum(member, axis=0) - member
    slot_rank = jnp.sum(before * member, axis=1)
    slot_index = targets * capacity + slot_rank
    slot_total = devices * capacity
    matches = slot_index[:, None] == jnp.arange(slot_total, dtype=jnp.int32)[None, :]
    filled = jnp.any(matches, axis=0)
    owners = jnp.sum(
        jnp.where(matches, jnp.arange(entry_count, dtype=jnp.int32)[:, None], 0), axis=0
    )
    slot_weight = jnp.where(filled, weights[owners], 0.0)
    slot_place = jnp.where(filled, places[owners], nblocks)
    payload = blocks[:, sources[owners], :] * slot_weight[None, :, None]
    payload = payload.reshape(fields, size_x, size_y, capacity, block_len)
    place_ids = slot_place.reshape(1, size_x, size_y, capacity)
    arrived, arrived_ids = (
        lax.all_to_all(
            lax.all_to_all(payload, "zx", split_axis=1, concat_axis=1, tiled=True),
            "zy",
            split_axis=2,
            concat_axis=2,
            tiled=True,
        ),
        lax.all_to_all(
            lax.all_to_all(place_ids, "zx", split_axis=1, concat_axis=1, tiled=True),
            "zy",
            split_axis=2,
            concat_axis=2,
            tiled=True,
        ),
    )
    arrived = arrived.reshape(fields, slot_total, block_len)
    arrived_ids = arrived_ids.reshape(slot_total)
    landed = (
        jnp.zeros((fields, nblocks + 1, block_len), jnp.float32).at[:, arrived_ids, :].add(arrived)
    )
    result = blocks * keep[0, 0][None, :, None] + landed[:, :nblocks, :]
    remapped = result.reshape(3, materials, rows_x, rows_y)
    return (remapped, speed_after, shift_after)


def solution(mesh):
    in_specs = (
        P(None, "zx", "zy"),
        P(None, "zx", "zy"),
        P(None, "zx", "zy"),
        P(None, "zx", "zy"),
        P(None, "zx", "zy"),
        P("zx", "zy", None, None),
        P("zx", "zy", None),
        P("zx", "zy", None),
        P("zx", "zy", None),
        P("zx", "zy", None),
    )
    out_specs = (P(None, None, "zx", "zy"), P(None, "zx", "zy"), P(None, "zx", "zy"))
    return jax.shard_map(local, mesh=mesh, in_specs=in_specs, out_specs=out_specs, check_vma=False)
```

```python
import jax
import jax.numpy as jnp
import numpy as np
from jax import lax
from jax.experimental import pallas as pl
from jax.experimental.pallas import tpu as pltpu
from jax.sharding import PartitionSpec as P

TIME_STEP = 0.02
VISC_COEF = 0.25


def shifted(value, axis, by):
    peers = lax.axis_size(axis)
    return lax.ppermute(value, axis, [(i, (i + by) % peers) for i in range(peers)])


def corner_geometry(corners):
    corner_one, corner_two, corner_three, corner_four = corners
    rise_x = 1.0 + corner_three[0] - corner_one[0]
    rise_y = 1.0 + corner_three[1] - corner_one[1]
    cross_x = -1.0 + corner_four[0] - corner_two[0]
    cross_y = 1.0 + corner_four[1] - corner_two[1]
    return (rise_x, rise_y, cross_x, cross_y)


def zone_area(corners):
    rise_x, rise_y, cross_x, cross_y = corner_geometry(corners)
    return 0.5 * (rise_x * cross_y - cross_x * rise_y)


def zone_phase(frac, density, energy, shifts, speeds):
    rise_x, rise_y, cross_x, cross_y = corner_geometry(shifts)
    area_now = 0.5 * (rise_x * cross_y - cross_x * rise_y)
    speed_one, speed_two, speed_three, speed_four = speeds
    area_rate = 0.5 * (
        (speed_three[0] - speed_one[0]) * cross_y
        + rise_x * (speed_four[1] - speed_two[1])
        - (speed_four[0] - speed_two[0]) * rise_y
        - cross_x * (speed_three[1] - speed_one[1])
    )
    squeeze = jnp.minimum(area_rate / area_now, 0.0)
    gammas = (1.3 + 0.05 * jnp.arange(frac.shape[0], dtype=jnp.int32).astype(jnp.float32))[
        :, None, None
    ]
    mat_pressure = (gammas - 1.0) * density * energy
    zone_density = jnp.sum(frac * density, axis=0)
    viscous = VISC_COEF * zone_density * area_now * squeeze * squeeze
    total_pressure = jnp.sum(frac * mat_pressure, axis=0) + viscous
    half_press = 0.5 * total_pressure
    quarter_mass = 0.25 * zone_density * area_now
    term_one = jnp.stack([-half_press * cross_y, half_press * cross_x, quarter_mass])
    term_two = jnp.stack([half_press * rise_y, -half_press * rise_x, quarter_mass])
    term_three = jnp.stack([half_press * cross_y, -half_press * cross_x, quarter_mass])
    term_four = jnp.stack([-half_press * rise_y, half_press * rise_x, quarter_mass])
    return (area_now, mat_pressure, viscous, (term_one, term_two, term_three, term_four))


def node_update(totals, node_shift, node_speed):
    accel_xy = totals[0:2] / totals[2:3]
    speed_after = node_speed + TIME_STEP * accel_xy
    shift_after = node_shift + TIME_STEP * speed_after
    return (speed_after, shift_after)


def material_state(frac, density, energy, area_now, area_after, mat_pressure, viscous):
    energy_after = energy - (mat_pressure + viscous) * (area_after - area_now) / (
        density * area_now
    )
    volume = frac * area_after
    mass_now = frac * density * area_now
    return jnp.stack([volume, mass_now, mass_now * energy_after])


def upper_along_x(values):
    received = shifted(values[:, 0:1, :], "zx", -1)
    return jnp.concatenate([values, received], axis=1)


def upper_along_y(values):
    received = shifted(values[:, :, 0:1], "zy", -1)
    return jnp.concatenate([values, received], axis=2)


def upper_rim(values):
    return upper_along_y(upper_along_x(values))


def spill_along_x(values):
    received = shifted(values[:, -1:, :], "zx", 1)
    return jnp.concatenate([values[:, 0:1, :] + received, values[:, 1:-1, :]], axis=1)


def spill_along_y(values):
    received = shifted(values[:, :, -1:], "zy", 1)
    return jnp.concatenate([values[:, :, 0:1] + received, values[:, :, 1:-1]], axis=2)


def spill_rim(values):
    return spill_along_y(spill_along_x(values))


def slice_corners(extended):
    return (extended[:, :-1, :-1], extended[:, 1:, :-1], extended[:, 1:, 1:], extended[:, :-1, 1:])


SUB = 8
LANES = 128
QUAD = 4


def lower_half(shape):
    return lax.broadcasted_iota(jnp.int32, shape, len(shape) - 2) % SUB < QUAD


def zones_first(field):
    return jnp.concatenate([field[:, :LANES], field[:, LANES:]], axis=0).T


def pair_to_pieces(first, second, low):
    even = jnp.where(low, first, pltpu.roll(second, QUAD, 0))
    odd = jnp.where(low, pltpu.roll(first, QUAD, 0), second)
    return even, odd


def pack_kernel(frac_ref, density_ref, energy_ref, out_ref):
    low = lower_half((SUB, LANES))
    for group, ref in enumerate((frac_ref, density_ref, energy_ref)):
        for pair in range(ref.shape[0] // 2):
            first, second = zones_first(ref[2 * pair]), zones_first(ref[2 * pair + 1])
            row = SUB * (group * (ref.shape[0] // 2) + pair)
            for octet in range(LANES // SUB):
                at = slice(SUB * octet, SUB * octet + SUB)
                even, odd = pair_to_pieces(first[at], second[at], low)
                out_ref[2 * octet, row : row + SUB, :] = even
                out_ref[2 * octet + 1, row : row + SUB, :] = odd


def split3(value):
    high = value.astype(jnp.bfloat16)
    left = value - high.astype(jnp.float32)
    middle = left.astype(jnp.bfloat16)
    low = (left - middle.astype(jnp.float32)).astype(jnp.bfloat16)
    return high, middle, low


def table_kernel(me_ref, target_ref, source_ref, place_ref, weight_ref, keep_ref, out_ref):
    entries = target_ref.shape[0]
    capacity = LANES // SUB
    me = me_ref[0, 0]
    target = target_ref[...]
    down = lax.broadcasted_iota(jnp.int32, (entries, entries), 0)
    across = lax.broadcasted_iota(jnp.int32, (entries, entries), 1)
    column = target.astype(jnp.float32)
    row = jnp.sum(jnp.where(down == across, column, 0.0), axis=0, keepdims=True)
    earlier = (row == column) & (across < down)
    rank = jnp.sum(jnp.where(earlier, 1.0, 0.0), axis=1, keepdims=True).astype(jnp.int32)
    slot = (target >> 3) * LANES + ((target & 7) ^ (me & 7)) * capacity + rank
    slots = 4 * LANES
    hot = jnp.where(lax.broadcasted_iota(jnp.int32, (entries, slots), 1) == slot, 1.0, 0.0)
    weight = weight_ref[...]
    source, place = source_ref[...], place_ref[...]
    source = ((source & 1) * 64 + (source >> 1)).astype(jnp.float32).astype(jnp.bfloat16)
    place = ((place & 1) * 64 + (place >> 1)).astype(jnp.float32).astype(jnp.bfloat16)
    parts = [part.astype(jnp.float32) for part in (*split3(weight), source, place)]
    values = jnp.concatenate(parts + [jnp.zeros((SUB - len(parts), entries), jnp.float32)], axis=0)
    tables = jnp.dot(
        values.astype(jnp.bfloat16), hot.astype(jnp.bfloat16), preferred_element_type=jnp.float32
    )
    weights = tables[0:1] + tables[1:2] + tables[2:3]
    for octet in range(4):
        at = slice(LANES * octet, LANES * octet + LANES)
        out_ref[octet : octet + 1, :] = tables[3:4, at]
        out_ref[4 + octet : 5 + octet, :] = weights[:, at]
        out_ref[8 + octet : 9 + octet, :] = tables[4:5, at]
    lane = lax.broadcasted_iota(jnp.int32, (SUB, LANES), 1)
    block = 2 * (lane % 64) + lane // 64
    keep = jnp.take_along_axis(
        jnp.broadcast_to(keep_ref[...], (SUB, LANES)), block, axis=1, mode="promise_in_bounds"
    )
    out_ref[12:16, :] = keep[0:4]


def stiffness(materials):
    gammas = np.float32(1.3) + np.float32(0.05) * np.arange(materials, dtype=np.float32)
    return [float(gamma) for gamma in gammas - np.float32(1.0)]


def sums_kernel(frac_ref, density_ref, energy_ref, shift_ref, speed_ref, sums_ref, rim_ref):
    stiff = stiffness(frac_ref.shape[0])
    mass = pressure = None
    for material in range(frac_ref.shape[0]):
        part = frac_ref[material] * density_ref[material]
        force = part * energy_ref[material] * stiff[material]
        mass = part if mass is None else mass + part
        pressure = force if pressure is None else pressure + force
    sums_ref[0], sums_ref[1] = mass, pressure
    last = mass.shape[0] - 1
    for field in range(2):
        for at, ref in ((0, shift_ref), (4, speed_ref)):
            rim_ref[at + 2 * field : at + 2 * field + 2, :] = ref[field, 0:2, :]
            rim_ref[10 + at // 2 + field : 11 + at // 2 + field, :] = ref[field, last : last + 1, :]
    for field, value in enumerate((mass, pressure)):
        rim_ref[8 + field : 9 + field, :] = value[0:1]
        rim_ref[14 + field : 15 + field, :] = value[last : last + 1]


def rows_kernel(shift_ref, speed_ref, sums_ref, above_ref, below_ref, out_ref, first_ref, last_ref):
    height, width = shift_ref.shape[1:]
    for field in range(6):
        value = (shift_ref, speed_ref, sums_ref)[field // 2][field % 2]
        out_ref[field, 1 : height + 1, :] = value
        out_ref[field, 0:1, :] = below_ref[10 + field : 11 + field, :]
        if field < 4:
            out_ref[field, height + 1 : height + 3, :] = above_ref[2 * field : 2 * field + 2, :]
        else:
            for row in (1, 2):
                out_ref[field, height + row : height + row + 1, :] = above_ref[4 + field : 5 + field, :]
        out_ref[field, height + 3 : height + 8, :] = jnp.zeros((5, width), jnp.float32)
        whole_column = out_ref[field]
        if field < 4:
            first_ref[:, 2 * field : 2 * field + 2] = whole_column[:, 0:2]
        else:
            first_ref[:, 4 + field : 5 + field] = whole_column[:, 0:1]
        last_ref[:, field : field + 1] = whole_column[:, width - 1 : width]


def lagrange_kernel(
    rows_ref, right_ref, left_ref, raw_ref, tables_ref, speed_ref, shift_ref, out_ref
):
    height, width = rows_ref.shape[1] - SUB, rows_ref.shape[2]
    shape = (height + SUB, width + LANES)
    lane = lax.broadcasted_iota(jnp.int32, shape, 1)
    right, left = right_ref[...], left_ref[...]

    def extend(field):
        value = jnp.concatenate([rows_ref[field], jnp.zeros((shape[0], LANES), jnp.float32)], axis=1)
        value = pltpu.roll(value, 1, 1)
        value = jnp.where(lane == 0, left[:, field : field + 1], value)
        if field < 4:
            value = jnp.where(lane == width + 1, right[:, 2 * field : 2 * field + 1], value)
            return jnp.where(lane == width + 2, right[:, 2 * field + 1 : 2 * field + 2], value)
        return jnp.where(lane == width + 1, right[:, 4 + field : 5 + field], value)

    def next_row(value):
        return pltpu.roll(value, shape[0] - 1, 0)

    def next_column(value):
        return pltpu.roll(value, shape[1] - 1, 1)

    def before_row(value):
        return pltpu.roll(value, 1, 0)

    def before_column(value):
        return pltpu.roll(value, 1, 1)

    def diagonals(value):
        across = next_column(value)
        down = next_row(value)
        return next_row(across) - value, across - down

    def geometry(shift_x, shift_y):
        rise_x, cross_x = diagonals(shift_x)
        rise_y, cross_y = diagonals(shift_y)
        return 1.0 + rise_x, 1.0 + rise_y, -1.0 + cross_x, 1.0 + cross_y

    shift_x, shift_y, speed_x, speed_y, density, pressure = [extend(field) for field in range(6)]
    rise_x, rise_y, cross_x, cross_y = geometry(shift_x, shift_y)
    area = 0.5 * (rise_x * cross_y - cross_x * rise_y)
    up_x, over_x = diagonals(speed_x)
    up_y, over_y = diagonals(speed_y)
    rate = 0.5 * (up_x * cross_y + rise_x * over_y - over_x * rise_y - cross_x * up_y)
    squeeze = jnp.minimum(rate / area, 0.0)
    viscous = VISC_COEF * density * area * squeeze * squeeze
    half = 0.5 * (pressure + viscous)
    quarter = 0.25 * density * area

    def corners(one, two, sign):
        upper = before_row(two - before_column(one))
        return sign * (one - before_column(two) + upper)

    force_x = corners(-half * cross_y, half * rise_y, 1.0)
    force_y = corners(half * cross_x, -half * rise_x, 1.0)
    both = quarter + before_column(quarter)
    mass = both + before_row(both)
    speed_x = speed_x + TIME_STEP * (force_x / mass)
    speed_y = speed_y + TIME_STEP * (force_y / mass)
    shift_x = shift_x + TIME_STEP * speed_x
    shift_y = shift_y + TIME_STEP * speed_y
    rise_x, rise_y, cross_x, cross_y = geometry(shift_x, shift_y)
    after = 0.5 * (rise_x * cross_y - cross_x * rise_y)

    def own(value):
        return next_column(next_row(value))[0:height, 0:width]

    speed_ref[0], speed_ref[1] = own(speed_x), own(speed_y)
    shift_ref[0], shift_ref[1] = own(shift_x), own(shift_y)

    low = lower_half((SUB, LANES))
    area, after, viscous = [zones_first(own(value)) for value in (area, after, viscous)]
    pairs = raw_ref.shape[1] // (3 * SUB)
    stiff = stiffness(2 * pairs)
    for octet in range(LANES // SUB):
        at = slice(SUB * octet, SUB * octet + SUB)
        tiles = [pair_to_pieces(value[at], value[at], low) for value in (area, after, viscous)]
        for side in range(2):
            piece = 2 * octet + side
            now, then, thick = [tile[side] for tile in tiles]
            change = then - now
            for pair in range(pairs):
                at_pair = [slice(SUB * (pair + pairs * g), SUB * (pair + pairs * g) + SUB) for g in range(3)]
                frac, rho, heat = [raw_ref[piece, rows] for rows in at_pair]
                held = frac * rho
                mass_now = held * now
                force = jnp.where(low, stiff[2 * pair], stiff[2 * pair + 1]) * rho * heat
                out_ref[piece, at_pair[0]] = frac * then
                out_ref[piece, at_pair[1]] = mass_now
                out_ref[piece, at_pair[2]] = mass_now * heat - frac * (force + thick) * change
            end = 3 * SUB * pairs
            out_ref[piece, end : end + 2 * SUB] = tables_ref[...]


def crossing_kernel(state_ref, out_ref, slots_ref, places_ref):
    devices = state_ref.shape[0]
    rows = state_ref.shape[1] - 2 * SUB
    tiles = rows // SUB
    piece = lax.broadcasted_iota(jnp.int32, (SUB, LANES), 1) // (LANES // SUB)
    odd = [(piece >> bit) & 1 == 1 for bit in range(3)]

    def regroup(values):
        for bit in range(3):
            values = [
                jnp.where(odd[bit], values[i | (1 << bit)], values[i & ~(1 << bit)])
                if not (i >> bit) & 1
                else jnp.where(odd[bit], values[i & ~(1 << bit)], values[i | (1 << bit)])
                for i in range(SUB)
            ]
        return values

    def gather(a, carry):
        for octet in range(devices // SUB):
            index, weight, place = [], [], []
            for sigma in range(SUB):
                source = a * SUB + sigma
                spread = (SUB, LANES)
                index.append(
                    jnp.broadcast_to(state_ref[source, rows + octet : rows + octet + 1], spread).astype(jnp.int32)
                )
                weight.append(jnp.broadcast_to(state_ref[source, rows + 4 + octet : rows + octet + 5], spread))
                place.append(jnp.broadcast_to(state_ref[source, rows + 8 + octet : rows + octet + 9], spread))
            for delta, value in enumerate(regroup(place)):
                places_ref[SUB * octet + delta, a] = value
            for tile in range(tiles):
                at = slice(SUB * tile, SUB * tile + SUB)
                values = [
                    jnp.take_along_axis(
                        state_ref[a * SUB + sigma, at], index[sigma], axis=1, mode="promise_in_bounds"
                    )
                    * weight[sigma]
                    for sigma in range(SUB)
                ]
                for delta, value in enumerate(regroup(values)):
                    slots_ref[SUB * octet + delta, a, at] = value
        return carry

    lax.fori_loop(0, devices // SUB, gather, 0)

    def scatter(target, carry):
        groups = devices // SUB
        value = jnp.concatenate([slots_ref[target, a] for a in range(groups)], axis=1)
        parts = jnp.concatenate(split3(value), axis=0)
        place = [places_ref[target, a] for a in range(groups)]
        block = lax.broadcasted_iota(jnp.int32, (SUB, LANES), 0).astype(jnp.float32)
        hot = jnp.concatenate(
            [
                jnp.concatenate(
                    [
                        jnp.where(place[a] == block + float(SUB * tile), 1.0, 0.0)
                        for tile in range(LANES // SUB)
                    ],
                    axis=0,
                )
                for a in range(groups)
            ],
            axis=1,
        ).astype(jnp.bfloat16)
        total = lax.dot_general(
            parts, hot, (((1,), (1,)), ((), ())), preferred_element_type=jnp.float32
        )
        keep = jnp.broadcast_to(state_ref[target, rows + 12 : rows + 13], (rows, LANES))
        stay = keep * state_ref[target, 0:rows]
        out_ref[target] = stay + total[0:rows] + total[rows : 2 * rows] + total[2 * rows : 3 * rows]
        return carry

    lax.fori_loop(0, devices, scatter, 0)


def unpack_kernel(sums_ref, out_ref):
    low = lower_half((SUB, LANES))
    half = LANES // 2
    for pair in range(sums_ref.shape[1] // SUB):
        at = slice(SUB * pair, SUB * pair + SUB)
        first, second = [], []
        for octet in range(LANES // SUB):
            even, odd = pair_to_pieces(sums_ref[2 * octet, at], sums_ref[2 * octet + 1, at], low)
            first.append(even)
            second.append(odd)
        for field, tiles in ((2 * pair, first), (2 * pair + 1, second)):
            blocks = jnp.concatenate(tiles, axis=0).T
            out_ref[field, :, :LANES] = blocks[:half]
            out_ref[field, :, LANES:] = blocks[half:]


def whole(count):
    return [pl.BlockSpec(memory_space=pltpu.VMEM)] * count


def call(kernel, name, outs, inputs, scratch=(), cycles=0):
    specs = [
        pl.BlockSpec(memory_space=pltpu.SMEM if value.size == 1 else pltpu.VMEM) for value in inputs
    ]
    shapes = [jax.ShapeDtypeStruct(shape, jnp.float32) for shape in outs]
    return pl.pallas_call(
        kernel,
        out_shape=shapes if len(shapes) > 1 else shapes[0],
        in_specs=specs,
        out_specs=whole(len(shapes)) if len(shapes) > 1 else whole(1)[0],
        scratch_shapes=[pltpu.VMEM(shape, jnp.float32) for shape in scratch],
        name=name,
    )(*inputs)


def exchange(value):
    return lax.all_to_all(value, ("zx", "zy"), 0, 0, tiled=True)


def local(*arguments):
    materials, rows_x, rows_y = arguments[0].shape
    devices = lax.axis_size("zx") * lax.axis_size("zy")
    entries, nblocks = arguments[6].shape[2], arguments[9].shape[2]
    fits = (rows_x, rows_y, nblocks) == (64, 256, LANES) and materials == 8
    if fits and devices == LANES // QUAD and entries == 2 * LANES:
        return local_by_zones(*arguments)
    return local_by_entries(*arguments)


def local_by_zones(
    frac, density, energy, node_shift, node_speed, dest_tile, src_block, dest_block, crossing, keep
):
    materials, rows_x, rows_y = frac.shape
    devices = lax.axis_size("zx") * lax.axis_size("zy")
    fields = 3 * materials
    rows = fields * QUAD
    plane = (2, rows_x, rows_y)
    sums, rim = call(
        sums_kernel, "sums", [plane, (16, rows_y)], (frac, density, energy, node_shift, node_speed)
    )
    above = shifted(rim, "zx", -1)
    below = above if lax.axis_size("zx") == 2 else shifted(rim, "zx", 1)
    tall = (rows_x + SUB, LANES)
    extended, first, last = call(
        rows_kernel,
        "rows",
        [(6, rows_x + SUB, rows_y), tall, tall],
        (node_shift, node_speed, sums, above, below),
    )
    right = shifted(first, "zy", -1)
    left = shifted(last, "zy", 1)
    me = (lax.axis_index("zx") * lax.axis_size("zy") + lax.axis_index("zy")).astype(jnp.int32)
    tables = call(
        table_kernel,
        "tables",
        [(16, LANES)],
        (me.reshape(1, 1), dest_tile[0, 0], src_block[0], dest_block[0], crossing[0], keep[0]),
    )
    raw = call(pack_kernel, "pack", [(devices, rows, LANES)], (frac, density, energy))
    speed_after, shift_after, state = call(
        lagrange_kernel,
        "lagrange",
        [plane, plane, (devices, rows + 2 * SUB, LANES)],
        (extended, right, left, raw, tables),
    )
    state = exchange(state)
    groups = devices // SUB
    totals = call(
        crossing_kernel,
        "crossings",
        [(devices, rows, LANES)],
        (state,),
        scratch=[(devices, groups, rows, LANES), (devices, groups, SUB, LANES)],
    )
    totals = exchange(totals)
    remapped = call(unpack_kernel, "unpack", [(fields, rows_x, rows_y)], (totals,))
    return (remapped.reshape(3, materials, rows_x, rows_y), speed_after, shift_after)


def local_by_entries(
    frac, density, energy, node_shift, node_speed, dest_tile, src_block, dest_block, crossing, keep
):
    materials, rows_x, rows_y = frac.shape
    node_fields = jnp.concatenate([node_shift, node_speed], axis=0)
    extended = upper_rim(node_fields)
    area_now, mat_pressure, viscous, terms = zone_phase(
        frac, density, energy, slice_corners(extended[0:2]), slice_corners(extended[2:4])
    )
    term_one, term_two, term_three, term_four = terms
    gathered = (
        jnp.pad(term_one, ((0, 0), (0, 1), (0, 1)))
        + jnp.pad(term_two, ((0, 0), (1, 0), (0, 1)))
        + jnp.pad(term_three, ((0, 0), (1, 0), (1, 0)))
        + jnp.pad(term_four, ((0, 0), (0, 1), (1, 0)))
    )
    totals = spill_rim(gathered)
    speed_after, shift_after = node_update(totals, node_shift, node_speed)
    moved_rim = upper_rim(shift_after)
    area_after = zone_area(slice_corners(moved_rim))
    conserved = material_state(frac, density, energy, area_now, area_after, mat_pressure, viscous)
    nblocks = keep.shape[2]
    block_len = rows_x * rows_y // nblocks
    fields = 3 * materials
    blocks = conserved.reshape(fields, nblocks, block_len)
    size_x = lax.axis_size("zx")
    size_y = lax.axis_size("zy")
    devices = size_x * size_y
    targets = dest_tile[0, 0, :, 0]
    sources = src_block[0, 0]
    places = dest_block[0, 0]
    weights = crossing[0, 0]
    entry_count = targets.shape[0]
    capacity = max(2, 2 * entry_count // devices)
    member = (targets[:, None] == jnp.arange(devices, dtype=jnp.int32)[None, :]).astype(jnp.int32)
    before = jnp.cumsum(member, axis=0) - member
    slot_rank = jnp.sum(before * member, axis=1)
    slot_index = targets * capacity + slot_rank
    slot_total = devices * capacity
    matches = slot_index[:, None] == jnp.arange(slot_total, dtype=jnp.int32)[None, :]
    filled = jnp.any(matches, axis=0)
    owners = jnp.sum(
        jnp.where(matches, jnp.arange(entry_count, dtype=jnp.int32)[:, None], 0), axis=0
    )
    slot_weight = jnp.where(filled, weights[owners], 0.0)
    slot_place = jnp.where(filled, places[owners], nblocks)
    payload = blocks[:, sources[owners], :] * slot_weight[None, :, None]
    payload = payload.reshape(fields, size_x, size_y, capacity, block_len)
    place_ids = slot_place.reshape(1, size_x, size_y, capacity)
    arrived, arrived_ids = (
        lax.all_to_all(
            lax.all_to_all(payload, "zx", split_axis=1, concat_axis=1, tiled=True),
            "zy",
            split_axis=2,
            concat_axis=2,
            tiled=True,
        ),
        lax.all_to_all(
            lax.all_to_all(place_ids, "zx", split_axis=1, concat_axis=1, tiled=True),
            "zy",
            split_axis=2,
            concat_axis=2,
            tiled=True,
        ),
    )
    arrived = arrived.reshape(fields, slot_total, block_len)
    arrived_ids = arrived_ids.reshape(slot_total)
    landed = (
        jnp.zeros((fields, nblocks + 1, block_len), jnp.float32).at[:, arrived_ids, :].add(arrived)
    )
    result = blocks * keep[0, 0][None, :, None] + landed[:, :nblocks, :]
    remapped = result.reshape(3, materials, rows_x, rows_y)
    return (remapped, speed_after, shift_after)


def solution(mesh):
    in_specs = (
        P(None, "zx", "zy"),
        P(None, "zx", "zy"),
        P(None, "zx", "zy"),
        P(None, "zx", "zy"),
        P(None, "zx", "zy"),
        P("zx", "zy", None, None),
        P("zx", "zy", None),
        P("zx", "zy", None),
        P("zx", "zy", None),
        P("zx", "zy", None),
    )
    out_specs = (P(None, None, "zx", "zy"), P(None, "zx", "zy"), P(None, "zx", "zy"))
    return jax.shard_map(local, mesh=mesh, in_specs=in_specs, out_specs=out_specs, check_vma=False)
```

```python
import jax
import jax.numpy as jnp
import numpy as np
from jax import lax
from jax.experimental import pallas as pl
from jax.experimental.pallas import tpu as pltpu
from jax.sharding import PartitionSpec as P

TIME_STEP = 0.02
VISC_COEF = 0.25


def shifted(value, axis, by):
    peers = lax.axis_size(axis)
    return lax.ppermute(value, axis, [(i, (i + by) % peers) for i in range(peers)])


def corner_geometry(corners):
    corner_one, corner_two, corner_three, corner_four = corners
    rise_x = 1.0 + corner_three[0] - corner_one[0]
    rise_y = 1.0 + corner_three[1] - corner_one[1]
    cross_x = -1.0 + corner_four[0] - corner_two[0]
    cross_y = 1.0 + corner_four[1] - corner_two[1]
    return (rise_x, rise_y, cross_x, cross_y)


def zone_area(corners):
    rise_x, rise_y, cross_x, cross_y = corner_geometry(corners)
    return 0.5 * (rise_x * cross_y - cross_x * rise_y)


def zone_phase(frac, density, energy, shifts, speeds):
    rise_x, rise_y, cross_x, cross_y = corner_geometry(shifts)
    area_now = 0.5 * (rise_x * cross_y - cross_x * rise_y)
    speed_one, speed_two, speed_three, speed_four = speeds
    area_rate = 0.5 * (
        (speed_three[0] - speed_one[0]) * cross_y
        + rise_x * (speed_four[1] - speed_two[1])
        - (speed_four[0] - speed_two[0]) * rise_y
        - cross_x * (speed_three[1] - speed_one[1])
    )
    squeeze = jnp.minimum(area_rate / area_now, 0.0)
    gammas = (1.3 + 0.05 * jnp.arange(frac.shape[0], dtype=jnp.int32).astype(jnp.float32))[
        :, None, None
    ]
    mat_pressure = (gammas - 1.0) * density * energy
    zone_density = jnp.sum(frac * density, axis=0)
    viscous = VISC_COEF * zone_density * area_now * squeeze * squeeze
    total_pressure = jnp.sum(frac * mat_pressure, axis=0) + viscous
    half_press = 0.5 * total_pressure
    quarter_mass = 0.25 * zone_density * area_now
    term_one = jnp.stack([-half_press * cross_y, half_press * cross_x, quarter_mass])
    term_two = jnp.stack([half_press * rise_y, -half_press * rise_x, quarter_mass])
    term_three = jnp.stack([half_press * cross_y, -half_press * cross_x, quarter_mass])
    term_four = jnp.stack([-half_press * rise_y, half_press * rise_x, quarter_mass])
    return (area_now, mat_pressure, viscous, (term_one, term_two, term_three, term_four))


def node_update(totals, node_shift, node_speed):
    accel_xy = totals[0:2] / totals[2:3]
    speed_after = node_speed + TIME_STEP * accel_xy
    shift_after = node_shift + TIME_STEP * speed_after
    return (speed_after, shift_after)


def material_state(frac, density, energy, area_now, area_after, mat_pressure, viscous):
    energy_after = energy - (mat_pressure + viscous) * (area_after - area_now) / (
        density * area_now
    )
    volume = frac * area_after
    mass_now = frac * density * area_now
    return jnp.stack([volume, mass_now, mass_now * energy_after])


def upper_along_x(values):
    received = shifted(values[:, 0:1, :], "zx", -1)
    return jnp.concatenate([values, received], axis=1)


def upper_along_y(values):
    received = shifted(values[:, :, 0:1], "zy", -1)
    return jnp.concatenate([values, received], axis=2)


def upper_rim(values):
    return upper_along_y(upper_along_x(values))


def spill_along_x(values):
    received = shifted(values[:, -1:, :], "zx", 1)
    return jnp.concatenate([values[:, 0:1, :] + received, values[:, 1:-1, :]], axis=1)


def spill_along_y(values):
    received = shifted(values[:, :, -1:], "zy", 1)
    return jnp.concatenate([values[:, :, 0:1] + received, values[:, :, 1:-1]], axis=2)


def spill_rim(values):
    return spill_along_y(spill_along_x(values))


def slice_corners(extended):
    return (extended[:, :-1, :-1], extended[:, 1:, :-1], extended[:, 1:, 1:], extended[:, :-1, 1:])


SUB = 8
LANES = 128
QUAD = 4


def lower_half(shape):
    return lax.broadcasted_iota(jnp.int32, shape, len(shape) - 2) % SUB < QUAD


def zones_first(field):
    return jnp.concatenate([field[:, :LANES], field[:, LANES:]], axis=0).T


def pair_to_pieces(first, second, low):
    even = jnp.where(low, first, pltpu.roll(second, QUAD, 0))
    odd = jnp.where(low, pltpu.roll(first, QUAD, 0), second)
    return even, odd


def store_pairs(values, out_ref, row):
    low = lower_half((SUB, LANES))
    for pair in range(len(values) // 2):
        first, second = zones_first(values[2 * pair]), zones_first(values[2 * pair + 1])
        rows = slice(row + SUB * pair, row + SUB * pair + SUB)
        for octet in range(LANES // SUB):
            at = slice(SUB * octet, SUB * octet + SUB)
            even, odd = pair_to_pieces(first[at], second[at], low)
            out_ref[2 * octet, rows, :] = even
            out_ref[2 * octet + 1, rows, :] = odd


def split3(value):
    high = value.astype(jnp.bfloat16)
    left = value - high.astype(jnp.float32)
    middle = left.astype(jnp.bfloat16)
    low = (left - middle.astype(jnp.float32)).astype(jnp.bfloat16)
    return high, middle, low


def table_kernel(target_ref, source_ref, place_ref, weight_ref, keep_ref, out_ref):
    entries = target_ref.shape[0]
    column = target_ref[...].astype(jnp.float32)
    down = lax.broadcasted_iota(jnp.int32, (entries, entries), 0)
    across = lax.broadcasted_iota(jnp.int32, (entries, entries), 1)
    row = jnp.sum(jnp.where(down == across, column, 0.0), axis=0, keepdims=True)
    earlier = (row < column) | ((row == column) & (across < down))
    order = jnp.sum(jnp.where(earlier, 1.0, 0.0), axis=1, keepdims=True)
    hot = jnp.where(across.astype(jnp.float32) == order, 1.0, 0.0)
    source, place = source_ref[...], place_ref[...]
    half = LANES // 2
    source = ((source & 1) * half + (source >> 1)).astype(jnp.float32)
    place = ((place & 1) * half + (place >> 1)).astype(jnp.float32)
    parts = [part.astype(jnp.float32) for part in split3(weight_ref[...])] + [source, place]
    values = jnp.concatenate(parts + [jnp.zeros((SUB - len(parts), entries), jnp.float32)], axis=0)
    tables = jnp.dot(
        values.astype(jnp.bfloat16), hot.astype(jnp.bfloat16), preferred_element_type=jnp.float32
    )
    weights = tables[0:1] + tables[1:2] + tables[2:3]
    for table, value in enumerate((tables[3:4], weights, tables[4:5])):
        for side in range(2):
            at = slice(LANES * side, LANES * side + LANES)
            out_ref[2 * table + side : 2 * table + side + 1, :] = value[:, at]
    device = lax.broadcasted_iota(jnp.int32, (entries, LANES), 1).astype(jnp.float32)
    out_ref[6:7, :] = jnp.sum(jnp.where(column < device, 1.0, 0.0), axis=0, keepdims=True)
    lane = lax.broadcasted_iota(jnp.int32, (SUB, LANES), 1)
    keep = jnp.take_along_axis(
        jnp.broadcast_to(keep_ref[...], (SUB, LANES)),
        2 * (lane % half) + lane // half,
        axis=1,
        mode="promise_in_bounds",
    )
    out_ref[7:8, :] = keep[0:1]


def stiffness(materials):
    gammas = np.float32(1.3) + np.float32(0.05) * np.arange(materials, dtype=np.float32)
    return [float(gamma) for gamma in gammas - np.float32(1.0)]


def early_kernel(
    frac_ref, density_ref, energy_ref, shift_ref, speed_ref, out_ref, sums_ref, rim_ref
):
    materials = frac_ref.shape[0]
    stiff = stiffness(materials)
    mass = pressure = None
    held = []
    for material in range(materials):
        part = frac_ref[material] * density_ref[material]
        force = part * energy_ref[material] * stiff[material]
        mass = part if mass is None else mass + part
        pressure = force if pressure is None else pressure + force
        held.append(part)
    sums_ref[0], sums_ref[1] = mass, pressure
    last = mass.shape[0] - 1
    for field in range(2):
        for at, ref in ((0, shift_ref), (4, speed_ref)):
            rim_ref[at + 2 * field : at + 2 * field + 2, :] = ref[field, 0:2, :]
            rim_ref[10 + at // 2 + field : 11 + at // 2 + field, :] = ref[field, last : last + 1, :]
    for field, value in enumerate((mass, pressure)):
        rim_ref[8 + field : 9 + field, :] = value[0:1]
        rim_ref[14 + field : 15 + field, :] = value[last : last + 1]
    store_pairs([frac_ref[material] for material in range(materials)] + held, out_ref, 0)


def rows_kernel(shift_ref, speed_ref, sums_ref, above_ref, below_ref, out_ref, first_ref, last_ref):
    height, width = shift_ref.shape[1:]
    for field in range(6):
        value = (shift_ref, speed_ref, sums_ref)[field // 2][field % 2]
        out_ref[field, 1 : height + 1, :] = value
        out_ref[field, 0:1, :] = below_ref[10 + field : 11 + field, :]
        if field < 4:
            out_ref[field, height + 1 : height + 3, :] = above_ref[2 * field : 2 * field + 2, :]
        else:
            for row in (1, 2):
                out_ref[field, height + row : height + row + 1, :] = above_ref[4 + field : 5 + field, :]
        out_ref[field, height + 3 : height + 8, :] = jnp.zeros((5, width), jnp.float32)
        whole_column = out_ref[field]
        if field < 4:
            first_ref[:, 2 * field : 2 * field + 2] = whole_column[:, 0:2]
        else:
            first_ref[:, 4 + field : 5 + field] = whole_column[:, 0:1]
        last_ref[:, field : field + 1] = whole_column[:, width - 1 : width]


def lagrange_kernel(
    rows_ref, right_ref, left_ref, frac_ref, density_ref, energy_ref, tables_ref,
    speed_ref, shift_ref, out_ref,
):
    height, width = rows_ref.shape[1] - SUB, rows_ref.shape[2]
    shape = (height + SUB, width + LANES)
    lane = lax.broadcasted_iota(jnp.int32, shape, 1)
    right, left = right_ref[...], left_ref[...]

    def extend(field):
        value = jnp.concatenate([rows_ref[field], jnp.zeros((shape[0], LANES), jnp.float32)], axis=1)
        value = pltpu.roll(value, 1, 1)
        value = jnp.where(lane == 0, left[:, field : field + 1], value)
        if field < 4:
            value = jnp.where(lane == width + 1, right[:, 2 * field : 2 * field + 1], value)
            return jnp.where(lane == width + 2, right[:, 2 * field + 1 : 2 * field + 2], value)
        return jnp.where(lane == width + 1, right[:, 4 + field : 5 + field], value)

    def next_row(value):
        return pltpu.roll(value, shape[0] - 1, 0)

    def next_column(value):
        return pltpu.roll(value, shape[1] - 1, 1)

    def before_row(value):
        return pltpu.roll(value, 1, 0)

    def before_column(value):
        return pltpu.roll(value, 1, 1)

    def diagonals(value):
        across = next_column(value)
        down = next_row(value)
        return next_row(across) - value, across - down

    def geometry(shift_x, shift_y):
        rise_x, cross_x = diagonals(shift_x)
        rise_y, cross_y = diagonals(shift_y)
        return 1.0 + rise_x, 1.0 + rise_y, -1.0 + cross_x, 1.0 + cross_y

    shift_x, shift_y, speed_x, speed_y, density, pressure = [extend(field) for field in range(6)]
    rise_x, rise_y, cross_x, cross_y = geometry(shift_x, shift_y)
    area = 0.5 * (rise_x * cross_y - cross_x * rise_y)
    up_x, over_x = diagonals(speed_x)
    up_y, over_y = diagonals(speed_y)
    rate = 0.5 * (up_x * cross_y + rise_x * over_y - over_x * rise_y - cross_x * up_y)
    squeeze = jnp.minimum(rate / area, 0.0)
    viscous = VISC_COEF * density * area * squeeze * squeeze
    half = 0.5 * (pressure + viscous)
    quarter = 0.25 * density * area

    def corners(one, two, sign):
        upper = before_row(two - before_column(one))
        return sign * (one - before_column(two) + upper)

    force_x = corners(-half * cross_y, half * rise_y, 1.0)
    force_y = corners(half * cross_x, -half * rise_x, 1.0)
    both = quarter + before_column(quarter)
    mass = both + before_row(both)
    speed_x = speed_x + TIME_STEP * (force_x / mass)
    speed_y = speed_y + TIME_STEP * (force_y / mass)
    shift_x = shift_x + TIME_STEP * speed_x
    shift_y = shift_y + TIME_STEP * speed_y
    rise_x, rise_y, cross_x, cross_y = geometry(shift_x, shift_y)
    after = 0.5 * (rise_x * cross_y - cross_x * rise_y)

    def own(value):
        return next_column(next_row(value))[0:height, 0:width]

    speed_ref[0], speed_ref[1] = own(speed_x), own(speed_y)
    shift_ref[0], shift_ref[1] = own(shift_x), own(shift_y)

    area, after, viscous = own(area), own(after), own(viscous)
    change = after - area
    materials = frac_ref.shape[0]
    values = []
    for material, stiff in enumerate(stiffness(materials)):
        frac, density, energy = frac_ref[material], density_ref[material], energy_ref[material]
        force = stiff * density * energy + viscous
        values.append(frac * density * area * energy - frac * force * change)
    store_pairs(values + [area, after], out_ref, 0)
    for piece in range(out_ref.shape[0]):
        out_ref[piece, (materials + 2) * QUAD : (materials + 2) * QUAD + SUB] = tables_ref[...]


def crossing_kernel(
    early_ref, late_ref, out_ref, state_ref, even_ref, odd_ref, places_ref, sources_ref, weights_ref
):
    devices, rows = state_ref.shape[0], state_ref.shape[1]
    table_row = late_ref.shape[1] - SUB
    tiles = rows // SUB
    groups = devices // SUB
    capacity = LANES // SUB
    slots_ref = (even_ref, odd_ref)
    spread = (SUB, LANES)
    lane = lax.broadcasted_iota(jnp.int32, spread, 1)
    source_of = lax.broadcasted_iota(jnp.int32, spread, 0)
    piece = lane // capacity
    odd = [(piece >> bit) & 1 == 1 for bit in range(3)]

    def take(values, index):
        return jnp.take_along_axis(values, index, axis=1, mode="promise_in_bounds")

    def regroup(values):
        for bit in range(3):
            values = [
                jnp.where(odd[bit], values[i | (1 << bit)], values[i & ~(1 << bit)])
                if not (i >> bit) & 1
                else jnp.where(odd[bit], values[i & ~(1 << bit)], values[i | (1 << bit)])
                for i in range(SUB)
            ]
        return values

    low = lower_half(spread)
    third = rows // 3

    def conserve(source, carry):
        areas = late_ref[source, third : third + SUB]
        swapped = pltpu.roll(areas, QUAD, 0)
        area, after = jnp.where(low, areas, swapped), jnp.where(low, swapped, areas)
        for tile in range(tiles // 3):
            at = [slice(SUB * tile + third * g, SUB * tile + third * g + SUB) for g in range(3)]
            state_ref[source, at[0]] = early_ref[source, at[0]] * after
            state_ref[source, at[1]] = early_ref[source, at[1]] * area
            state_ref[source, at[2]] = late_ref[source, at[0]]
        return carry

    lax.fori_loop(0, devices, conserve, 0, unroll=4)
    for a in range(groups):
        table = [late_ref[a * SUB : a * SUB + SUB, table_row + i, :] for i in range(7)]
        starts = table[6].astype(jnp.int32)
        for octet in range(groups):
            target = SUB * octet + (piece ^ source_of)
            at = take(starts, target) + lane % capacity
            valid = at < take(starts, target + 1)
            later, at = at >= LANES, at & (LANES - 1)
            source, weight, place = [
                jnp.where(later, take(table[2 * i + 1], at), take(table[2 * i], at)) for i in range(3)
            ]
            sources_ref[octet, a] = source
            weights_ref[octet, a] = jnp.where(valid, weight, 0.0)
            places = [jnp.broadcast_to(place[i : i + 1], spread) for i in range(SUB)]
            for delta, value in enumerate(regroup(places)):
                places_ref[SUB * octet + delta, a] = value

    def gather(octet, a):
        sources, weights = sources_ref[octet, a].astype(jnp.int32), weights_ref[octet, a]
        index = [jnp.broadcast_to(sources[i : i + 1], spread) for i in range(SUB)]
        weight = [jnp.broadcast_to(weights[i : i + 1], spread) for i in range(SUB)]
        for first in range(0, tiles, tiles // 2):
            at = [slice(SUB * tile, SUB * tile + SUB) for tile in range(first, first + tiles // 2)]
            values = [
                [take(state_ref[a * SUB + i, rows_of], index[i]) * weight[i] for rows_of in at]
                for i in range(SUB)
            ]
            for tile, rows_of in enumerate(at):
                for delta, value in enumerate(regroup([value[tile] for value in values])):
                    slots_ref[octet % 2][delta, a, rows_of] = value

    block = lax.broadcasted_iota(jnp.int32, spread, 0).astype(jnp.float32)

    def scatter(octet, delta):
        target = SUB * octet + delta
        slots = slots_ref[octet % 2]
        value = jnp.concatenate([slots[delta, a] for a in range(groups)], axis=1)
        parts = jnp.concatenate(split3(value), axis=0)
        place = [places_ref[target, a] for a in range(groups)]
        hot = [
            [
                jnp.where(place[a] == block + float(SUB * tile), 1.0, 0.0)
                for tile in range(LANES // SUB)
            ]
            for a in range(groups)
        ]
        hot = jnp.concatenate([jnp.concatenate(column, axis=0) for column in hot], axis=1)
        total = lax.dot_general(
            parts,
            hot.astype(jnp.bfloat16),
            (((1,), (1,)), ((), ())),
            preferred_element_type=jnp.float32,
        )
        keep = jnp.broadcast_to(late_ref[target, table_row + 7 : table_row + 8], (rows, LANES))
        stay = keep * state_ref[target, 0:rows]
        out_ref[target] = stay + total[0:rows] + total[rows : 2 * rows] + total[2 * rows : 3 * rows]

    lax.fori_loop(0, groups, lambda a, carry: (gather(0, a), carry)[1], 0)
    for octet in range(groups):

        def step(a, carry):
            if octet + 1 < groups:
                gather(octet + 1, a)
            for i in range(SUB // groups):
                scatter(octet, SUB // groups * a + i)
            return carry

        lax.fori_loop(0, groups, step, 0, unroll=True)


def unpack_kernel(sums_ref, out_ref):
    low = lower_half((SUB, LANES))
    half = LANES // 2
    for pair in range(sums_ref.shape[1] // SUB):
        at = slice(SUB * pair, SUB * pair + SUB)
        first, second = [], []
        for octet in range(LANES // SUB):
            even, odd = pair_to_pieces(sums_ref[2 * octet, at], sums_ref[2 * octet + 1, at], low)
            first.append(even)
            second.append(odd)
        for field, tiles in ((2 * pair, first), (2 * pair + 1, second)):
            blocks = jnp.concatenate(tiles, axis=0).T
            out_ref[field, :, :LANES] = blocks[:half]
            out_ref[field, :, LANES:] = blocks[half:]


def whole(count):
    return [pl.BlockSpec(memory_space=pltpu.VMEM)] * count


def call(kernel, name, outs, inputs, scratch=()):
    shapes = [jax.ShapeDtypeStruct(shape, jnp.float32) for shape in outs]
    return pl.pallas_call(
        kernel,
        out_shape=shapes if len(shapes) > 1 else shapes[0],
        in_specs=whole(len(inputs)),
        out_specs=whole(len(shapes)) if len(shapes) > 1 else whole(1)[0],
        scratch_shapes=[pltpu.VMEM(shape, jnp.float32) for shape in scratch],
        name=name,
    )(*inputs)


def exchange(value):
    return lax.all_to_all(value, ("zx", "zy"), 0, 0, tiled=True)


def local(*arguments):
    materials, rows_x, rows_y = arguments[0].shape
    devices = lax.axis_size("zx") * lax.axis_size("zy")
    entries, nblocks = arguments[6].shape[2], arguments[9].shape[2]
    fits = (rows_x, rows_y, nblocks) == (64, 256, LANES) and materials == 8
    if fits and devices == LANES // QUAD and entries == 2 * LANES:
        return local_by_zones(*arguments)
    return local_by_entries(*arguments)


def local_by_zones(
    frac, density, energy, node_shift, node_speed, dest_tile, src_block, dest_block, crossing, keep
):
    materials, rows_x, rows_y = frac.shape
    devices = lax.axis_size("zx") * lax.axis_size("zy")
    fields = 3 * materials
    rows = fields * QUAD
    plane = (2, rows_x, rows_y)
    early, sums, rim = call(
        early_kernel,
        "early",
        [(devices, 2 * materials * QUAD, LANES), plane, (16, rows_y)],
        (frac, density, energy, node_shift, node_speed),
    )
    early = exchange(early)
    above = shifted(rim, "zx", -1)
    below = above if lax.axis_size("zx") == 2 else shifted(rim, "zx", 1)
    tall = (rows_x + SUB, LANES)
    extended, first, last = call(
        rows_kernel,
        "rows",
        [(6, rows_x + SUB, rows_y), tall, tall],
        (node_shift, node_speed, sums, above, below),
    )
    right = shifted(first, "zy", -1)
    left = shifted(last, "zy", 1)
    tables = call(
        table_kernel,
        "tables",
        [(SUB, LANES)],
        (dest_tile[0, 0], src_block[0], dest_block[0], crossing[0], keep[0]),
    )
    speed_after, shift_after, late = call(
        lagrange_kernel,
        "lagrange",
        [plane, plane, (devices, (materials + 2) * QUAD + SUB, LANES)],
        (extended, right, left, frac, density, energy, tables),
    )
    early, late = lax.optimization_barrier((early, late))
    late = exchange(late)
    groups = devices // SUB
    totals = call(
        crossing_kernel,
        "crossings",
        [(devices, rows, LANES)],
        (early, late),
        scratch=[(devices, rows, LANES)]
        + [(SUB, groups, rows, LANES)] * 2
        + [(devices, groups, SUB, LANES)]
        + [(groups, groups, SUB, LANES)] * 2,
    )
    totals = exchange(totals)
    remapped = call(unpack_kernel, "unpack", [(fields, rows_x, rows_y)], (totals,))
    return (remapped.reshape(3, materials, rows_x, rows_y), speed_after, shift_after)


def local_by_entries(
    frac, density, energy, node_shift, node_speed, dest_tile, src_block, dest_block, crossing, keep
):
    materials, rows_x, rows_y = frac.shape
    node_fields = jnp.concatenate([node_shift, node_speed], axis=0)
    extended = upper_rim(node_fields)
    area_now, mat_pressure, viscous, terms = zone_phase(
        frac, density, energy, slice_corners(extended[0:2]), slice_corners(extended[2:4])
    )
    term_one, term_two, term_three, term_four = terms
    gathered = (
        jnp.pad(term_one, ((0, 0), (0, 1), (0, 1)))
        + jnp.pad(term_two, ((0, 0), (1, 0), (0, 1)))
        + jnp.pad(term_three, ((0, 0), (1, 0), (1, 0)))
        + jnp.pad(term_four, ((0, 0), (0, 1), (1, 0)))
    )
    totals = spill_rim(gathered)
    speed_after, shift_after = node_update(totals, node_shift, node_speed)
    moved_rim = upper_rim(shift_after)
    area_after = zone_area(slice_corners(moved_rim))
    conserved = material_state(frac, density, energy, area_now, area_after, mat_pressure, viscous)
    nblocks = keep.shape[2]
    block_len = rows_x * rows_y // nblocks
    fields = 3 * materials
    blocks = conserved.reshape(fields, nblocks, block_len)
    size_x = lax.axis_size("zx")
    size_y = lax.axis_size("zy")
    devices = size_x * size_y
    targets = dest_tile[0, 0, :, 0]
    sources = src_block[0, 0]
    places = dest_block[0, 0]
    weights = crossing[0, 0]
    entry_count = targets.shape[0]
    capacity = max(2, 2 * entry_count // devices)
    member = (targets[:, None] == jnp.arange(devices, dtype=jnp.int32)[None, :]).astype(jnp.int32)
    before = jnp.cumsum(member, axis=0) - member
    slot_rank = jnp.sum(before * member, axis=1)
    slot_index = targets * capacity + slot_rank
    slot_total = devices * capacity
    matches = slot_index[:, None] == jnp.arange(slot_total, dtype=jnp.int32)[None, :]
    filled = jnp.any(matches, axis=0)
    owners = jnp.sum(
        jnp.where(matches, jnp.arange(entry_count, dtype=jnp.int32)[:, None], 0), axis=0
    )
    slot_weight = jnp.where(filled, weights[owners], 0.0)
    slot_place = jnp.where(filled, places[owners], nblocks)
    payload = blocks[:, sources[owners], :] * slot_weight[None, :, None]
    payload = payload.reshape(fields, size_x, size_y, capacity, block_len)
    place_ids = slot_place.reshape(1, size_x, size_y, capacity)
    arrived, arrived_ids = (
        lax.all_to_all(
            lax.all_to_all(payload, "zx", split_axis=1, concat_axis=1, tiled=True),
            "zy",
            split_axis=2,
            concat_axis=2,
            tiled=True,
        ),
        lax.all_to_all(
            lax.all_to_all(place_ids, "zx", split_axis=1, concat_axis=1, tiled=True),
            "zy",
            split_axis=2,
            concat_axis=2,
            tiled=True,
        ),
    )
    arrived = arrived.reshape(fields, slot_total, block_len)
    arrived_ids = arrived_ids.reshape(slot_total)
    landed = (
        jnp.zeros((fields, nblocks + 1, block_len), jnp.float32).at[:, arrived_ids, :].add(arrived)
    )
    result = blocks * keep[0, 0][None, :, None] + landed[:, :nblocks, :]
    remapped = result.reshape(3, materials, rows_x, rows_y)
    return (remapped, speed_after, shift_after)


def solution(mesh):
    in_specs = (
        P(None, "zx", "zy"),
        P(None, "zx", "zy"),
        P(None, "zx", "zy"),
        P(None, "zx", "zy"),
        P(None, "zx", "zy"),
        P("zx", "zy", None, None),
        P("zx", "zy", None),
        P("zx", "zy", None),
        P("zx", "zy", None),
        P("zx", "zy", None),
    )
    out_specs = (P(None, None, "zx", "zy"), P(None, "zx", "zy"), P(None, "zx", "zy"))
    return jax.shard_map(local, mesh=mesh, in_specs=in_specs, out_specs=out_specs, check_vma=False)
```

```python
import jax
import jax.numpy as jnp
import numpy as np
from jax import lax
from jax.experimental import pallas as pl
from jax.experimental.pallas import tpu as pltpu
from jax.sharding import PartitionSpec as P

TIME_STEP = 0.02
VISC_COEF = 0.25


def shifted(value, axis, by):
    peers = lax.axis_size(axis)
    return lax.ppermute(value, axis, [(i, (i + by) % peers) for i in range(peers)])


def corner_geometry(corners):
    corner_one, corner_two, corner_three, corner_four = corners
    rise_x = 1.0 + corner_three[0] - corner_one[0]
    rise_y = 1.0 + corner_three[1] - corner_one[1]
    cross_x = -1.0 + corner_four[0] - corner_two[0]
    cross_y = 1.0 + corner_four[1] - corner_two[1]
    return (rise_x, rise_y, cross_x, cross_y)


def zone_area(corners):
    rise_x, rise_y, cross_x, cross_y = corner_geometry(corners)
    return 0.5 * (rise_x * cross_y - cross_x * rise_y)


def zone_phase(frac, density, energy, shifts, speeds):
    rise_x, rise_y, cross_x, cross_y = corner_geometry(shifts)
    area_now = 0.5 * (rise_x * cross_y - cross_x * rise_y)
    speed_one, speed_two, speed_three, speed_four = speeds
    area_rate = 0.5 * (
        (speed_three[0] - speed_one[0]) * cross_y
        + rise_x * (speed_four[1] - speed_two[1])
        - (speed_four[0] - speed_two[0]) * rise_y
        - cross_x * (speed_three[1] - speed_one[1])
    )
    squeeze = jnp.minimum(area_rate / area_now, 0.0)
    gammas = (1.3 + 0.05 * jnp.arange(frac.shape[0], dtype=jnp.int32).astype(jnp.float32))[
        :, None, None
    ]
    mat_pressure = (gammas - 1.0) * density * energy
    zone_density = jnp.sum(frac * density, axis=0)
    viscous = VISC_COEF * zone_density * area_now * squeeze * squeeze
    total_pressure = jnp.sum(frac * mat_pressure, axis=0) + viscous
    half_press = 0.5 * total_pressure
    quarter_mass = 0.25 * zone_density * area_now
    term_one = jnp.stack([-half_press * cross_y, half_press * cross_x, quarter_mass])
    term_two = jnp.stack([half_press * rise_y, -half_press * rise_x, quarter_mass])
    term_three = jnp.stack([half_press * cross_y, -half_press * cross_x, quarter_mass])
    term_four = jnp.stack([-half_press * rise_y, half_press * rise_x, quarter_mass])
    return (area_now, mat_pressure, viscous, (term_one, term_two, term_three, term_four))


def node_update(totals, node_shift, node_speed):
    accel_xy = totals[0:2] / totals[2:3]
    speed_after = node_speed + TIME_STEP * accel_xy
    shift_after = node_shift + TIME_STEP * speed_after
    return (speed_after, shift_after)


def material_state(frac, density, energy, area_now, area_after, mat_pressure, viscous):
    energy_after = energy - (mat_pressure + viscous) * (area_after - area_now) / (
        density * area_now
    )
    volume = frac * area_after
    mass_now = frac * density * area_now
    return jnp.stack([volume, mass_now, mass_now * energy_after])


def upper_along_x(values):
    received = shifted(values[:, 0:1, :], "zx", -1)
    return jnp.concatenate([values, received], axis=1)


def upper_along_y(values):
    received = shifted(values[:, :, 0:1], "zy", -1)
    return jnp.concatenate([values, received], axis=2)


def upper_rim(values):
    return upper_along_y(upper_along_x(values))


def spill_along_x(values):
    received = shifted(values[:, -1:, :], "zx", 1)
    return jnp.concatenate([values[:, 0:1, :] + received, values[:, 1:-1, :]], axis=1)


def spill_along_y(values):
    received = shifted(values[:, :, -1:], "zy", 1)
    return jnp.concatenate([values[:, :, 0:1] + received, values[:, :, 1:-1]], axis=2)


def spill_rim(values):
    return spill_along_y(spill_along_x(values))


def slice_corners(extended):
    return (extended[:, :-1, :-1], extended[:, 1:, :-1], extended[:, 1:, 1:], extended[:, :-1, 1:])


SUB = 8
LANES = 128
QUAD = 4


def lower_half(shape):
    return lax.broadcasted_iota(jnp.int32, shape, len(shape) - 2) % SUB < QUAD


def zones_first(field):
    return jnp.concatenate([field[:, :LANES], field[:, LANES:]], axis=0).T


def pair_to_pieces(first, second, low):
    even = jnp.where(low, first, pltpu.roll(second, QUAD, 0))
    odd = jnp.where(low, pltpu.roll(first, QUAD, 0), second)
    return even, odd


def store_pairs(values, out_ref, row):
    low = lower_half((SUB, LANES))
    for pair in range(len(values) // 2):
        first, second = zones_first(values[2 * pair]), zones_first(values[2 * pair + 1])
        rows = slice(row + SUB * pair, row + SUB * pair + SUB)
        for octet in range(LANES // SUB):
            at = slice(SUB * octet, SUB * octet + SUB)
            even, odd = pair_to_pieces(first[at], second[at], low)
            out_ref[2 * octet, rows, :] = even
            out_ref[2 * octet + 1, rows, :] = odd


def split3(value):
    high = value.astype(jnp.bfloat16)
    left = value - high.astype(jnp.float32)
    middle = left.astype(jnp.bfloat16)
    low = (left - middle.astype(jnp.float32)).astype(jnp.bfloat16)
    return high, middle, low


def table_kernel(target_ref, source_ref, place_ref, weight_ref, keep_ref, out_ref):
    entries = target_ref.shape[1]
    row = target_ref[...].astype(jnp.float32)
    down = lax.broadcasted_iota(jnp.int32, (entries, entries), 0)
    across = lax.broadcasted_iota(jnp.int32, (entries, entries), 1)
    column = jnp.sum(jnp.where(down == across, row, 0.0), axis=1, keepdims=True)
    earlier = (row < column) | ((row == column) & (across < down))
    order = jnp.sum(jnp.where(earlier, 1.0, 0.0), axis=1, keepdims=True)
    hot = jnp.where(across.astype(jnp.float32) == order, 1.0, 0.0)
    source, place = source_ref[...], place_ref[...]
    half = LANES // 2
    source = ((source & 1) * half + (source >> 1)).astype(jnp.float32)
    place = ((place & 1) * half + (place >> 1)).astype(jnp.float32)
    parts = [part.astype(jnp.float32) for part in split3(weight_ref[...])] + [source, place]
    values = jnp.concatenate(parts + [jnp.zeros((SUB - len(parts), entries), jnp.float32)], axis=0)
    tables = jnp.dot(
        values.astype(jnp.bfloat16), hot.astype(jnp.bfloat16), preferred_element_type=jnp.float32
    )
    weights = tables[0:1] + tables[1:2] + tables[2:3]
    for table, value in enumerate((tables[3:4], weights, tables[4:5])):
        for side in range(2):
            at = slice(LANES * side, LANES * side + LANES)
            out_ref[2 * table + side : 2 * table + side + 1, :] = value[:, at]
    device = lax.broadcasted_iota(jnp.int32, (entries, LANES), 1).astype(jnp.float32)
    out_ref[6:7, :] = jnp.sum(jnp.where(column < device, 1.0, 0.0), axis=0, keepdims=True)
    lane = lax.broadcasted_iota(jnp.int32, (SUB, LANES), 1)
    keep = jnp.take_along_axis(
        jnp.broadcast_to(keep_ref[...], (SUB, LANES)),
        2 * (lane % half) + lane // half,
        axis=1,
        mode="promise_in_bounds",
    )
    out_ref[7:8, :] = keep[0:1]


def stiffness(materials):
    gammas = np.float32(1.3) + np.float32(0.05) * np.arange(materials, dtype=np.float32)
    return [float(gamma) for gamma in gammas - np.float32(1.0)]


def early_kernel(
    frac_ref, density_ref, energy_ref, shift_ref, speed_ref, out_ref, sums_ref, rim_ref
):
    materials = frac_ref.shape[0]
    stiff = stiffness(materials)
    mass = pressure = None
    held = []
    for material in range(materials):
        part = frac_ref[material] * density_ref[material]
        force = part * energy_ref[material] * stiff[material]
        mass = part if mass is None else mass + part
        pressure = force if pressure is None else pressure + force
        held.append(part)
    sums_ref[0], sums_ref[1] = mass, pressure
    last = mass.shape[0] - 1
    for field in range(2):
        for at, ref in ((0, shift_ref), (4, speed_ref)):
            rim_ref[at + 2 * field : at + 2 * field + 2, :] = ref[field, 0:2, :]
            for copy in range(2):
                row = 16 + at + 2 * field + copy
                rim_ref[row : row + 1, :] = ref[field, last : last + 1, :]
    for field, value in enumerate((mass, pressure)):
        rim_ref[8 + field : 9 + field, :] = value[0:1]
        rim_ref[24 + field : 25 + field, :] = value[last : last + 1]
    store_pairs([frac_ref[material] for material in range(materials)] + held, out_ref, 0)


def columns_kernel(shift_ref, speed_ref, sums_ref, out_ref):
    height, width = shift_ref.shape[1:]
    lane = lax.broadcasted_iota(jnp.int32, (height, LANES), 1)
    wanted = jnp.zeros((height, LANES), jnp.float32)
    for field in range(6):
        ref = (shift_ref, speed_ref, sums_ref)[field // 2]
        first = ref[field % 2, :, :LANES]
        last = ref[field % 2, :, width - LANES :]
        row = 2 * field if field < 4 else 4 + field
        for column in range(2 if field < 4 else 1):
            moved = pltpu.roll(first, row, 1) if row else first
            wanted = jnp.where(lane == row + column, moved, wanted)
        wanted = jnp.where(lane == 16 + row, pltpu.roll(last, 17 + row, 1), wanted)
    wanted = jnp.concatenate([wanted, jnp.zeros((LANES - height, LANES), jnp.float32)], axis=0)
    out_ref[...] = wanted.T[0 : out_ref.shape[0]]


def corners_kernel(columns_ref, above_ref, below_ref, first_ref, last_ref):
    height, width = 64, above_ref.shape[1]
    shape = (16, LANES)
    lane = lax.broadcasted_iota(jnp.int32, shape, 1)
    row = lax.broadcasted_iota(jnp.int32, shape, 0)
    second = (row % 2 == 1) & (row < 8)

    def column(ref, base, at):
        return jnp.broadcast_to(ref[base : base + 16, at : at + 1], shape)

    def up(value):
        return pltpu.roll(value, 15, 0)

    def down(value):
        return pltpu.roll(value, 1, 0)

    left, right = column(above_ref, 0, 0), column(above_ref, 0, 1)
    value = columns_ref[0:16]
    value = jnp.where(lane == height, jnp.where(second, down(right), left), value)
    value = jnp.where(lane == height + 1, jnp.where(second, right, up(left)), value)
    under = jnp.where(second, column(below_ref, 16, 1), column(below_ref, 16, 0))
    first_ref[...] = jnp.where(lane == LANES - 1, under, value)
    end = column(above_ref, 0, width - 1)
    value = jnp.where(lane == height, end, columns_ref[16:32])
    value = jnp.where(lane == height + 1, up(end), value)
    last_ref[...] = jnp.where(lane == LANES - 1, column(below_ref, 16, width - 1), value)


def lagrange_kernel(
    now_shift_ref,
    now_speed_ref,
    sums_ref,
    above_ref,
    below_ref,
    right_ref,
    left_ref,
    frac_ref,
    density_ref,
    energy_ref,
    tables_ref,
    speed_ref,
    shift_ref,
    out_ref,
):
    height, width = sums_ref.shape[1:]
    shape = (height + SUB, width + LANES)
    lane = lax.broadcasted_iota(jnp.int32, shape, 1)
    line = lax.broadcasted_iota(jnp.int32, (shape[0], width), 0)
    sides = [pltpu.roll(ref[...], 1, 1) for ref in (right_ref, left_ref)]
    sides.append(jnp.zeros((LANES - 32, LANES), jnp.float32))
    sides = jnp.concatenate(sides, axis=0).T[0 : shape[0]]

    def extend(field):
        value = (now_shift_ref, now_speed_ref, sums_ref)[field // 2][field % 2]
        value = jnp.concatenate([value, jnp.zeros((SUB, width), jnp.float32)], axis=0)
        value = pltpu.roll(value, 1, 0)
        at = 2 * field if field < 4 else 4 + field
        value = jnp.where(line == 0, below_ref[16 + at : 17 + at, :], value)
        value = jnp.where(line == height + 1, above_ref[at : at + 1, :], value)
        if field < 4:
            value = jnp.where(line == height + 2, above_ref[at + 1 : at + 2, :], value)
        value = jnp.concatenate([value, jnp.zeros((shape[0], LANES), jnp.float32)], axis=1)
        value = pltpu.roll(value, 1, 1)
        value = jnp.where(lane == 0, sides[:, 16 + at : 17 + at], value)
        value = jnp.where(lane == width + 1, sides[:, at : at + 1], value)
        if field < 4:
            value = jnp.where(lane == width + 2, sides[:, at + 1 : at + 2], value)
        return value

    def next_row(value):
        return pltpu.roll(value, shape[0] - 1, 0)

    def next_column(value):
        return pltpu.roll(value, shape[1] - 1, 1)

    def before_row(value):
        return pltpu.roll(value, 1, 0)

    def before_column(value):
        return pltpu.roll(value, 1, 1)

    def diagonals(value):
        across = next_column(value)
        down = next_row(value)
        return next_row(across) - value, across - down

    def geometry(shift_x, shift_y):
        rise_x, cross_x = diagonals(shift_x)
        rise_y, cross_y = diagonals(shift_y)
        return 1.0 + rise_x, 1.0 + rise_y, -1.0 + cross_x, 1.0 + cross_y

    shift_x, shift_y, speed_x, speed_y, density, pressure = [extend(field) for field in range(6)]
    rise_x, rise_y, cross_x, cross_y = geometry(shift_x, shift_y)
    area = 0.5 * (rise_x * cross_y - cross_x * rise_y)
    up_x, over_x = diagonals(speed_x)
    up_y, over_y = diagonals(speed_y)
    rate = 0.5 * (up_x * cross_y + rise_x * over_y - over_x * rise_y - cross_x * up_y)
    squeeze = jnp.minimum(rate / area, 0.0)
    viscous = VISC_COEF * density * area * squeeze * squeeze
    half = 0.5 * (pressure + viscous)
    quarter = 0.25 * density * area

    def corners(one, two, sign):
        upper = before_row(two - before_column(one))
        return sign * (one - before_column(two) + upper)

    force_x = corners(-half * cross_y, half * rise_y, 1.0)
    force_y = corners(half * cross_x, -half * rise_x, 1.0)
    both = quarter + before_column(quarter)
    mass = both + before_row(both)
    speed_x = speed_x + TIME_STEP * (force_x / mass)
    speed_y = speed_y + TIME_STEP * (force_y / mass)
    shift_x = shift_x + TIME_STEP * speed_x
    shift_y = shift_y + TIME_STEP * speed_y
    rise_x, rise_y, cross_x, cross_y = geometry(shift_x, shift_y)
    after = 0.5 * (rise_x * cross_y - cross_x * rise_y)

    def own(value):
        return next_column(next_row(value))[0:height, 0:width]

    speed_ref[0], speed_ref[1] = own(speed_x), own(speed_y)
    shift_ref[0], shift_ref[1] = own(shift_x), own(shift_y)

    area, after, viscous = own(area), own(after), own(viscous)
    change = after - area
    materials = frac_ref.shape[0]
    values = []
    for material, stiff in enumerate(stiffness(materials)):
        frac, density, energy = frac_ref[material], density_ref[material], energy_ref[material]
        force = stiff * density * energy + viscous
        values.append(frac * density * area * energy - frac * force * change)
    store_pairs(values + [area, after], out_ref, 0)
    for piece in range(out_ref.shape[0]):
        out_ref[piece, (materials + 2) * QUAD : (materials + 2) * QUAD + SUB] = tables_ref[...]


def crossing_kernel(
    early_ref, late_ref, out_ref, state_ref, even_ref, odd_ref, places_ref, sources_ref, weights_ref
):
    devices, rows = state_ref.shape[0], state_ref.shape[1]
    table_row = late_ref.shape[1] - SUB
    tiles = rows // SUB
    groups = devices // SUB
    capacity = LANES // SUB
    slots_ref = (even_ref, odd_ref)
    spread = (SUB, LANES)
    lane = lax.broadcasted_iota(jnp.int32, spread, 1)
    source_of = lax.broadcasted_iota(jnp.int32, spread, 0)
    piece = lane // capacity
    odd = [(piece >> bit) & 1 == 1 for bit in range(3)]

    def take(values, index):
        return jnp.take_along_axis(values, index, axis=1, mode="promise_in_bounds")

    def regroup(values):
        for bit in range(3):
            values = [
                jnp.where(odd[bit], values[i | (1 << bit)], values[i & ~(1 << bit)])
                if not (i >> bit) & 1
                else jnp.where(odd[bit], values[i & ~(1 << bit)], values[i | (1 << bit)])
                for i in range(SUB)
            ]
        return values

    low = lower_half(spread)
    third = rows // 3

    def conserve(source, carry):
        areas = late_ref[source, third : third + SUB]
        swapped = pltpu.roll(areas, QUAD, 0)
        area, after = jnp.where(low, areas, swapped), jnp.where(low, swapped, areas)
        for tile in range(tiles // 3):
            at = [slice(SUB * tile + third * g, SUB * tile + third * g + SUB) for g in range(3)]
            state_ref[source, at[0]] = early_ref[source, at[0]] * after
            state_ref[source, at[1]] = early_ref[source, at[1]] * area
            state_ref[source, at[2]] = late_ref[source, at[0]]
        return carry

    lax.fori_loop(0, devices, conserve, 0, unroll=4)
    for a in range(groups):
        table = [late_ref[a * SUB : a * SUB + SUB, table_row + i, :] for i in range(7)]
        starts = table[6].astype(jnp.int32)
        for octet in range(groups):
            target = SUB * octet + (piece ^ source_of)
            at = take(starts, target) + lane % capacity
            valid = at < take(starts, target + 1)
            later, at = at >= LANES, at & (LANES - 1)
            source, weight, place = [
                jnp.where(later, take(table[2 * i + 1], at), take(table[2 * i], at)) for i in range(3)
            ]
            sources_ref[octet, a] = source
            weights_ref[octet, a] = jnp.where(valid, weight, 0.0)
            places = [jnp.broadcast_to(place[i : i + 1], spread) for i in range(SUB)]
            for delta, value in enumerate(regroup(places)):
                places_ref[SUB * octet + delta, a] = value

    def gather(octet, a):
        sources, weights = sources_ref[octet, a].astype(jnp.int32), weights_ref[octet, a]
        index = [jnp.broadcast_to(sources[i : i + 1], spread) for i in range(SUB)]
        weight = [jnp.broadcast_to(weights[i : i + 1], spread) for i in range(SUB)]
        for first in range(0, tiles, tiles // 2):
            at = [slice(SUB * tile, SUB * tile + SUB) for tile in range(first, first + tiles // 2)]
            values = [
                [take(state_ref[a * SUB + i, rows_of], index[i]) * weight[i] for rows_of in at]
                for i in range(SUB)
            ]
            for tile, rows_of in enumerate(at):
                for delta, value in enumerate(regroup([value[tile] for value in values])):
                    slots_ref[octet % 2][delta, a, rows_of] = value

    block = lax.broadcasted_iota(jnp.int32, spread, 0).astype(jnp.float32)

    def scatter(octet, delta):
        target = SUB * octet + delta
        slots = slots_ref[octet % 2]
        value = jnp.concatenate([slots[delta, a] for a in range(groups)], axis=1)
        parts = jnp.concatenate(split3(value), axis=0)
        place = [places_ref[target, a] for a in range(groups)]
        hot = [
            [
                jnp.where(place[a] == block + float(SUB * tile), 1.0, 0.0)
                for tile in range(LANES // SUB)
            ]
            for a in range(groups)
        ]
        hot = jnp.concatenate([jnp.concatenate(column, axis=0) for column in hot], axis=1)
        total = lax.dot_general(
            parts,
            hot.astype(jnp.bfloat16),
            (((1,), (1,)), ((), ())),
            preferred_element_type=jnp.float32,
        )
        keep = jnp.broadcast_to(late_ref[target, table_row + 7 : table_row + 8], (rows, LANES))
        stay = keep * state_ref[target, 0:rows]
        out_ref[target] = stay + total[0:rows] + total[rows : 2 * rows] + total[2 * rows : 3 * rows]

    lax.fori_loop(0, groups, lambda a, carry: (gather(0, a), carry)[1], 0)
    for octet in range(groups):

        def step(a, carry):
            if octet + 1 < groups:
                gather(octet + 1, a)
            for i in range(SUB // groups):
                scatter(octet, SUB // groups * a + i)
            return carry

        lax.fori_loop(0, groups, step, 0, unroll=True)


UNPACK_PARTS = 4


def unpack_kernel(sums_ref, out_ref, rows_ref, sems):
    low = lower_half((SUB, LANES))
    half = LANES // 2
    fields = out_ref.shape[0] // UNPACK_PARTS
    copies = []
    for pair in range(sums_ref.shape[1] // SUB):
        at = slice(SUB * pair, SUB * pair + SUB)
        first, second = [], []
        for octet in range(LANES // SUB):
            even, odd = pair_to_pieces(sums_ref[2 * octet, at], sums_ref[2 * octet + 1, at], low)
            first.append(even)
            second.append(odd)
        for field, tiles in ((2 * pair, first), (2 * pair + 1, second)):
            blocks = jnp.concatenate(tiles, axis=0).T
            rows_ref[field, :, :LANES] = blocks[:half]
            rows_ref[field, :, LANES:] = blocks[half:]
        if (2 * pair + 2) % fields == 0:
            part = pl.ds(2 * pair + 2 - fields, fields)
            sem = sems.at[len(copies)]
            copies.append(pltpu.make_async_copy(rows_ref.at[part], out_ref.at[part], sem))
            copies[-1].start()
    for copy in copies:
        copy.wait()


def unpack(sums, shape):
    return pl.pallas_call(
        unpack_kernel,
        out_shape=jax.ShapeDtypeStruct(shape, jnp.float32),
        in_specs=whole(1),
        out_specs=pl.BlockSpec(memory_space=pl.ANY),
        scratch_shapes=[pltpu.VMEM(shape, jnp.float32), pltpu.SemaphoreType.DMA((UNPACK_PARTS,))],
        name="unpack",
    )(near(sums))


def whole(count):
    return [pl.BlockSpec(memory_space=pltpu.VMEM)] * count


def near(value):
    return pltpu.with_memory_space_constraint(value, pltpu.VMEM)


def call(kernel, name, outs, inputs, scratch=(), near_ins=(), near_outs=()):
    inputs = [
        near(value) if i in near_ins else value for i, value in enumerate(inputs)
    ]
    shapes = [
        pltpu.VMEM(shape, jnp.float32) if i in near_outs else jax.ShapeDtypeStruct(shape, jnp.float32)
        for i, shape in enumerate(outs)
    ]
    return pl.pallas_call(
        kernel,
        out_shape=shapes if len(shapes) > 1 else shapes[0],
        in_specs=whole(len(inputs)),
        out_specs=whole(len(shapes)) if len(shapes) > 1 else whole(1)[0],
        scratch_shapes=[pltpu.VMEM(shape, jnp.float32) for shape in scratch],
        name=name,
    )(*inputs)


def exchange(value):
    return lax.all_to_all(value, ("zx", "zy"), 0, 0, tiled=True)


def local(*arguments):
    materials, rows_x, rows_y = arguments[0].shape
    devices = lax.axis_size("zx") * lax.axis_size("zy")
    entries, nblocks = arguments[6].shape[2], arguments[9].shape[2]
    fits = (rows_x, rows_y, nblocks) == (64, 256, LANES) and materials == 8
    if fits and devices == LANES // QUAD and entries == 2 * LANES:
        return local_by_zones(*arguments)
    return local_by_entries(*arguments)


def local_by_zones(
    frac, density, energy, node_shift, node_speed, dest_tile, src_block, dest_block, crossing, keep
):
    materials, rows_x, rows_y = frac.shape
    devices = lax.axis_size("zx") * lax.axis_size("zy")
    fields = 3 * materials
    rows = fields * QUAD
    plane = (2, rows_x, rows_y)
    early, sums, rim = call(
        early_kernel,
        "early",
        [(devices, 2 * materials * QUAD, LANES), plane, (32, rows_y)],
        (frac, density, energy, node_shift, node_speed),
        near_outs=(0, 1, 2),
    )
    early = near(exchange(early))
    above = shifted(rim, "zx", -1)
    below = above if lax.axis_size("zx") == 2 else shifted(rim, "zx", 1)
    columns = call(columns_kernel, "columns", [(32, LANES)], (node_shift, node_speed, sums), near_ins=(2,), near_outs=(0,))
    first, last = call(corners_kernel, "corners", [(16, LANES)] * 2, (columns, above, below), near_ins=(0, 1, 2), near_outs=(0, 1))
    right = shifted(first, "zy", -1)
    left = shifted(last, "zy", 1)
    tables = call(
        table_kernel,
        "tables",
        [(SUB, LANES)],
        (dest_tile.reshape(1, -1), src_block[0], dest_block[0], crossing[0], keep[0]),
        near_outs=(0,),
    )
    speed_after, shift_after, late = call(
        lagrange_kernel,
        "lagrange",
        [plane, plane, (devices, (materials + 2) * QUAD + SUB, LANES)],
        (node_shift, node_speed, sums, above, below, right, left, frac, density, energy, tables),
        near_ins=(2, 3, 4, 5, 6, 7, 8, 9, 10),
        near_outs=(2,),
    )
    early, late = lax.optimization_barrier((early, late))
    late = exchange(late)
    groups = devices // SUB
    totals = call(
        crossing_kernel,
        "crossings",
        [(devices, rows, LANES)],
        (early, late),
        scratch=[(devices, rows, LANES)]
        + [(SUB, groups, rows, LANES)] * 2
        + [(devices, groups, SUB, LANES)]
        + [(groups, groups, SUB, LANES)] * 2,
        near_ins=(1,),
        near_outs=(0,),
    )
    totals = exchange(totals)
    remapped = unpack(totals, (fields, rows_x, rows_y))
    return (remapped.reshape(3, materials, rows_x, rows_y), speed_after, shift_after)


def local_by_entries(
    frac, density, energy, node_shift, node_speed, dest_tile, src_block, dest_block, crossing, keep
):
    materials, rows_x, rows_y = frac.shape
    node_fields = jnp.concatenate([node_shift, node_speed], axis=0)
    extended = upper_rim(node_fields)
    area_now, mat_pressure, viscous, terms = zone_phase(
        frac, density, energy, slice_corners(extended[0:2]), slice_corners(extended[2:4])
    )
    term_one, term_two, term_three, term_four = terms
    gathered = (
        jnp.pad(term_one, ((0, 0), (0, 1), (0, 1)))
        + jnp.pad(term_two, ((0, 0), (1, 0), (0, 1)))
        + jnp.pad(term_three, ((0, 0), (1, 0), (1, 0)))
        + jnp.pad(term_four, ((0, 0), (0, 1), (1, 0)))
    )
    totals = spill_rim(gathered)
    speed_after, shift_after = node_update(totals, node_shift, node_speed)
    moved_rim = upper_rim(shift_after)
    area_after = zone_area(slice_corners(moved_rim))
    conserved = material_state(frac, density, energy, area_now, area_after, mat_pressure, viscous)
    nblocks = keep.shape[2]
    block_len = rows_x * rows_y // nblocks
    fields = 3 * materials
    blocks = conserved.reshape(fields, nblocks, block_len)
    size_x = lax.axis_size("zx")
    size_y = lax.axis_size("zy")
    devices = size_x * size_y
    targets = dest_tile[0, 0, :, 0]
    sources = src_block[0, 0]
    places = dest_block[0, 0]
    weights = crossing[0, 0]
    entry_count = targets.shape[0]
    capacity = max(2, 2 * entry_count // devices)
    member = (targets[:, None] == jnp.arange(devices, dtype=jnp.int32)[None, :]).astype(jnp.int32)
    before = jnp.cumsum(member, axis=0) - member
    slot_rank = jnp.sum(before * member, axis=1)
    slot_index = targets * capacity + slot_rank
    slot_total = devices * capacity
    matches = slot_index[:, None] == jnp.arange(slot_total, dtype=jnp.int32)[None, :]
    filled = jnp.any(matches, axis=0)
    owners = jnp.sum(
        jnp.where(matches, jnp.arange(entry_count, dtype=jnp.int32)[:, None], 0), axis=0
    )
    slot_weight = jnp.where(filled, weights[owners], 0.0)
    slot_place = jnp.where(filled, places[owners], nblocks)
    payload = blocks[:, sources[owners], :] * slot_weight[None, :, None]
    payload = payload.reshape(fields, size_x, size_y, capacity, block_len)
    place_ids = slot_place.reshape(1, size_x, size_y, capacity)
    arrived, arrived_ids = (
        lax.all_to_all(
            lax.all_to_all(payload, "zx", split_axis=1, concat_axis=1, tiled=True),
            "zy",
            split_axis=2,
            concat_axis=2,
            tiled=True,
        ),
        lax.all_to_all(
            lax.all_to_all(place_ids, "zx", split_axis=1, concat_axis=1, tiled=True),
            "zy",
            split_axis=2,
            concat_axis=2,
            tiled=True,
        ),
    )
    arrived = arrived.reshape(fields, slot_total, block_len)
    arrived_ids = arrived_ids.reshape(slot_total)
    landed = (
        jnp.zeros((fields, nblocks + 1, block_len), jnp.float32).at[:, arrived_ids, :].add(arrived)
    )
    result = blocks * keep[0, 0][None, :, None] + landed[:, :nblocks, :]
    remapped = result.reshape(3, materials, rows_x, rows_y)
    return (remapped, speed_after, shift_after)


def solution(mesh):
    in_specs = (
        P(None, "zx", "zy"),
        P(None, "zx", "zy"),
        P(None, "zx", "zy"),
        P(None, "zx", "zy"),
        P(None, "zx", "zy"),
        P("zx", "zy", None, None),
        P("zx", "zy", None),
        P("zx", "zy", None),
        P("zx", "zy", None),
        P("zx", "zy", None),
    )
    out_specs = (P(None, None, "zx", "zy"), P(None, "zx", "zy"), P(None, "zx", "zy"))
    return jax.shard_map(local, mesh=mesh, in_specs=in_specs, out_specs=out_specs, check_vma=False)
```

```python
import jax
import jax.numpy as jnp
import numpy as np
from jax import lax
from jax.experimental import pallas as pl
from jax.experimental.pallas import tpu as pltpu
from jax.sharding import PartitionSpec as P

TIME_STEP = 0.02
VISC_COEF = 0.25


def shifted(value, axis, by):
    peers = lax.axis_size(axis)
    return lax.ppermute(value, axis, [(i, (i + by) % peers) for i in range(peers)])


def corner_geometry(corners):
    corner_one, corner_two, corner_three, corner_four = corners
    rise_x = 1.0 + corner_three[0] - corner_one[0]
    rise_y = 1.0 + corner_three[1] - corner_one[1]
    cross_x = -1.0 + corner_four[0] - corner_two[0]
    cross_y = 1.0 + corner_four[1] - corner_two[1]
    return (rise_x, rise_y, cross_x, cross_y)


def zone_area(corners):
    rise_x, rise_y, cross_x, cross_y = corner_geometry(corners)
    return 0.5 * (rise_x * cross_y - cross_x * rise_y)


def zone_phase(frac, density, energy, shifts, speeds):
    rise_x, rise_y, cross_x, cross_y = corner_geometry(shifts)
    area_now = 0.5 * (rise_x * cross_y - cross_x * rise_y)
    speed_one, speed_two, speed_three, speed_four = speeds
    area_rate = 0.5 * (
        (speed_three[0] - speed_one[0]) * cross_y
        + rise_x * (speed_four[1] - speed_two[1])
        - (speed_four[0] - speed_two[0]) * rise_y
        - cross_x * (speed_three[1] - speed_one[1])
    )
    squeeze = jnp.minimum(area_rate / area_now, 0.0)
    gammas = (1.3 + 0.05 * jnp.arange(frac.shape[0], dtype=jnp.int32).astype(jnp.float32))[
        :, None, None
    ]
    mat_pressure = (gammas - 1.0) * density * energy
    zone_density = jnp.sum(frac * density, axis=0)
    viscous = VISC_COEF * zone_density * area_now * squeeze * squeeze
    total_pressure = jnp.sum(frac * mat_pressure, axis=0) + viscous
    half_press = 0.5 * total_pressure
    quarter_mass = 0.25 * zone_density * area_now
    term_one = jnp.stack([-half_press * cross_y, half_press * cross_x, quarter_mass])
    term_two = jnp.stack([half_press * rise_y, -half_press * rise_x, quarter_mass])
    term_three = jnp.stack([half_press * cross_y, -half_press * cross_x, quarter_mass])
    term_four = jnp.stack([-half_press * rise_y, half_press * rise_x, quarter_mass])
    return (area_now, mat_pressure, viscous, (term_one, term_two, term_three, term_four))


def node_update(totals, node_shift, node_speed):
    accel_xy = totals[0:2] / totals[2:3]
    speed_after = node_speed + TIME_STEP * accel_xy
    shift_after = node_shift + TIME_STEP * speed_after
    return (speed_after, shift_after)


def material_state(frac, density, energy, area_now, area_after, mat_pressure, viscous):
    energy_after = energy - (mat_pressure + viscous) * (area_after - area_now) / (
        density * area_now
    )
    volume = frac * area_after
    mass_now = frac * density * area_now
    return jnp.stack([volume, mass_now, mass_now * energy_after])


def upper_along_x(values):
    received = shifted(values[:, 0:1, :], "zx", -1)
    return jnp.concatenate([values, received], axis=1)


def upper_along_y(values):
    received = shifted(values[:, :, 0:1], "zy", -1)
    return jnp.concatenate([values, received], axis=2)


def upper_rim(values):
    return upper_along_y(upper_along_x(values))


def spill_along_x(values):
    received = shifted(values[:, -1:, :], "zx", 1)
    return jnp.concatenate([values[:, 0:1, :] + received, values[:, 1:-1, :]], axis=1)


def spill_along_y(values):
    received = shifted(values[:, :, -1:], "zy", 1)
    return jnp.concatenate([values[:, :, 0:1] + received, values[:, :, 1:-1]], axis=2)


def spill_rim(values):
    return spill_along_y(spill_along_x(values))


def slice_corners(extended):
    return (extended[:, :-1, :-1], extended[:, 1:, :-1], extended[:, 1:, 1:], extended[:, :-1, 1:])


SUB = 8
LANES = 128
QUAD = 4


def lower_half(shape):
    return lax.broadcasted_iota(jnp.int32, shape, len(shape) - 2) % SUB < QUAD


def zones_first(field):
    return jnp.concatenate([field[:, :LANES], field[:, LANES:]], axis=0).T


def pair_to_pieces(first, second, low):
    even = jnp.where(low, first, pltpu.roll(second, QUAD, 0))
    odd = jnp.where(low, pltpu.roll(first, QUAD, 0), second)
    return even, odd


def store_pairs(values, out_ref, row):
    low = lower_half((SUB, LANES))
    for pair in range(len(values) // 2):
        first, second = zones_first(values[2 * pair]), zones_first(values[2 * pair + 1])
        rows = slice(row + SUB * pair, row + SUB * pair + SUB)
        for octet in range(LANES // SUB):
            at = slice(SUB * octet, SUB * octet + SUB)
            even, odd = pair_to_pieces(first[at], second[at], low)
            out_ref[2 * octet, rows, :] = even
            out_ref[2 * octet + 1, rows, :] = odd


def split3(value):
    high = value.astype(jnp.bfloat16)
    left = value - high.astype(jnp.float32)
    middle = left.astype(jnp.bfloat16)
    low = (left - middle.astype(jnp.float32)).astype(jnp.bfloat16)
    return high, middle, low


def table_kernel(target_ref, source_ref, place_ref, weight_ref, keep_ref, out_ref):
    entries = target_ref.shape[1]
    row = target_ref[...].astype(jnp.float32)
    down = lax.broadcasted_iota(jnp.int32, (entries, entries), 0)
    across = lax.broadcasted_iota(jnp.int32, (entries, entries), 1)
    column = jnp.sum(jnp.where(down == across, row, 0.0), axis=1, keepdims=True)
    earlier = (row < column) | ((row == column) & (across < down))
    order = jnp.sum(jnp.where(earlier, 1.0, 0.0), axis=1, keepdims=True)
    hot = jnp.where(across.astype(jnp.float32) == order, 1.0, 0.0)
    source, place = source_ref[...], place_ref[...]
    half = LANES // 2
    source = ((source & 1) * half + (source >> 1)).astype(jnp.float32)
    place = ((place & 1) * half + (place >> 1)).astype(jnp.float32)
    parts = [part.astype(jnp.float32) for part in split3(weight_ref[...])] + [source, place]
    values = jnp.concatenate(parts + [jnp.zeros((SUB - len(parts), entries), jnp.float32)], axis=0)
    tables = jnp.dot(
        values.astype(jnp.bfloat16), hot.astype(jnp.bfloat16), preferred_element_type=jnp.float32
    )
    weights = tables[0:1] + tables[1:2] + tables[2:3]
    for table, value in enumerate((tables[3:4], weights, tables[4:5])):
        for side in range(2):
            at = slice(LANES * side, LANES * side + LANES)
            out_ref[2 * table + side : 2 * table + side + 1, :] = value[:, at]
    device = lax.broadcasted_iota(jnp.int32, (entries, LANES), 1).astype(jnp.float32)
    out_ref[6:7, :] = jnp.sum(jnp.where(column < device, 1.0, 0.0), axis=0, keepdims=True)
    lane = lax.broadcasted_iota(jnp.int32, (SUB, LANES), 1)
    keep = jnp.take_along_axis(
        jnp.broadcast_to(keep_ref[...], (SUB, LANES)),
        2 * (lane % half) + lane // half,
        axis=1,
        mode="promise_in_bounds",
    )
    out_ref[7:8, :] = keep[0:1]


def stiffness(materials):
    gammas = np.float32(1.3) + np.float32(0.05) * np.arange(materials, dtype=np.float32)
    return [float(gamma) for gamma in gammas - np.float32(1.0)]


def early_kernel(
    frac_ref, density_ref, energy_ref, shift_ref, speed_ref, out_ref, sums_ref, rim_ref
):
    materials = frac_ref.shape[0]
    stiff = stiffness(materials)
    mass = pressure = None
    held = []
    for material in range(materials):
        part = frac_ref[material] * density_ref[material]
        force = part * energy_ref[material] * stiff[material]
        mass = part if mass is None else mass + part
        pressure = force if pressure is None else pressure + force
        held.append(part)
    sums_ref[0], sums_ref[1] = mass, pressure
    last = mass.shape[0] - 1
    for field in range(2):
        for at, ref in ((0, shift_ref), (4, speed_ref)):
            rim_ref[at + 2 * field : at + 2 * field + 2, :] = ref[field, 0:2, :]
            for copy in range(2):
                row = 16 + at + 2 * field + copy
                rim_ref[row : row + 1, :] = ref[field, last : last + 1, :]
    for field, value in enumerate((mass, pressure)):
        rim_ref[8 + field : 9 + field, :] = value[0:1]
        rim_ref[24 + field : 25 + field, :] = value[last : last + 1]
    store_pairs([frac_ref[material] for material in range(materials)] + held, out_ref, 0)


def columns_kernel(shift_ref, speed_ref, sums_ref, out_ref):
    height, width = shift_ref.shape[1:]
    lane = lax.broadcasted_iota(jnp.int32, (height, LANES), 1)
    wanted = jnp.zeros((height, LANES), jnp.float32)
    for field in range(6):
        ref = (shift_ref, speed_ref, sums_ref)[field // 2]
        first = ref[field % 2, :, :LANES]
        last = ref[field % 2, :, width - LANES :]
        row = 2 * field if field < 4 else 4 + field
        for column in range(2 if field < 4 else 1):
            moved = pltpu.roll(first, row, 1) if row else first
            wanted = jnp.where(lane == row + column, moved, wanted)
        wanted = jnp.where(lane == 16 + row, pltpu.roll(last, 17 + row, 1), wanted)
    wanted = jnp.concatenate([wanted, jnp.zeros((LANES - height, LANES), jnp.float32)], axis=0)
    out_ref[...] = wanted.T[0 : out_ref.shape[0]]


def corners_kernel(columns_ref, above_ref, below_ref, first_ref, last_ref):
    height, width = 64, above_ref.shape[1]
    shape = (16, LANES)
    lane = lax.broadcasted_iota(jnp.int32, shape, 1)
    row = lax.broadcasted_iota(jnp.int32, shape, 0)
    second = (row % 2 == 1) & (row < 8)

    def column(ref, base, at):
        return jnp.broadcast_to(ref[base : base + 16, at : at + 1], shape)

    def up(value):
        return pltpu.roll(value, 15, 0)

    def down(value):
        return pltpu.roll(value, 1, 0)

    left, right = column(above_ref, 0, 0), column(above_ref, 0, 1)
    value = columns_ref[0:16]
    value = jnp.where(lane == height, jnp.where(second, down(right), left), value)
    value = jnp.where(lane == height + 1, jnp.where(second, right, up(left)), value)
    under = jnp.where(second, column(below_ref, 16, 1), column(below_ref, 16, 0))
    first_ref[...] = jnp.where(lane == LANES - 1, under, value)
    end = column(above_ref, 0, width - 1)
    value = jnp.where(lane == height, end, columns_ref[16:32])
    value = jnp.where(lane == height + 1, up(end), value)
    last_ref[...] = jnp.where(lane == LANES - 1, column(below_ref, 16, width - 1), value)


def lagrange_kernel(
    now_shift_ref,
    now_speed_ref,
    sums_ref,
    above_ref,
    below_ref,
    right_ref,
    left_ref,
    frac_ref,
    density_ref,
    energy_ref,
    tables_ref,
    speed_ref,
    shift_ref,
    out_ref,
):
    height, width = sums_ref.shape[1:]
    shape = (height + SUB, width + LANES)
    lane = lax.broadcasted_iota(jnp.int32, shape, 1)
    line = lax.broadcasted_iota(jnp.int32, (shape[0], width), 0)
    sides = [pltpu.roll(ref[...], 1, 1) for ref in (right_ref, left_ref)]
    sides.append(jnp.zeros((LANES - 32, LANES), jnp.float32))
    sides = jnp.concatenate(sides, axis=0).T[0 : shape[0]]

    def extend(field):
        value = (now_shift_ref, now_speed_ref, sums_ref)[field // 2][field % 2]
        value = jnp.concatenate([value, jnp.zeros((SUB, width), jnp.float32)], axis=0)
        value = pltpu.roll(value, 1, 0)
        at = 2 * field if field < 4 else 4 + field
        value = jnp.where(line == 0, below_ref[16 + at : 17 + at, :], value)
        value = jnp.where(line == height + 1, above_ref[at : at + 1, :], value)
        if field < 4:
            value = jnp.where(line == height + 2, above_ref[at + 1 : at + 2, :], value)
        value = jnp.concatenate([value, jnp.zeros((shape[0], LANES), jnp.float32)], axis=1)
        value = pltpu.roll(value, 1, 1)
        value = jnp.where(lane == 0, sides[:, 16 + at : 17 + at], value)
        value = jnp.where(lane == width + 1, sides[:, at : at + 1], value)
        if field < 4:
            value = jnp.where(lane == width + 2, sides[:, at + 1 : at + 2], value)
        return value

    def next_row(value):
        return pltpu.roll(value, shape[0] - 1, 0)

    def next_column(value):
        return pltpu.roll(value, shape[1] - 1, 1)

    def before_row(value):
        return pltpu.roll(value, 1, 0)

    def before_column(value):
        return pltpu.roll(value, 1, 1)

    def diagonals(value):
        across = next_column(value)
        down = next_row(value)
        return next_row(across) - value, across - down

    def geometry(shift_x, shift_y):
        rise_x, cross_x = diagonals(shift_x)
        rise_y, cross_y = diagonals(shift_y)
        return 1.0 + rise_x, 1.0 + rise_y, -1.0 + cross_x, 1.0 + cross_y

    shift_x, shift_y, speed_x, speed_y, density, pressure = [extend(field) for field in range(6)]
    rise_x, rise_y, cross_x, cross_y = geometry(shift_x, shift_y)
    area = 0.5 * (rise_x * cross_y - cross_x * rise_y)
    up_x, over_x = diagonals(speed_x)
    up_y, over_y = diagonals(speed_y)
    rate = 0.5 * (up_x * cross_y + rise_x * over_y - over_x * rise_y - cross_x * up_y)
    squeeze = jnp.minimum(rate / area, 0.0)
    viscous = VISC_COEF * density * area * squeeze * squeeze
    half = 0.5 * (pressure + viscous)
    quarter = 0.25 * density * area

    def corners(one, two, sign):
        upper = before_row(two - before_column(one))
        return sign * (one - before_column(two) + upper)

    force_x = corners(-half * cross_y, half * rise_y, 1.0)
    force_y = corners(half * cross_x, -half * rise_x, 1.0)
    both = quarter + before_column(quarter)
    mass = both + before_row(both)
    speed_x = speed_x + TIME_STEP * (force_x / mass)
    speed_y = speed_y + TIME_STEP * (force_y / mass)
    shift_x = shift_x + TIME_STEP * speed_x
    shift_y = shift_y + TIME_STEP * speed_y
    rise_x, rise_y, cross_x, cross_y = geometry(shift_x, shift_y)
    after = 0.5 * (rise_x * cross_y - cross_x * rise_y)

    def own(value):
        return next_column(next_row(value))[0:height, 0:width]

    speed_ref[0], speed_ref[1] = own(speed_x), own(speed_y)
    shift_ref[0], shift_ref[1] = own(shift_x), own(shift_y)

    area, after, viscous = own(area), own(after), own(viscous)
    change = after - area
    materials = frac_ref.shape[0]
    values = []
    for material, stiff in enumerate(stiffness(materials)):
        frac, density, energy = frac_ref[material], density_ref[material], energy_ref[material]
        force = stiff * density * energy + viscous
        values.append(frac * density * area * energy - frac * force * change)
    store_pairs(values + [area, after], out_ref, 0)
    for piece in range(out_ref.shape[0]):
        out_ref[piece, (materials + 2) * QUAD : (materials + 2) * QUAD + SUB] = tables_ref[...]


def crossing_kernel(
    early_hbm,
    late_ref,
    out_ref,
    state_ref,
    even_ref,
    odd_ref,
    places_ref,
    sources_ref,
    weights_ref,
    sems,
):
    devices, rows = state_ref.shape[0], state_ref.shape[1]
    table_row = late_ref.shape[1] - SUB
    tiles = rows // SUB
    groups = devices // SUB
    capacity = LANES // SUB
    slots_ref = (even_ref, odd_ref)
    copies = []
    for i in range(WORKER_PARTS):
        part = pl.ds(devices // WORKER_PARTS * i, devices // WORKER_PARTS)
        target = state_ref.at[part, pl.ds(0, early_hbm.shape[1])]
        copies.append(pltpu.make_async_copy(early_hbm.at[part], target, sems.at[i]))
        copies[-1].start()
    spread = (SUB, LANES)
    lane = lax.broadcasted_iota(jnp.int32, spread, 1)
    source_of = lax.broadcasted_iota(jnp.int32, spread, 0)
    piece = lane // capacity
    odd = [(piece >> bit) & 1 == 1 for bit in range(3)]

    def take(values, index):
        return jnp.take_along_axis(values, index, axis=1, mode="promise_in_bounds")

    def regroup(values):
        for bit in range(3):
            values = [
                jnp.where(odd[bit], values[i | (1 << bit)], values[i & ~(1 << bit)])
                if not (i >> bit) & 1
                else jnp.where(odd[bit], values[i & ~(1 << bit)], values[i | (1 << bit)])
                for i in range(SUB)
            ]
        return values

    for a in range(groups):
        table = [late_ref[a * SUB : a * SUB + SUB, table_row + i, :] for i in range(7)]
        starts = table[6].astype(jnp.int32)
        for octet in range(groups):
            target = SUB * octet + (piece ^ source_of)
            at = take(starts, target) + lane % capacity
            valid = at < take(starts, target + 1)
            later, at = at >= LANES, at & (LANES - 1)
            source, weight, place = [
                jnp.where(later, take(table[2 * i + 1], at), take(table[2 * i], at)) for i in range(3)
            ]
            sources_ref[octet, a] = source
            weights_ref[octet, a] = jnp.where(valid, weight, 0.0)
            places = [jnp.broadcast_to(place[i : i + 1], spread) for i in range(SUB)]
            for delta, value in enumerate(regroup(places)):
                places_ref[SUB * octet + delta, a] = value

    low = lower_half(spread)
    third = rows // 3

    def conserve(source, carry):
        areas = late_ref[source, third : third + SUB]
        swapped = pltpu.roll(areas, QUAD, 0)
        area, after = jnp.where(low, areas, swapped), jnp.where(low, swapped, areas)
        for tile in range(tiles // 3):
            at = [slice(SUB * tile + third * g, SUB * tile + third * g + SUB) for g in range(3)]
            state_ref[source, at[0]] = state_ref[source, at[0]] * after
            state_ref[source, at[1]] = state_ref[source, at[1]] * area
            state_ref[source, at[2]] = late_ref[source, at[0]]
        return carry

    for copy in copies:
        copy.wait()
    lax.fori_loop(0, devices, conserve, 0, unroll=4)

    def gather(octet, a):
        sources, weights = sources_ref[octet, a].astype(jnp.int32), weights_ref[octet, a]
        index = [jnp.broadcast_to(sources[i : i + 1], spread) for i in range(SUB)]
        weight = [jnp.broadcast_to(weights[i : i + 1], spread) for i in range(SUB)]
        for first in range(0, tiles, tiles // 2):
            at = [slice(SUB * tile, SUB * tile + SUB) for tile in range(first, first + tiles // 2)]
            values = [
                [take(state_ref[a * SUB + i, rows_of], index[i]) * weight[i] for rows_of in at]
                for i in range(SUB)
            ]
            for tile, rows_of in enumerate(at):
                for delta, value in enumerate(regroup([value[tile] for value in values])):
                    slots_ref[octet % 2][delta, a, rows_of] = value

    block = lax.broadcasted_iota(jnp.int32, spread, 0).astype(jnp.float32)

    def scatter(octet, delta):
        target = SUB * octet + delta
        slots = slots_ref[octet % 2]
        value = jnp.concatenate([slots[delta, a] for a in range(groups)], axis=1)
        parts = jnp.concatenate(split3(value), axis=0)
        place = [places_ref[target, a] for a in range(groups)]
        hot = [
            [
                jnp.where(place[a] == block + float(SUB * tile), 1.0, 0.0)
                for tile in range(LANES // SUB)
            ]
            for a in range(groups)
        ]
        hot = jnp.concatenate([jnp.concatenate(column, axis=0) for column in hot], axis=1)
        total = lax.dot_general(
            parts,
            hot.astype(jnp.bfloat16),
            (((1,), (1,)), ((), ())),
            preferred_element_type=jnp.float32,
        )
        keep = jnp.broadcast_to(late_ref[target, table_row + 7 : table_row + 8], (rows, LANES))
        stay = keep * state_ref[target, 0:rows]
        out_ref[target] = stay + total[0:rows] + total[rows : 2 * rows] + total[2 * rows : 3 * rows]

    lax.fori_loop(0, groups, lambda a, carry: (gather(0, a), carry)[1], 0)
    for octet in range(groups):

        def step(a, carry):
            if octet + 1 < groups:
                gather(octet + 1, a)
            for i in range(SUB // groups):
                scatter(octet, SUB // groups * a + i)
            return carry

        lax.fori_loop(0, groups, step, 0, unroll=True)


WORKER_PARTS = 4
UNPACK_PARTS = 4


def unpack_kernel(sums_ref, out_ref, rows_ref, sems):
    low = lower_half((SUB, LANES))
    half = LANES // 2
    fields = out_ref.shape[0] // UNPACK_PARTS
    copies = []
    for pair in range(sums_ref.shape[1] // SUB):
        at = slice(SUB * pair, SUB * pair + SUB)
        first, second = [], []
        for octet in range(LANES // SUB):
            even, odd = pair_to_pieces(sums_ref[2 * octet, at], sums_ref[2 * octet + 1, at], low)
            first.append(even)
            second.append(odd)
        for field, tiles in ((2 * pair, first), (2 * pair + 1, second)):
            blocks = jnp.concatenate(tiles, axis=0).T
            rows_ref[field, :, :LANES] = blocks[:half]
            rows_ref[field, :, LANES:] = blocks[half:]
        if (2 * pair + 2) % fields == 0:
            part = pl.ds(2 * pair + 2 - fields, fields)
            sem = sems.at[len(copies)]
            copies.append(pltpu.make_async_copy(rows_ref.at[part], out_ref.at[part], sem))
            copies[-1].start()
    for copy in copies:
        copy.wait()


def unpack(sums, shape):
    return pl.pallas_call(
        unpack_kernel,
        out_shape=jax.ShapeDtypeStruct(shape, jnp.float32),
        in_specs=whole(1),
        out_specs=pl.BlockSpec(memory_space=pl.ANY),
        scratch_shapes=[pltpu.VMEM(shape, jnp.float32), pltpu.SemaphoreType.DMA((UNPACK_PARTS,))],
        name="unpack",
    )(near(sums))


def whole(count):
    return [pl.BlockSpec(memory_space=pltpu.VMEM)] * count


def near(value):
    return pltpu.with_memory_space_constraint(value, pltpu.VMEM)


def call(kernel, name, outs, inputs, scratch=(), near_ins=(), near_outs=(), far_ins=(), sems=()):
    inputs = [
        near(value) if i in near_ins else value for i, value in enumerate(inputs)
    ]
    shapes = [
        pltpu.VMEM(shape, jnp.float32) if i in near_outs else jax.ShapeDtypeStruct(shape, jnp.float32)
        for i, shape in enumerate(outs)
    ]
    return pl.pallas_call(
        kernel,
        out_shape=shapes if len(shapes) > 1 else shapes[0],
        in_specs=[
            pl.BlockSpec(memory_space=pl.ANY if i in far_ins else pltpu.VMEM)
            for i in range(len(inputs))
        ],
        out_specs=whole(len(shapes)) if len(shapes) > 1 else whole(1)[0],
        scratch_shapes=[pltpu.VMEM(shape, jnp.float32) for shape in scratch]
        + [pltpu.SemaphoreType.DMA((count,)) for count in sems],
        name=name,
    )(*inputs)


def exchange(value):
    return lax.all_to_all(value, ("zx", "zy"), 0, 0, tiled=True)


def local(*arguments):
    materials, rows_x, rows_y = arguments[0].shape
    devices = lax.axis_size("zx") * lax.axis_size("zy")
    entries, nblocks = arguments[6].shape[2], arguments[9].shape[2]
    fits = (rows_x, rows_y, nblocks) == (64, 256, LANES) and materials == 8
    if fits and devices == LANES // QUAD and entries == 2 * LANES:
        return local_by_zones(*arguments)
    return local_by_entries(*arguments)


def local_by_zones(
    frac, density, energy, node_shift, node_speed, dest_tile, src_block, dest_block, crossing, keep
):
    materials, rows_x, rows_y = frac.shape
    devices = lax.axis_size("zx") * lax.axis_size("zy")
    fields = 3 * materials
    rows = fields * QUAD
    plane = (2, rows_x, rows_y)
    early, sums, rim = call(
        early_kernel,
        "early",
        [(devices, 2 * materials * QUAD, LANES), plane, (32, rows_y)],
        (frac, density, energy, node_shift, node_speed),
        near_outs=(0, 1, 2),
    )
    early = exchange(early)
    above = shifted(rim, "zx", -1)
    below = above if lax.axis_size("zx") == 2 else shifted(rim, "zx", 1)
    columns = call(columns_kernel, "columns", [(32, LANES)], (node_shift, node_speed, sums), near_ins=(2,), near_outs=(0,))
    first, last = call(corners_kernel, "corners", [(16, LANES)] * 2, (columns, above, below), near_ins=(0, 1, 2), near_outs=(0, 1))
    right = shifted(first, "zy", -1)
    left = shifted(last, "zy", 1)
    tables = call(
        table_kernel,
        "tables",
        [(SUB, LANES)],
        (dest_tile.reshape(1, -1), src_block[0], dest_block[0], crossing[0], keep[0]),
        near_outs=(0,),
    )
    speed_after, shift_after, late = call(
        lagrange_kernel,
        "lagrange",
        [plane, plane, (devices, (materials + 2) * QUAD + SUB, LANES)],
        (node_shift, node_speed, sums, above, below, right, left, frac, density, energy, tables),
        near_ins=(2, 3, 4, 5, 6, 7, 8, 9, 10),
        near_outs=(2,),
    )
    early, late = lax.optimization_barrier((early, late))
    late = exchange(late)
    groups = devices // SUB
    totals = call(
        crossing_kernel,
        "crossings",
        [(devices, rows, LANES)],
        (early, late),
        scratch=[(devices, rows, LANES)]
        + [(SUB, groups, rows, LANES)] * 2
        + [(devices, groups, SUB, LANES)]
        + [(groups, groups, SUB, LANES)] * 2,
        near_ins=(1,),
        near_outs=(0,),
        far_ins=(0,),
        sems=(WORKER_PARTS,),
    )
    totals = exchange(totals)
    remapped = unpack(totals, (fields, rows_x, rows_y))
    return (remapped.reshape(3, materials, rows_x, rows_y), speed_after, shift_after)


def local_by_entries(
    frac, density, energy, node_shift, node_speed, dest_tile, src_block, dest_block, crossing, keep
):
    materials, rows_x, rows_y = frac.shape
    node_fields = jnp.concatenate([node_shift, node_speed], axis=0)
    extended = upper_rim(node_fields)
    area_now, mat_pressure, viscous, terms = zone_phase(
        frac, density, energy, slice_corners(extended[0:2]), slice_corners(extended[2:4])
    )
    term_one, term_two, term_three, term_four = terms
    gathered = (
        jnp.pad(term_one, ((0, 0), (0, 1), (0, 1)))
        + jnp.pad(term_two, ((0, 0), (1, 0), (0, 1)))
        + jnp.pad(term_three, ((0, 0), (1, 0), (1, 0)))
        + jnp.pad(term_four, ((0, 0), (0, 1), (1, 0)))
    )
    totals = spill_rim(gathered)
    speed_after, shift_after = node_update(totals, node_shift, node_speed)
    moved_rim = upper_rim(shift_after)
    area_after = zone_area(slice_corners(moved_rim))
    conserved = material_state(frac, density, energy, area_now, area_after, mat_pressure, viscous)
    nblocks = keep.shape[2]
    block_len = rows_x * rows_y // nblocks
    fields = 3 * materials
    blocks = conserved.reshape(fields, nblocks, block_len)
    size_x = lax.axis_size("zx")
    size_y = lax.axis_size("zy")
    devices = size_x * size_y
    targets = dest_tile[0, 0, :, 0]
    sources = src_block[0, 0]
    places = dest_block[0, 0]
    weights = crossing[0, 0]
    entry_count = targets.shape[0]
    capacity = max(2, 2 * entry_count // devices)
    member = (targets[:, None] == jnp.arange(devices, dtype=jnp.int32)[None, :]).astype(jnp.int32)
    before = jnp.cumsum(member, axis=0) - member
    slot_rank = jnp.sum(before * member, axis=1)
    slot_index = targets * capacity + slot_rank
    slot_total = devices * capacity
    matches = slot_index[:, None] == jnp.arange(slot_total, dtype=jnp.int32)[None, :]
    filled = jnp.any(matches, axis=0)
    owners = jnp.sum(
        jnp.where(matches, jnp.arange(entry_count, dtype=jnp.int32)[:, None], 0), axis=0
    )
    slot_weight = jnp.where(filled, weights[owners], 0.0)
    slot_place = jnp.where(filled, places[owners], nblocks)
    payload = blocks[:, sources[owners], :] * slot_weight[None, :, None]
    payload = payload.reshape(fields, size_x, size_y, capacity, block_len)
    place_ids = slot_place.reshape(1, size_x, size_y, capacity)
    arrived, arrived_ids = (
        lax.all_to_all(
            lax.all_to_all(payload, "zx", split_axis=1, concat_axis=1, tiled=True),
            "zy",
            split_axis=2,
            concat_axis=2,
            tiled=True,
        ),
        lax.all_to_all(
            lax.all_to_all(place_ids, "zx", split_axis=1, concat_axis=1, tiled=True),
            "zy",
            split_axis=2,
            concat_axis=2,
            tiled=True,
        ),
    )
    arrived = arrived.reshape(fields, slot_total, block_len)
    arrived_ids = arrived_ids.reshape(slot_total)
    landed = (
        jnp.zeros((fields, nblocks + 1, block_len), jnp.float32).at[:, arrived_ids, :].add(arrived)
    )
    result = blocks * keep[0, 0][None, :, None] + landed[:, :nblocks, :]
    remapped = result.reshape(3, materials, rows_x, rows_y)
    return (remapped, speed_after, shift_after)


def solution(mesh):
    in_specs = (
        P(None, "zx", "zy"),
        P(None, "zx", "zy"),
        P(None, "zx", "zy"),
        P(None, "zx", "zy"),
        P(None, "zx", "zy"),
        P("zx", "zy", None, None),
        P("zx", "zy", None),
        P("zx", "zy", None),
        P("zx", "zy", None),
        P("zx", "zy", None),
    )
    out_specs = (P(None, None, "zx", "zy"), P(None, "zx", "zy"), P(None, "zx", "zy"))
    return jax.shard_map(local, mesh=mesh, in_specs=in_specs, out_specs=out_specs, check_vma=False)
```

```python
import jax
import jax.numpy as jnp
import numpy as np
from jax import lax
from jax.experimental import pallas as pl
from jax.experimental.pallas import tpu as pltpu
from jax.sharding import PartitionSpec as P

TIME_STEP = 0.02
VISC_COEF = 0.25


def shifted(value, axis, by):
    peers = lax.axis_size(axis)
    return lax.ppermute(value, axis, [(i, (i + by) % peers) for i in range(peers)])


def corner_geometry(corners):
    corner_one, corner_two, corner_three, corner_four = corners
    rise_x = 1.0 + corner_three[0] - corner_one[0]
    rise_y = 1.0 + corner_three[1] - corner_one[1]
    cross_x = -1.0 + corner_four[0] - corner_two[0]
    cross_y = 1.0 + corner_four[1] - corner_two[1]
    return (rise_x, rise_y, cross_x, cross_y)


def zone_area(corners):
    rise_x, rise_y, cross_x, cross_y = corner_geometry(corners)
    return 0.5 * (rise_x * cross_y - cross_x * rise_y)


def zone_phase(frac, density, energy, shifts, speeds):
    rise_x, rise_y, cross_x, cross_y = corner_geometry(shifts)
    area_now = 0.5 * (rise_x * cross_y - cross_x * rise_y)
    speed_one, speed_two, speed_three, speed_four = speeds
    area_rate = 0.5 * (
        (speed_three[0] - speed_one[0]) * cross_y
        + rise_x * (speed_four[1] - speed_two[1])
        - (speed_four[0] - speed_two[0]) * rise_y
        - cross_x * (speed_three[1] - speed_one[1])
    )
    squeeze = jnp.minimum(area_rate / area_now, 0.0)
    gammas = (1.3 + 0.05 * jnp.arange(frac.shape[0], dtype=jnp.int32).astype(jnp.float32))[
        :, None, None
    ]
    mat_pressure = (gammas - 1.0) * density * energy
    zone_density = jnp.sum(frac * density, axis=0)
    viscous = VISC_COEF * zone_density * area_now * squeeze * squeeze
    total_pressure = jnp.sum(frac * mat_pressure, axis=0) + viscous
    half_press = 0.5 * total_pressure
    quarter_mass = 0.25 * zone_density * area_now
    term_one = jnp.stack([-half_press * cross_y, half_press * cross_x, quarter_mass])
    term_two = jnp.stack([half_press * rise_y, -half_press * rise_x, quarter_mass])
    term_three = jnp.stack([half_press * cross_y, -half_press * cross_x, quarter_mass])
    term_four = jnp.stack([-half_press * rise_y, half_press * rise_x, quarter_mass])
    return (area_now, mat_pressure, viscous, (term_one, term_two, term_three, term_four))


def node_update(totals, node_shift, node_speed):
    accel_xy = totals[0:2] / totals[2:3]
    speed_after = node_speed + TIME_STEP * accel_xy
    shift_after = node_shift + TIME_STEP * speed_after
    return (speed_after, shift_after)


def material_state(frac, density, energy, area_now, area_after, mat_pressure, viscous):
    energy_after = energy - (mat_pressure + viscous) * (area_after - area_now) / (
        density * area_now
    )
    volume = frac * area_after
    mass_now = frac * density * area_now
    return jnp.stack([volume, mass_now, mass_now * energy_after])


def upper_along_x(values):
    received = shifted(values[:, 0:1, :], "zx", -1)
    return jnp.concatenate([values, received], axis=1)


def upper_along_y(values):
    received = shifted(values[:, :, 0:1], "zy", -1)
    return jnp.concatenate([values, received], axis=2)


def upper_rim(values):
    return upper_along_y(upper_along_x(values))


def spill_along_x(values):
    received = shifted(values[:, -1:, :], "zx", 1)
    return jnp.concatenate([values[:, 0:1, :] + received, values[:, 1:-1, :]], axis=1)


def spill_along_y(values):
    received = shifted(values[:, :, -1:], "zy", 1)
    return jnp.concatenate([values[:, :, 0:1] + received, values[:, :, 1:-1]], axis=2)


def spill_rim(values):
    return spill_along_y(spill_along_x(values))


def slice_corners(extended):
    return (extended[:, :-1, :-1], extended[:, 1:, :-1], extended[:, 1:, 1:], extended[:, :-1, 1:])


SUB = 8
LANES = 128
QUAD = 4


def lower_half(shape):
    return lax.broadcasted_iota(jnp.int32, shape, len(shape) - 2) % SUB < QUAD


def zones_first(field):
    return jnp.concatenate([field[:, :LANES], field[:, LANES:]], axis=0).T


def pair_to_pieces(first, second, low):
    even = jnp.where(low, first, pltpu.roll(second, QUAD, 0))
    odd = jnp.where(low, pltpu.roll(first, QUAD, 0), second)
    return even, odd


def store_pairs(values, out_ref, row):
    low = lower_half((SUB, LANES))
    for pair in range(len(values) // 2):
        first, second = zones_first(values[2 * pair]), zones_first(values[2 * pair + 1])
        rows = slice(row + SUB * pair, row + SUB * pair + SUB)
        for octet in range(LANES // SUB):
            at = slice(SUB * octet, SUB * octet + SUB)
            even, odd = pair_to_pieces(first[at], second[at], low)
            out_ref[2 * octet, rows, :] = even
            out_ref[2 * octet + 1, rows, :] = odd


def split3(value):
    high = value.astype(jnp.bfloat16)
    left = value - high.astype(jnp.float32)
    middle = left.astype(jnp.bfloat16)
    low = (left - middle.astype(jnp.float32)).astype(jnp.bfloat16)
    return high, middle, low


def table_kernel(target_ref, source_ref, place_ref, weight_ref, keep_ref, out_ref):
    entries = target_ref.shape[1]
    row = target_ref[...].astype(jnp.float32)
    down = lax.broadcasted_iota(jnp.int32, (entries, entries), 0)
    across = lax.broadcasted_iota(jnp.int32, (entries, entries), 1)
    column = jnp.sum(jnp.where(down == across, row, 0.0), axis=1, keepdims=True)
    earlier = (row < column) | ((row == column) & (across < down))
    order = jnp.sum(jnp.where(earlier, 1.0, 0.0), axis=1, keepdims=True)
    hot = jnp.where(across.astype(jnp.float32) == order, 1.0, 0.0)
    source, place = source_ref[...], place_ref[...]
    half = LANES // 2
    source = ((source & 1) * half + (source >> 1)).astype(jnp.float32)
    place = ((place & 1) * half + (place >> 1)).astype(jnp.float32)
    parts = [part.astype(jnp.float32) for part in split3(weight_ref[...])] + [source, place]
    values = jnp.concatenate(parts + [jnp.zeros((SUB - len(parts), entries), jnp.float32)], axis=0)
    tables = jnp.dot(
        values.astype(jnp.bfloat16), hot.astype(jnp.bfloat16), preferred_element_type=jnp.float32
    )
    weights = tables[0:1] + tables[1:2] + tables[2:3]
    for table, value in enumerate((tables[3:4], weights, tables[4:5])):
        for side in range(2):
            at = slice(LANES * side, LANES * side + LANES)
            out_ref[2 * table + side : 2 * table + side + 1, :] = value[:, at]
    device = lax.broadcasted_iota(jnp.int32, (entries, LANES), 1).astype(jnp.float32)
    out_ref[6:7, :] = jnp.sum(jnp.where(column < device, 1.0, 0.0), axis=0, keepdims=True)
    lane = lax.broadcasted_iota(jnp.int32, (SUB, LANES), 1)
    keep = jnp.take_along_axis(
        jnp.broadcast_to(keep_ref[...], (SUB, LANES)),
        2 * (lane % half) + lane // half,
        axis=1,
        mode="promise_in_bounds",
    )
    out_ref[7:8, :] = keep[0:1]


def stiffness(materials):
    gammas = np.float32(1.3) + np.float32(0.05) * np.arange(materials, dtype=np.float32)
    return [float(gamma) for gamma in gammas - np.float32(1.0)]


def sums_kernel(frac_ref, density_ref, energy_ref, shift_ref, speed_ref, sums_ref, rim_ref):
    materials = frac_ref.shape[0]
    stiff = stiffness(materials)
    mass = pressure = None
    for material in range(materials):
        part = frac_ref[material] * density_ref[material]
        force = part * energy_ref[material] * stiff[material]
        mass = part if mass is None else mass + part
        pressure = force if pressure is None else pressure + force
    sums_ref[0], sums_ref[1] = mass, pressure
    last = mass.shape[0] - 1
    for field in range(2):
        for at, ref in ((0, shift_ref), (4, speed_ref)):
            rim_ref[at + 2 * field : at + 2 * field + 2, :] = ref[field, 0:2, :]
            for copy in range(2):
                row = 16 + at + 2 * field + copy
                rim_ref[row : row + 1, :] = ref[field, last : last + 1, :]
    for field, value in enumerate((mass, pressure)):
        rim_ref[8 + field : 9 + field, :] = value[0:1]
        rim_ref[24 + field : 25 + field, :] = value[last : last + 1]


def columns_kernel(shift_ref, speed_ref, sums_ref, out_ref):
    height, width = shift_ref.shape[1:]
    lane = lax.broadcasted_iota(jnp.int32, (height, LANES), 1)
    wanted = jnp.zeros((height, LANES), jnp.float32)
    for field in range(6):
        ref = (shift_ref, speed_ref, sums_ref)[field // 2]
        first = ref[field % 2, :, :LANES]
        last = ref[field % 2, :, width - LANES :]
        row = 2 * field if field < 4 else 4 + field
        for column in range(2 if field < 4 else 1):
            moved = pltpu.roll(first, row, 1) if row else first
            wanted = jnp.where(lane == row + column, moved, wanted)
        wanted = jnp.where(lane == 16 + row, pltpu.roll(last, 17 + row, 1), wanted)
    wanted = jnp.concatenate([wanted, jnp.zeros((LANES - height, LANES), jnp.float32)], axis=0)
    out_ref[...] = wanted.T[0 : out_ref.shape[0]]


def corners_kernel(columns_ref, above_ref, below_ref, first_ref, last_ref):
    height, width = 64, above_ref.shape[1]
    shape = (16, LANES)
    lane = lax.broadcasted_iota(jnp.int32, shape, 1)
    row = lax.broadcasted_iota(jnp.int32, shape, 0)
    second = (row % 2 == 1) & (row < 8)

    def column(ref, base, at):
        return jnp.broadcast_to(ref[base : base + 16, at : at + 1], shape)

    def up(value):
        return pltpu.roll(value, 15, 0)

    def down(value):
        return pltpu.roll(value, 1, 0)

    left, right = column(above_ref, 0, 0), column(above_ref, 0, 1)
    value = columns_ref[0:16]
    value = jnp.where(lane == height, jnp.where(second, down(right), left), value)
    value = jnp.where(lane == height + 1, jnp.where(second, right, up(left)), value)
    under = jnp.where(second, column(below_ref, 16, 1), column(below_ref, 16, 0))
    first_ref[...] = jnp.where(lane == LANES - 1, under, value)
    end = column(above_ref, 0, width - 1)
    value = jnp.where(lane == height, end, columns_ref[16:32])
    value = jnp.where(lane == height + 1, up(end), value)
    last_ref[...] = jnp.where(lane == LANES - 1, column(below_ref, 16, width - 1), value)


def lagrange_kernel(
    now_shift_ref,
    now_speed_ref,
    sums_ref,
    above_ref,
    below_ref,
    right_ref,
    left_ref,
    frac_ref,
    density_ref,
    energy_ref,
    tables_ref,
    speed_ref,
    shift_ref,
    out_ref,
):
    height, width = sums_ref.shape[1:]
    shape = (height + SUB, width + LANES)
    lane = lax.broadcasted_iota(jnp.int32, shape, 1)
    line = lax.broadcasted_iota(jnp.int32, (shape[0], width), 0)
    sides = [pltpu.roll(ref[...], 1, 1) for ref in (right_ref, left_ref)]
    sides.append(jnp.zeros((LANES - 32, LANES), jnp.float32))
    sides = jnp.concatenate(sides, axis=0).T[0 : shape[0]]

    def extend(field):
        value = (now_shift_ref, now_speed_ref, sums_ref)[field // 2][field % 2]
        value = jnp.concatenate([value, jnp.zeros((SUB, width), jnp.float32)], axis=0)
        value = pltpu.roll(value, 1, 0)
        at = 2 * field if field < 4 else 4 + field
        value = jnp.where(line == 0, below_ref[16 + at : 17 + at, :], value)
        value = jnp.where(line == height + 1, above_ref[at : at + 1, :], value)
        if field < 4:
            value = jnp.where(line == height + 2, above_ref[at + 1 : at + 2, :], value)
        value = jnp.concatenate([value, jnp.zeros((shape[0], LANES), jnp.float32)], axis=1)
        value = pltpu.roll(value, 1, 1)
        value = jnp.where(lane == 0, sides[:, 16 + at : 17 + at], value)
        value = jnp.where(lane == width + 1, sides[:, at : at + 1], value)
        if field < 4:
            value = jnp.where(lane == width + 2, sides[:, at + 1 : at + 2], value)
        return value

    def next_row(value):
        return pltpu.roll(value, shape[0] - 1, 0)

    def next_column(value):
        return pltpu.roll(value, shape[1] - 1, 1)

    def before_row(value):
        return pltpu.roll(value, 1, 0)

    def before_column(value):
        return pltpu.roll(value, 1, 1)

    def diagonals(value):
        across = next_column(value)
        down = next_row(value)
        return next_row(across) - value, across - down

    def geometry(shift_x, shift_y):
        rise_x, cross_x = diagonals(shift_x)
        rise_y, cross_y = diagonals(shift_y)
        return 1.0 + rise_x, 1.0 + rise_y, -1.0 + cross_x, 1.0 + cross_y

    shift_x, shift_y, speed_x, speed_y, density, pressure = [extend(field) for field in range(6)]
    rise_x, rise_y, cross_x, cross_y = geometry(shift_x, shift_y)
    area = 0.5 * (rise_x * cross_y - cross_x * rise_y)
    up_x, over_x = diagonals(speed_x)
    up_y, over_y = diagonals(speed_y)
    rate = 0.5 * (up_x * cross_y + rise_x * over_y - over_x * rise_y - cross_x * up_y)
    squeeze = jnp.minimum(rate / area, 0.0)
    viscous = VISC_COEF * density * area * squeeze * squeeze
    half = 0.5 * (pressure + viscous)
    quarter = 0.25 * density * area

    def corners(one, two, sign):
        upper = before_row(two - before_column(one))
        return sign * (one - before_column(two) + upper)

    force_x = corners(-half * cross_y, half * rise_y, 1.0)
    force_y = corners(half * cross_x, -half * rise_x, 1.0)
    both = quarter + before_column(quarter)
    mass = both + before_row(both)
    speed_x = speed_x + TIME_STEP * (force_x / mass)
    speed_y = speed_y + TIME_STEP * (force_y / mass)
    shift_x = shift_x + TIME_STEP * speed_x
    shift_y = shift_y + TIME_STEP * speed_y
    rise_x, rise_y, cross_x, cross_y = geometry(shift_x, shift_y)
    after = 0.5 * (rise_x * cross_y - cross_x * rise_y)

    def own(value):
        return next_column(next_row(value))[0:height, 0:width]

    speed_ref[0], speed_ref[1] = own(speed_x), own(speed_y)
    shift_ref[0], shift_ref[1] = own(shift_x), own(shift_y)

    area, after, viscous = own(area), own(after), own(viscous)
    change = after - area
    materials = frac_ref.shape[0]
    volumes, masses, energies = [], [], []
    for material, stiff in enumerate(stiffness(materials)):
        frac, density, energy = frac_ref[material], density_ref[material], energy_ref[material]
        force = stiff * density * energy + viscous
        volumes.append(frac * after)
        masses.append(frac * density * area)
        energies.append(masses[-1] * energy - frac * force * change)
    for third, values in enumerate((volumes, masses, energies)):
        store_pairs(values, out_ref, third * materials * QUAD)
    rows = 3 * materials * QUAD
    for piece in range(out_ref.shape[0]):
        out_ref[piece, rows : rows + SUB] = tables_ref[...]


def crossing_kernel(
    state_ref, out_ref, even_ref, odd_ref, places_ref, sources_ref, weights_ref
):
    devices, rows = out_ref.shape[0], out_ref.shape[1]
    tiles = rows // SUB
    groups = devices // SUB
    capacity = LANES // SUB
    slots_ref = (even_ref, odd_ref)
    spread = (SUB, LANES)
    lane = lax.broadcasted_iota(jnp.int32, spread, 1)
    source_of = lax.broadcasted_iota(jnp.int32, spread, 0)
    piece = lane // capacity
    odd = [(piece >> bit) & 1 == 1 for bit in range(3)]

    def take(values, index):
        return jnp.take_along_axis(values, index, axis=1, mode="promise_in_bounds")

    def regroup(values):
        for bit in range(3):
            values = [
                jnp.where(odd[bit], values[i | (1 << bit)], values[i & ~(1 << bit)])
                if not (i >> bit) & 1
                else jnp.where(odd[bit], values[i & ~(1 << bit)], values[i | (1 << bit)])
                for i in range(SUB)
            ]
        return values

    for a in range(groups):
        table = [state_ref[a * SUB : a * SUB + SUB, rows + i, :] for i in range(7)]
        starts = table[6].astype(jnp.int32)
        for octet in range(groups):
            target = SUB * octet + (piece ^ source_of)
            at = take(starts, target) + lane % capacity
            valid = at < take(starts, target + 1)
            later, at = at >= LANES, at & (LANES - 1)
            source, weight, place = [
                jnp.where(later, take(table[2 * i + 1], at), take(table[2 * i], at)) for i in range(3)
            ]
            sources_ref[octet, a] = source
            weights_ref[octet, a] = jnp.where(valid, weight, 0.0)
            places = [jnp.broadcast_to(place[i : i + 1], spread) for i in range(SUB)]
            for delta, value in enumerate(regroup(places)):
                places_ref[SUB * octet + delta, a] = value

    def gather(octet, a):
        sources, weights = sources_ref[octet, a].astype(jnp.int32), weights_ref[octet, a]
        index = [jnp.broadcast_to(sources[i : i + 1], spread) for i in range(SUB)]
        weight = [jnp.broadcast_to(weights[i : i + 1], spread) for i in range(SUB)]
        for first in range(0, tiles, tiles // 2):
            at = [slice(SUB * tile, SUB * tile + SUB) for tile in range(first, first + tiles // 2)]
            values = [
                [take(state_ref[a * SUB + i, rows_of], index[i]) * weight[i] for rows_of in at]
                for i in range(SUB)
            ]
            for tile, rows_of in enumerate(at):
                for delta, value in enumerate(regroup([value[tile] for value in values])):
                    slots_ref[octet % 2][delta, a, rows_of] = value

    block = lax.broadcasted_iota(jnp.int32, spread, 0).astype(jnp.float32)

    def scatter(octet, delta):
        target = SUB * octet + delta
        slots = slots_ref[octet % 2]
        value = jnp.concatenate([slots[delta, a] for a in range(groups)], axis=1)
        parts = jnp.concatenate(split3(value), axis=0)
        place = [places_ref[target, a] for a in range(groups)]
        hot = [
            [
                jnp.where(place[a] == block + float(SUB * tile), 1.0, 0.0)
                for tile in range(LANES // SUB)
            ]
            for a in range(groups)
        ]
        hot = jnp.concatenate([jnp.concatenate(column, axis=0) for column in hot], axis=1)
        total = lax.dot_general(
            parts,
            hot.astype(jnp.bfloat16),
            (((1,), (1,)), ((), ())),
            preferred_element_type=jnp.float32,
        )
        keep = jnp.broadcast_to(state_ref[target, rows + 7 : rows + 8], (rows, LANES))
        stay = keep * state_ref[target, 0:rows]
        out_ref[target] = stay + total[0:rows] + total[rows : 2 * rows] + total[2 * rows : 3 * rows]

    lax.fori_loop(0, groups, lambda a, carry: (gather(0, a), carry)[1], 0)
    for octet in range(groups):

        def step(a, carry):
            if octet + 1 < groups:
                gather(octet + 1, a)
            for i in range(SUB // groups):
                scatter(octet, SUB // groups * a + i)
            return carry

        lax.fori_loop(0, groups, step, 0, unroll=True)


UNPACK_PARTS = 4


def unpack_kernel(sums_ref, out_ref, rows_ref, sems):
    low = lower_half((SUB, LANES))
    half = LANES // 2
    fields = out_ref.shape[0] // UNPACK_PARTS
    copies = []
    for pair in range(sums_ref.shape[1] // SUB):
        at = slice(SUB * pair, SUB * pair + SUB)
        first, second = [], []
        for octet in range(LANES // SUB):
            even, odd = pair_to_pieces(sums_ref[2 * octet, at], sums_ref[2 * octet + 1, at], low)
            first.append(even)
            second.append(odd)
        for field, tiles in ((2 * pair, first), (2 * pair + 1, second)):
            blocks = jnp.concatenate(tiles, axis=0).T
            rows_ref[field, :, :LANES] = blocks[:half]
            rows_ref[field, :, LANES:] = blocks[half:]
        if (2 * pair + 2) % fields == 0:
            part = pl.ds(2 * pair + 2 - fields, fields)
            sem = sems.at[len(copies)]
            copies.append(pltpu.make_async_copy(rows_ref.at[part], out_ref.at[part], sem))
            copies[-1].start()
    for copy in copies:
        copy.wait()


def unpack(sums, shape):
    return pl.pallas_call(
        unpack_kernel,
        out_shape=jax.ShapeDtypeStruct(shape, jnp.float32),
        in_specs=whole(1),
        out_specs=pl.BlockSpec(memory_space=pl.ANY),
        scratch_shapes=[pltpu.VMEM(shape, jnp.float32), pltpu.SemaphoreType.DMA((UNPACK_PARTS,))],
        name="unpack",
    )(near(sums))


def whole(count):
    return [pl.BlockSpec(memory_space=pltpu.VMEM)] * count


def near(value):
    return pltpu.with_memory_space_constraint(value, pltpu.VMEM)


def call(kernel, name, outs, inputs, scratch=(), near_ins=(), near_outs=()):
    inputs = [
        near(value) if i in near_ins else value for i, value in enumerate(inputs)
    ]
    shapes = [
        pltpu.VMEM(shape, jnp.float32) if i in near_outs else jax.ShapeDtypeStruct(shape, jnp.float32)
        for i, shape in enumerate(outs)
    ]
    return pl.pallas_call(
        kernel,
        out_shape=shapes if len(shapes) > 1 else shapes[0],
        in_specs=whole(len(inputs)),
        out_specs=whole(len(shapes)) if len(shapes) > 1 else whole(1)[0],
        scratch_shapes=[pltpu.VMEM(shape, jnp.float32) for shape in scratch],
        name=name,
    )(*inputs)


def exchange(value):
    return lax.all_to_all(value, ("zx", "zy"), 0, 0, tiled=True)


def local(*arguments):
    materials, rows_x, rows_y = arguments[0].shape
    devices = lax.axis_size("zx") * lax.axis_size("zy")
    entries, nblocks = arguments[6].shape[2], arguments[9].shape[2]
    fits = (rows_x, rows_y, nblocks) == (64, 256, LANES) and materials == 8
    if fits and devices == LANES // QUAD and entries == 2 * LANES:
        return local_by_zones(*arguments)
    return local_by_entries(*arguments)


def local_by_zones(
    frac, density, energy, node_shift, node_speed, dest_tile, src_block, dest_block, crossing, keep
):
    materials, rows_x, rows_y = frac.shape
    devices = lax.axis_size("zx") * lax.axis_size("zy")
    fields = 3 * materials
    rows = fields * QUAD
    plane = (2, rows_x, rows_y)
    sums, rim = call(
        sums_kernel,
        "sums",
        [plane, (32, rows_y)],
        (frac, density, energy, node_shift, node_speed),
        near_outs=(0, 1),
    )
    above = shifted(rim, "zx", -1)
    below = above if lax.axis_size("zx") == 2 else shifted(rim, "zx", 1)
    columns = call(columns_kernel, "columns", [(32, LANES)], (node_shift, node_speed, sums), near_ins=(2,), near_outs=(0,))
    first, last = call(corners_kernel, "corners", [(16, LANES)] * 2, (columns, above, below), near_ins=(0, 1, 2), near_outs=(0, 1))
    right = shifted(first, "zy", -1)
    left = shifted(last, "zy", 1)
    tables = call(
        table_kernel,
        "tables",
        [(SUB, LANES)],
        (dest_tile.reshape(1, -1), src_block[0], dest_block[0], crossing[0], keep[0]),
        near_outs=(0,),
    )
    speed_after, shift_after, state = call(
        lagrange_kernel,
        "lagrange",
        [plane, plane, (devices, rows + SUB, LANES)],
        (
            node_shift, node_speed, sums, above, below, right, left, frac, density, energy, tables,
        ),
        near_ins=(2, 3, 4, 5, 6, 10),
        near_outs=(2,),
    )
    state = exchange(state)
    groups = devices // SUB
    totals = call(
        crossing_kernel,
        "crossings",
        [(devices, rows, LANES)],
        (state,),
        scratch=[(SUB, groups, rows, LANES)] * 2
        + [(devices, groups, SUB, LANES)]
        + [(groups, groups, SUB, LANES)] * 2,
        near_ins=(0,),
        near_outs=(0,),
    )
    totals = exchange(totals)
    remapped = unpack(totals, (fields, rows_x, rows_y))
    return (remapped.reshape(3, materials, rows_x, rows_y), speed_after, shift_after)


def local_by_entries(
    frac, density, energy, node_shift, node_speed, dest_tile, src_block, dest_block, crossing, keep
):
    materials, rows_x, rows_y = frac.shape
    node_fields = jnp.concatenate([node_shift, node_speed], axis=0)
    extended = upper_rim(node_fields)
    area_now, mat_pressure, viscous, terms = zone_phase(
        frac, density, energy, slice_corners(extended[0:2]), slice_corners(extended[2:4])
    )
    term_one, term_two, term_three, term_four = terms
    gathered = (
        jnp.pad(term_one, ((0, 0), (0, 1), (0, 1)))
        + jnp.pad(term_two, ((0, 0), (1, 0), (0, 1)))
        + jnp.pad(term_three, ((0, 0), (1, 0), (1, 0)))
        + jnp.pad(term_four, ((0, 0), (0, 1), (1, 0)))
    )
    totals = spill_rim(gathered)
    speed_after, shift_after = node_update(totals, node_shift, node_speed)
    moved_rim = upper_rim(shift_after)
    area_after = zone_area(slice_corners(moved_rim))
    conserved = material_state(frac, density, energy, area_now, area_after, mat_pressure, viscous)
    nblocks = keep.shape[2]
    block_len = rows_x * rows_y // nblocks
    fields = 3 * materials
    blocks = conserved.reshape(fields, nblocks, block_len)
    size_x = lax.axis_size("zx")
    size_y = lax.axis_size("zy")
    devices = size_x * size_y
    targets = dest_tile[0, 0, :, 0]
    sources = src_block[0, 0]
    places = dest_block[0, 0]
    weights = crossing[0, 0]
    entry_count = targets.shape[0]
    capacity = max(2, 2 * entry_count // devices)
    member = (targets[:, None] == jnp.arange(devices, dtype=jnp.int32)[None, :]).astype(jnp.int32)
    before = jnp.cumsum(member, axis=0) - member
    slot_rank = jnp.sum(before * member, axis=1)
    slot_index = targets * capacity + slot_rank
    slot_total = devices * capacity
    matches = slot_index[:, None] == jnp.arange(slot_total, dtype=jnp.int32)[None, :]
    filled = jnp.any(matches, axis=0)
    owners = jnp.sum(
        jnp.where(matches, jnp.arange(entry_count, dtype=jnp.int32)[:, None], 0), axis=0
    )
    slot_weight = jnp.where(filled, weights[owners], 0.0)
    slot_place = jnp.where(filled, places[owners], nblocks)
    payload = blocks[:, sources[owners], :] * slot_weight[None, :, None]
    payload = payload.reshape(fields, size_x, size_y, capacity, block_len)
    place_ids = slot_place.reshape(1, size_x, size_y, capacity)
    arrived, arrived_ids = (
        lax.all_to_all(
            lax.all_to_all(payload, "zx", split_axis=1, concat_axis=1, tiled=True),
            "zy",
            split_axis=2,
            concat_axis=2,
            tiled=True,
        ),
        lax.all_to_all(
            lax.all_to_all(place_ids, "zx", split_axis=1, concat_axis=1, tiled=True),
            "zy",
            split_axis=2,
            concat_axis=2,
            tiled=True,
        ),
    )
    arrived = arrived.reshape(fields, slot_total, block_len)
    arrived_ids = arrived_ids.reshape(slot_total)
    landed = (
        jnp.zeros((fields, nblocks + 1, block_len), jnp.float32).at[:, arrived_ids, :].add(arrived)
    )
    result = blocks * keep[0, 0][None, :, None] + landed[:, :nblocks, :]
    remapped = result.reshape(3, materials, rows_x, rows_y)
    return (remapped, speed_after, shift_after)


def solution(mesh):
    in_specs = (
        P(None, "zx", "zy"),
        P(None, "zx", "zy"),
        P(None, "zx", "zy"),
        P(None, "zx", "zy"),
        P(None, "zx", "zy"),
        P("zx", "zy", None, None),
        P("zx", "zy", None),
        P("zx", "zy", None),
        P("zx", "zy", None),
        P("zx", "zy", None),
    )
    out_specs = (P(None, None, "zx", "zy"), P(None, "zx", "zy"), P(None, "zx", "zy"))
    return jax.shard_map(local, mesh=mesh, in_specs=in_specs, out_specs=out_specs, check_vma=False)
```

```python
import jax
import jax.numpy as jnp
import numpy as np
from jax import lax
from jax.experimental import pallas as pl
from jax.experimental.pallas import tpu as pltpu
from jax.sharding import PartitionSpec as P

TIME_STEP = 0.02
VISC_COEF = 0.25


def shifted(value, axis, by):
    peers = lax.axis_size(axis)
    return lax.ppermute(value, axis, [(i, (i + by) % peers) for i in range(peers)])


def corner_geometry(corners):
    corner_one, corner_two, corner_three, corner_four = corners
    rise_x = 1.0 + corner_three[0] - corner_one[0]
    rise_y = 1.0 + corner_three[1] - corner_one[1]
    cross_x = -1.0 + corner_four[0] - corner_two[0]
    cross_y = 1.0 + corner_four[1] - corner_two[1]
    return (rise_x, rise_y, cross_x, cross_y)


def zone_area(corners):
    rise_x, rise_y, cross_x, cross_y = corner_geometry(corners)
    return 0.5 * (rise_x * cross_y - cross_x * rise_y)


def zone_phase(frac, density, energy, shifts, speeds):
    rise_x, rise_y, cross_x, cross_y = corner_geometry(shifts)
    area_now = 0.5 * (rise_x * cross_y - cross_x * rise_y)
    speed_one, speed_two, speed_three, speed_four = speeds
    area_rate = 0.5 * (
        (speed_three[0] - speed_one[0]) * cross_y
        + rise_x * (speed_four[1] - speed_two[1])
        - (speed_four[0] - speed_two[0]) * rise_y
        - cross_x * (speed_three[1] - speed_one[1])
    )
    squeeze = jnp.minimum(area_rate / area_now, 0.0)
    gammas = (1.3 + 0.05 * jnp.arange(frac.shape[0], dtype=jnp.int32).astype(jnp.float32))[
        :, None, None
    ]
    mat_pressure = (gammas - 1.0) * density * energy
    zone_density = jnp.sum(frac * density, axis=0)
    viscous = VISC_COEF * zone_density * area_now * squeeze * squeeze
    total_pressure = jnp.sum(frac * mat_pressure, axis=0) + viscous
    half_press = 0.5 * total_pressure
    quarter_mass = 0.25 * zone_density * area_now
    term_one = jnp.stack([-half_press * cross_y, half_press * cross_x, quarter_mass])
    term_two = jnp.stack([half_press * rise_y, -half_press * rise_x, quarter_mass])
    term_three = jnp.stack([half_press * cross_y, -half_press * cross_x, quarter_mass])
    term_four = jnp.stack([-half_press * rise_y, half_press * rise_x, quarter_mass])
    return (area_now, mat_pressure, viscous, (term_one, term_two, term_three, term_four))


def node_update(totals, node_shift, node_speed):
    accel_xy = totals[0:2] / totals[2:3]
    speed_after = node_speed + TIME_STEP * accel_xy
    shift_after = node_shift + TIME_STEP * speed_after
    return (speed_after, shift_after)


def material_state(frac, density, energy, area_now, area_after, mat_pressure, viscous):
    energy_after = energy - (mat_pressure + viscous) * (area_after - area_now) / (
        density * area_now
    )
    volume = frac * area_after
    mass_now = frac * density * area_now
    return jnp.stack([volume, mass_now, mass_now * energy_after])


def upper_along_x(values):
    received = shifted(values[:, 0:1, :], "zx", -1)
    return jnp.concatenate([values, received], axis=1)


def upper_along_y(values):
    received = shifted(values[:, :, 0:1], "zy", -1)
    return jnp.concatenate([values, received], axis=2)


def upper_rim(values):
    return upper_along_y(upper_along_x(values))


def spill_along_x(values):
    received = shifted(values[:, -1:, :], "zx", 1)
    return jnp.concatenate([values[:, 0:1, :] + received, values[:, 1:-1, :]], axis=1)


def spill_along_y(values):
    received = shifted(values[:, :, -1:], "zy", 1)
    return jnp.concatenate([values[:, :, 0:1] + received, values[:, :, 1:-1]], axis=2)


def spill_rim(values):
    return spill_along_y(spill_along_x(values))


def slice_corners(extended):
    return (extended[:, :-1, :-1], extended[:, 1:, :-1], extended[:, 1:, 1:], extended[:, :-1, 1:])


SUB = 8
LANES = 128
QUAD = 4


def lower_half(shape):
    return lax.broadcasted_iota(jnp.int32, shape, len(shape) - 2) % SUB < QUAD


def zones_first(field):
    return jnp.concatenate([field[:, :LANES], field[:, LANES:]], axis=0).T


def pair_to_pieces(first, second, low):
    even = jnp.where(low, first, pltpu.roll(second, QUAD, 0))
    odd = jnp.where(low, pltpu.roll(first, QUAD, 0), second)
    return even, odd


def store_pairs(values, out_ref, row):
    low = lower_half((SUB, LANES))
    for pair in range(len(values) // 2):
        first, second = zones_first(values[2 * pair]), zones_first(values[2 * pair + 1])
        rows = slice(row + SUB * pair, row + SUB * pair + SUB)
        for octet in range(LANES // SUB):
            at = slice(SUB * octet, SUB * octet + SUB)
            even, odd = pair_to_pieces(first[at], second[at], low)
            out_ref[2 * octet, rows, :] = even
            out_ref[2 * octet + 1, rows, :] = odd


def split3(value):
    high = value.astype(jnp.bfloat16)
    left = value - high.astype(jnp.float32)
    middle = left.astype(jnp.bfloat16)
    low = (left - middle.astype(jnp.float32)).astype(jnp.bfloat16)
    return high, middle, low


def table_kernel(target_ref, source_ref, place_ref, weight_ref, keep_ref, out_ref):
    entries = target_ref.shape[1]
    row = target_ref[...].astype(jnp.float32)
    down = lax.broadcasted_iota(jnp.int32, (entries, entries), 0)
    across = lax.broadcasted_iota(jnp.int32, (entries, entries), 1)
    column = jnp.sum(jnp.where(down == across, row, 0.0), axis=1, keepdims=True)
    earlier = (row < column) | ((row == column) & (across < down))
    order = jnp.sum(jnp.where(earlier, 1.0, 0.0), axis=1, keepdims=True)
    hot = jnp.where(across.astype(jnp.float32) == order, 1.0, 0.0)
    source, place = source_ref[...], place_ref[...]
    half = LANES // 2
    source = ((source & 1) * half + (source >> 1)).astype(jnp.float32)
    place = ((place & 1) * half + (place >> 1)).astype(jnp.float32)
    parts = [part.astype(jnp.float32) for part in split3(weight_ref[...])] + [source, place]
    values = jnp.concatenate(parts + [jnp.zeros((SUB - len(parts), entries), jnp.float32)], axis=0)
    tables = jnp.dot(
        values.astype(jnp.bfloat16), hot.astype(jnp.bfloat16), preferred_element_type=jnp.float32
    )
    weights = tables[0:1] + tables[1:2] + tables[2:3]
    for table, value in enumerate((tables[3:4], weights, tables[4:5])):
        for side in range(2):
            at = slice(LANES * side, LANES * side + LANES)
            out_ref[2 * table + side : 2 * table + side + 1, :] = value[:, at]
    device = lax.broadcasted_iota(jnp.int32, (entries, LANES), 1).astype(jnp.float32)
    out_ref[6:7, :] = jnp.sum(jnp.where(column < device, 1.0, 0.0), axis=0, keepdims=True)
    lane = lax.broadcasted_iota(jnp.int32, (SUB, LANES), 1)
    keep = jnp.take_along_axis(
        jnp.broadcast_to(keep_ref[...], (SUB, LANES)),
        2 * (lane % half) + lane // half,
        axis=1,
        mode="promise_in_bounds",
    )
    out_ref[7:8, :] = keep[0:1]


def stiffness(materials):
    gammas = np.float32(1.3) + np.float32(0.05) * np.arange(materials, dtype=np.float32)
    return [float(gamma) for gamma in gammas - np.float32(1.0)]


def sums_kernel(
    frac_ref, density_ref, energy_ref, shift_ref, speed_ref, sums_ref, rim_ref, first_ref, last_ref
):
    materials = frac_ref.shape[0]
    stiff = stiffness(materials)
    mass = pressure = None
    for material in range(materials):
        part = frac_ref[material] * density_ref[material]
        force = part * energy_ref[material] * stiff[material]
        mass = part if mass is None else mass + part
        pressure = force if pressure is None else pressure + force
    sums_ref[0], sums_ref[1] = mass, pressure
    last = mass.shape[0] - 1
    for field in range(2):
        for at, ref in ((0, shift_ref), (4, speed_ref)):
            rim_ref[at + 2 * field : at + 2 * field + 2, :] = ref[field, 0:2, :]
            for copy in range(2):
                row = 16 + at + 2 * field + copy
                rim_ref[row : row + 1, :] = ref[field, last : last + 1, :]
    for field, value in enumerate((mass, pressure)):
        rim_ref[8 + field : 9 + field, :] = value[0:1]
        rim_ref[24 + field : 25 + field, :] = value[last : last + 1]
    height, width = mass.shape
    lane = lax.broadcasted_iota(jnp.int32, (height, LANES), 1)
    wanted = jnp.zeros((height, LANES), jnp.float32)
    values = [shift_ref[0], shift_ref[1], speed_ref[0], speed_ref[1], mass, pressure]
    for field, value in enumerate(values):
        row = 2 * field if field < 4 else 4 + field
        moved = value[:, :LANES]
        moved = pltpu.roll(moved, row, 1) if row else moved
        ends = (lane == row) | (lane == row + 1) if field < 4 else lane == row
        wanted = jnp.where(ends, moved, wanted)
        moved = pltpu.roll(value[:, width - LANES :], 17 + row, 1)
        wanted = jnp.where(lane == 16 + row, moved, wanted)
    wanted = jnp.concatenate([wanted, jnp.zeros((LANES - height, LANES), jnp.float32)], axis=0).T
    first_ref[...], last_ref[...] = wanted[0:16], wanted[16:32]


def lagrange_kernel(
    now_shift_ref,
    now_speed_ref,
    sums_ref,
    left_above_ref,
    left_below_ref,
    left_ref,
    right_ref,
    right_above_ref,
    right_below_ref,
    above_ref,
    below_ref,
    frac_ref,
    density_ref,
    energy_ref,
    tables_ref,
    speed_ref,
    shift_ref,
    out_ref,
):
    height, width = sums_ref.shape[1:]
    shape = (height + SUB, width + LANES)
    lane = lax.broadcasted_iota(jnp.int32, shape, 1)
    line = lax.broadcasted_iota(jnp.int32, (shape[0], width), 0)
    side_lane = lax.broadcasted_iota(jnp.int32, (16, LANES), 1)
    sides = []
    for ref, above, below in (
        (right_ref, right_above_ref, right_below_ref),
        (left_ref, left_above_ref, left_below_ref),
    ):
        beyond = jnp.where(
            side_lane < LANES - 1, pltpu.roll(above[...], height, 1), pltpu.roll(below[...], height, 1)
        )
        sides.append(pltpu.roll(jnp.where(side_lane < height, ref[...], beyond), 1, 1))
    sides.append(jnp.zeros((LANES - 32, LANES), jnp.float32))
    sides = jnp.concatenate(sides, axis=0).T[0 : shape[0]]

    def extend(field):
        value = (now_shift_ref, now_speed_ref, sums_ref)[field // 2][field % 2]
        value = jnp.concatenate([value, jnp.zeros((SUB, width), jnp.float32)], axis=0)
        value = pltpu.roll(value, 1, 0)
        at = 2 * field if field < 4 else 4 + field
        value = jnp.where(line == 0, below_ref[16 + at : 17 + at, :], value)
        value = jnp.where(line == height + 1, above_ref[at : at + 1, :], value)
        if field < 4:
            value = jnp.where(line == height + 2, above_ref[at + 1 : at + 2, :], value)
        value = jnp.concatenate([value, jnp.zeros((shape[0], LANES), jnp.float32)], axis=1)
        value = pltpu.roll(value, 1, 1)
        value = jnp.where(lane == 0, sides[:, 16 + at : 17 + at], value)
        value = jnp.where(lane == width + 1, sides[:, at : at + 1], value)
        if field < 4:
            value = jnp.where(lane == width + 2, sides[:, at + 1 : at + 2], value)
        return value

    def next_row(value):
        return pltpu.roll(value, shape[0] - 1, 0)

    def next_column(value):
        return pltpu.roll(value, shape[1] - 1, 1)

    def before_row(value):
        return pltpu.roll(value, 1, 0)

    def before_column(value):
        return pltpu.roll(value, 1, 1)

    def diagonals(value):
        across = next_column(value)
        down = next_row(value)
        return next_row(across) - value, across - down

    def geometry(shift_x, shift_y):
        rise_x, cross_x = diagonals(shift_x)
        rise_y, cross_y = diagonals(shift_y)
        return 1.0 + rise_x, 1.0 + rise_y, -1.0 + cross_x, 1.0 + cross_y

    shift_x, shift_y, speed_x, speed_y, density, pressure = [extend(field) for field in range(6)]
    rise_x, rise_y, cross_x, cross_y = geometry(shift_x, shift_y)
    area = 0.5 * (rise_x * cross_y - cross_x * rise_y)
    up_x, over_x = diagonals(speed_x)
    up_y, over_y = diagonals(speed_y)
    rate = 0.5 * (up_x * cross_y + rise_x * over_y - over_x * rise_y - cross_x * up_y)
    squeeze = jnp.minimum(rate / area, 0.0)
    viscous = VISC_COEF * density * area * squeeze * squeeze
    half = 0.5 * (pressure + viscous)
    quarter = 0.25 * density * area

    def corners(one, two, sign):
        upper = before_row(two - before_column(one))
        return sign * (one - before_column(two) + upper)

    force_x = corners(-half * cross_y, half * rise_y, 1.0)
    force_y = corners(half * cross_x, -half * rise_x, 1.0)
    both = quarter + before_column(quarter)
    mass = both + before_row(both)
    speed_x = speed_x + TIME_STEP * (force_x / mass)
    speed_y = speed_y + TIME_STEP * (force_y / mass)
    shift_x = shift_x + TIME_STEP * speed_x
    shift_y = shift_y + TIME_STEP * speed_y
    rise_x, rise_y, cross_x, cross_y = geometry(shift_x, shift_y)
    after = 0.5 * (rise_x * cross_y - cross_x * rise_y)

    def own(value):
        return next_column(next_row(value))[0:height, 0:width]

    speed_ref[0], speed_ref[1] = own(speed_x), own(speed_y)
    shift_ref[0], shift_ref[1] = own(shift_x), own(shift_y)

    area, after, viscous = own(area), own(after), own(viscous)
    change = after - area
    materials = frac_ref.shape[0]
    volumes, masses, energies = [], [], []
    for material, stiff in enumerate(stiffness(materials)):
        frac, density, energy = frac_ref[material], density_ref[material], energy_ref[material]
        force = stiff * density * energy + viscous
        volumes.append(frac * after)
        masses.append(frac * density * area)
        energies.append(masses[-1] * energy - frac * force * change)
    for third, values in enumerate((volumes, masses, energies)):
        store_pairs(values, out_ref, third * materials * QUAD)
    rows = 3 * materials * QUAD
    for piece in range(out_ref.shape[0]):
        out_ref[piece, rows : rows + SUB] = tables_ref[...]


def crossing_kernel(
    state_ref, out_ref, even_ref, odd_ref, places_ref, sources_ref, weights_ref
):
    devices, rows = out_ref.shape[0], out_ref.shape[1]
    tiles = rows // SUB
    groups = devices // SUB
    capacity = LANES // SUB
    slots_ref = (even_ref, odd_ref)
    spread = (SUB, LANES)
    lane = lax.broadcasted_iota(jnp.int32, spread, 1)
    source_of = lax.broadcasted_iota(jnp.int32, spread, 0)
    piece = lane // capacity
    odd = [(piece >> bit) & 1 == 1 for bit in range(3)]

    def take(values, index):
        return jnp.take_along_axis(values, index, axis=1, mode="promise_in_bounds")

    def regroup(values):
        for bit in range(3):
            values = [
                jnp.where(odd[bit], values[i | (1 << bit)], values[i & ~(1 << bit)])
                if not (i >> bit) & 1
                else jnp.where(odd[bit], values[i & ~(1 << bit)], values[i | (1 << bit)])
                for i in range(SUB)
            ]
        return values

    for a in range(groups):
        table = [state_ref[a * SUB : a * SUB + SUB, rows + i, :] for i in range(7)]
        starts = table[6].astype(jnp.int32)
        for octet in range(groups):
            target = SUB * octet + (piece ^ source_of)
            at = take(starts, target) + lane % capacity
            valid = at < take(starts, target + 1)
            later, at = at >= LANES, at & (LANES - 1)
            source, weight, place = [
                jnp.where(later, take(table[2 * i + 1], at), take(table[2 * i], at)) for i in range(3)
            ]
            sources_ref[octet, a] = source
            weights_ref[octet, a] = jnp.where(valid, weight, 0.0)
            places = [jnp.broadcast_to(place[i : i + 1], spread) for i in range(SUB)]
            for delta, value in enumerate(regroup(places)):
                twice = jnp.concatenate([value, value], axis=0)
                places_ref[SUB * octet + delta, a] = twice.astype(jnp.bfloat16)

    def gather(octet, a):
        sources, weights = sources_ref[octet, a].astype(jnp.int32), weights_ref[octet, a]
        index = [jnp.broadcast_to(sources[i : i + 1], spread) for i in range(SUB)]
        weight = [jnp.broadcast_to(weights[i : i + 1], spread) for i in range(SUB)]
        at = [slice(SUB * tile, SUB * tile + SUB) for tile in range(tiles)]
        values = [
            [take(state_ref[a * SUB + i, rows_of], index[i]) * weight[i] for rows_of in at]
            for i in range(SUB)
        ]
        for tile, rows_of in enumerate(at):
            for delta, value in enumerate(regroup([value[tile] for value in values])):
                slots_ref[octet % 2][delta, a, rows_of] = value

    packed = (2 * SUB, LANES)
    block = lax.broadcasted_iota(jnp.int32, packed, 0).astype(jnp.float32).astype(jnp.bfloat16)
    one, zero = jnp.ones(packed, jnp.bfloat16), jnp.zeros(packed, jnp.bfloat16)

    def scatter(octet, delta):
        target = SUB * octet + delta
        slots = slots_ref[octet % 2]
        value = jnp.concatenate([slots[delta, a] for a in range(groups)], axis=1)
        parts = jnp.concatenate(split3(value), axis=0)
        place = [places_ref[target, a] for a in range(groups)]
        hot = [
            [
                jnp.where(place[a] == block + jnp.bfloat16(2 * SUB * tile), one, zero)
                for tile in range(LANES // SUB // 2)
            ]
            for a in range(groups)
        ]
        hot = jnp.concatenate([jnp.concatenate(column, axis=0) for column in hot], axis=1)
        total = lax.dot_general(
            parts,
            hot,
            (((1,), (1,)), ((), ())),
            preferred_element_type=jnp.float32,
        )
        keep = jnp.broadcast_to(state_ref[target, rows + 7 : rows + 8], (rows, LANES))
        stay = keep * state_ref[target, 0:rows]
        out_ref[target] = stay + total[0:rows] + total[rows : 2 * rows] + total[2 * rows : 3 * rows]

    lax.fori_loop(0, groups, lambda a, carry: (gather(0, a), carry)[1], 0)
    for octet in range(groups):

        def step(a, carry):
            if octet + 1 < groups:
                gather(octet + 1, a)
            for i in range(SUB // groups):
                scatter(octet, SUB // groups * a + i)
            return carry

        lax.fori_loop(0, groups, step, 0, unroll=True)


UNPACK_PARTS = 4


def unpack_kernel(sums_ref, out_ref, rows_ref, sems):
    low = lower_half((SUB, LANES))
    half = LANES // 2
    fields = out_ref.shape[0] // UNPACK_PARTS
    copies = []
    for pair in range(sums_ref.shape[1] // SUB):
        at = slice(SUB * pair, SUB * pair + SUB)
        first, second = [], []
        for octet in range(LANES // SUB):
            even, odd = pair_to_pieces(sums_ref[2 * octet, at], sums_ref[2 * octet + 1, at], low)
            first.append(even)
            second.append(odd)
        for field, tiles in ((2 * pair, first), (2 * pair + 1, second)):
            blocks = jnp.concatenate(tiles, axis=0).T
            rows_ref[field, :, :LANES] = blocks[:half]
            rows_ref[field, :, LANES:] = blocks[half:]
        if (2 * pair + 2) % fields == 0:
            part = pl.ds(2 * pair + 2 - fields, fields)
            sem = sems.at[len(copies)]
            copies.append(pltpu.make_async_copy(rows_ref.at[part], out_ref.at[part], sem))
            copies[-1].start()
    for copy in copies:
        copy.wait()


def unpack(sums, shape):
    return pl.pallas_call(
        unpack_kernel,
        out_shape=jax.ShapeDtypeStruct(shape, jnp.float32),
        in_specs=whole(1),
        out_specs=pl.BlockSpec(memory_space=pl.ANY),
        scratch_shapes=[pltpu.VMEM(shape, jnp.float32), pltpu.SemaphoreType.DMA((UNPACK_PARTS,))],
        name="unpack",
    )(near(sums))


def whole(count):
    return [pl.BlockSpec(memory_space=pltpu.VMEM)] * count


def near(value):
    return pltpu.with_memory_space_constraint(value, pltpu.VMEM)


def call(kernel, name, outs, inputs, scratch=(), near_ins=(), near_outs=()):
    inputs = [
        near(value) if i in near_ins else value for i, value in enumerate(inputs)
    ]
    shapes = [
        pltpu.VMEM(shape, jnp.float32) if i in near_outs else jax.ShapeDtypeStruct(shape, jnp.float32)
        for i, shape in enumerate(outs)
    ]
    return pl.pallas_call(
        kernel,
        out_shape=shapes if len(shapes) > 1 else shapes[0],
        in_specs=whole(len(inputs)),
        out_specs=whole(len(shapes)) if len(shapes) > 1 else whole(1)[0],
        scratch_shapes=scratch,
        name=name,
    )(*inputs)


def exchange(value):
    return lax.all_to_all(value, ("zx", "zy"), 0, 0, tiled=True)


def diagonal(value, by_x, by_y):
    size_x, size_y = lax.axis_size("zx"), lax.axis_size("zy")
    route = [
        (a * size_y + b, (a + by_x) % size_x * size_y + (b + by_y) % size_y)
        for a in range(size_x)
        for b in range(size_y)
    ]
    return lax.ppermute(value, ("zx", "zy"), route)


def local(*arguments):
    materials, rows_x, rows_y = arguments[0].shape
    devices = lax.axis_size("zx") * lax.axis_size("zy")
    entries, nblocks = arguments[6].shape[2], arguments[9].shape[2]
    fits = (rows_x, rows_y, nblocks) == (64, 256, LANES) and materials == 8
    if fits and devices == LANES // QUAD and entries == 2 * LANES:
        return local_by_zones(*arguments)
    return local_by_entries(*arguments)


def local_by_zones(
    frac, density, energy, node_shift, node_speed, dest_tile, src_block, dest_block, crossing, keep
):
    materials, rows_x, rows_y = frac.shape
    devices = lax.axis_size("zx") * lax.axis_size("zy")
    fields = 3 * materials
    rows = fields * QUAD
    plane = (2, rows_x, rows_y)
    sums, rim, first, last = call(
        sums_kernel,
        "sums",
        [plane, (32, rows_y), (16, LANES), (16, LANES)],
        (frac, density, energy, node_shift, node_speed),
        near_outs=(0, 1, 2, 3),
    )
    right_above, left_above = diagonal(first, -1, -1), diagonal(last, -1, 1)
    right, left = shifted(first, "zy", -1), shifted(last, "zy", 1)
    above = shifted(rim, "zx", -1)
    if lax.axis_size("zx") == 2:
        below, right_below, left_below = above, right_above, left_above
    else:
        below = shifted(rim, "zx", 1)
        right_below, left_below = diagonal(first, 1, -1), diagonal(last, 1, 1)
    tables = call(
        table_kernel,
        "tables",
        [(SUB, LANES)],
        (dest_tile.reshape(1, -1), src_block[0], dest_block[0], crossing[0], keep[0]),
        near_outs=(0,),
    )
    speed_after, shift_after, state = call(
        lagrange_kernel,
        "lagrange",
        [plane, plane, (devices, rows + SUB, LANES)],
        (
            node_shift,
            node_speed,
            sums,
            left_above,
            left_below,
            left,
            right,
            right_above,
            right_below,
            above,
            below,
            frac,
            density,
            energy,
            tables,
        ),
        near_ins=(2, 3, 4, 5, 6, 7, 8, 9, 10, 14),
        near_outs=(2,),
    )
    state = exchange(state)
    groups = devices // SUB
    totals = call(
        crossing_kernel,
        "crossings",
        [(devices, rows, LANES)],
        (state,),
        scratch=[pltpu.VMEM((SUB, groups, rows, LANES), jnp.float32)] * 2
        + [pltpu.VMEM((devices, groups, 2 * SUB, LANES), jnp.bfloat16)]
        + [pltpu.VMEM((groups, groups, SUB, LANES), jnp.float32)] * 2,
        near_ins=(0,),
        near_outs=(0,),
    )
    totals = exchange(totals)
    remapped = unpack(totals, (fields, rows_x, rows_y))
    return (remapped.reshape(3, materials, rows_x, rows_y), speed_after, shift_after)


def local_by_entries(
    frac, density, energy, node_shift, node_speed, dest_tile, src_block, dest_block, crossing, keep
):
    materials, rows_x, rows_y = frac.shape
    node_fields = jnp.concatenate([node_shift, node_speed], axis=0)
    extended = upper_rim(node_fields)
    area_now, mat_pressure, viscous, terms = zone_phase(
        frac, density, energy, slice_corners(extended[0:2]), slice_corners(extended[2:4])
    )
    term_one, term_two, term_three, term_four = terms
    gathered = (
        jnp.pad(term_one, ((0, 0), (0, 1), (0, 1)))
        + jnp.pad(term_two, ((0, 0), (1, 0), (0, 1)))
        + jnp.pad(term_three, ((0, 0), (1, 0), (1, 0)))
        + jnp.pad(term_four, ((0, 0), (0, 1), (1, 0)))
    )
    totals = spill_rim(gathered)
    speed_after, shift_after = node_update(totals, node_shift, node_speed)
    moved_rim = upper_rim(shift_after)
    area_after = zone_area(slice_corners(moved_rim))
    conserved = material_state(frac, density, energy, area_now, area_after, mat_pressure, viscous)
    nblocks = keep.shape[2]
    block_len = rows_x * rows_y // nblocks
    fields = 3 * materials
    blocks = conserved.reshape(fields, nblocks, block_len)
    size_x = lax.axis_size("zx")
    size_y = lax.axis_size("zy")
    devices = size_x * size_y
    targets = dest_tile[0, 0, :, 0]
    sources = src_block[0, 0]
    places = dest_block[0, 0]
    weights = crossing[0, 0]
    entry_count = targets.shape[0]
    capacity = max(2, 2 * entry_count // devices)
    member = (targets[:, None] == jnp.arange(devices, dtype=jnp.int32)[None, :]).astype(jnp.int32)
    before = jnp.cumsum(member, axis=0) - member
    slot_rank = jnp.sum(before * member, axis=1)
    slot_index = targets * capacity + slot_rank
    slot_total = devices * capacity
    matches = slot_index[:, None] == jnp.arange(slot_total, dtype=jnp.int32)[None, :]
    filled = jnp.any(matches, axis=0)
    owners = jnp.sum(
        jnp.where(matches, jnp.arange(entry_count, dtype=jnp.int32)[:, None], 0), axis=0
    )
    slot_weight = jnp.where(filled, weights[owners], 0.0)
    slot_place = jnp.where(filled, places[owners], nblocks)
    payload = blocks[:, sources[owners], :] * slot_weight[None, :, None]
    payload = payload.reshape(fields, size_x, size_y, capacity, block_len)
    place_ids = slot_place.reshape(1, size_x, size_y, capacity)
    arrived, arrived_ids = (
        lax.all_to_all(
            lax.all_to_all(payload, "zx", split_axis=1, concat_axis=1, tiled=True),
            "zy",
            split_axis=2,
            concat_axis=2,
            tiled=True,
        ),
        lax.all_to_all(
            lax.all_to_all(place_ids, "zx", split_axis=1, concat_axis=1, tiled=True),
            "zy",
            split_axis=2,
            concat_axis=2,
            tiled=True,
        ),
    )
    arrived = arrived.reshape(fields, slot_total, block_len)
    arrived_ids = arrived_ids.reshape(slot_total)
    landed = (
        jnp.zeros((fields, nblocks + 1, block_len), jnp.float32).at[:, arrived_ids, :].add(arrived)
    )
    result = blocks * keep[0, 0][None, :, None] + landed[:, :nblocks, :]
    remapped = result.reshape(3, materials, rows_x, rows_y)
    return (remapped, speed_after, shift_after)


def solution(mesh):
    in_specs = (
        P(None, "zx", "zy"),
        P(None, "zx", "zy"),
        P(None, "zx", "zy"),
        P(None, "zx", "zy"),
        P(None, "zx", "zy"),
        P("zx", "zy", None, None),
        P("zx", "zy", None),
        P("zx", "zy", None),
        P("zx", "zy", None),
        P("zx", "zy", None),
    )
    out_specs = (P(None, None, "zx", "zy"), P(None, "zx", "zy"), P(None, "zx", "zy"))
    return jax.shard_map(local, mesh=mesh, in_specs=in_specs, out_specs=out_specs, check_vma=False)
```

```python
import jax
import jax.numpy as jnp
import numpy as np
from jax import lax
from jax.experimental import pallas as pl
from jax.experimental.pallas import tpu as pltpu
from jax.sharding import PartitionSpec as P

TIME_STEP = 0.02
VISC_COEF = 0.25


def shifted(value, axis, by):
    peers = lax.axis_size(axis)
    return lax.ppermute(value, axis, [(i, (i + by) % peers) for i in range(peers)])


def corner_geometry(corners):
    corner_one, corner_two, corner_three, corner_four = corners
    rise_x = 1.0 + corner_three[0] - corner_one[0]
    rise_y = 1.0 + corner_three[1] - corner_one[1]
    cross_x = -1.0 + corner_four[0] - corner_two[0]
    cross_y = 1.0 + corner_four[1] - corner_two[1]
    return (rise_x, rise_y, cross_x, cross_y)


def zone_area(corners):
    rise_x, rise_y, cross_x, cross_y = corner_geometry(corners)
    return 0.5 * (rise_x * cross_y - cross_x * rise_y)


def zone_phase(frac, density, energy, shifts, speeds):
    rise_x, rise_y, cross_x, cross_y = corner_geometry(shifts)
    area_now = 0.5 * (rise_x * cross_y - cross_x * rise_y)
    speed_one, speed_two, speed_three, speed_four = speeds
    area_rate = 0.5 * (
        (speed_three[0] - speed_one[0]) * cross_y
        + rise_x * (speed_four[1] - speed_two[1])
        - (speed_four[0] - speed_two[0]) * rise_y
        - cross_x * (speed_three[1] - speed_one[1])
    )
    squeeze = jnp.minimum(area_rate / area_now, 0.0)
    gammas = (1.3 + 0.05 * jnp.arange(frac.shape[0], dtype=jnp.int32).astype(jnp.float32))[
        :, None, None
    ]
    mat_pressure = (gammas - 1.0) * density * energy
    zone_density = jnp.sum(frac * density, axis=0)
    viscous = VISC_COEF * zone_density * area_now * squeeze * squeeze
    total_pressure = jnp.sum(frac * mat_pressure, axis=0) + viscous
    half_press = 0.5 * total_pressure
    quarter_mass = 0.25 * zone_density * area_now
    term_one = jnp.stack([-half_press * cross_y, half_press * cross_x, quarter_mass])
    term_two = jnp.stack([half_press * rise_y, -half_press * rise_x, quarter_mass])
    term_three = jnp.stack([half_press * cross_y, -half_press * cross_x, quarter_mass])
    term_four = jnp.stack([-half_press * rise_y, half_press * rise_x, quarter_mass])
    return (area_now, mat_pressure, viscous, (term_one, term_two, term_three, term_four))


def node_update(totals, node_shift, node_speed):
    accel_xy = totals[0:2] / totals[2:3]
    speed_after = node_speed + TIME_STEP * accel_xy
    shift_after = node_shift + TIME_STEP * speed_after
    return (speed_after, shift_after)


def material_state(frac, density, energy, area_now, area_after, mat_pressure, viscous):
    energy_after = energy - (mat_pressure + viscous) * (area_after - area_now) / (
        density * area_now
    )
    volume = frac * area_after
    mass_now = frac * density * area_now
    return jnp.stack([volume, mass_now, mass_now * energy_after])


def upper_along_x(values):
    received = shifted(values[:, 0:1, :], "zx", -1)
    return jnp.concatenate([values, received], axis=1)


def upper_along_y(values):
    received = shifted(values[:, :, 0:1], "zy", -1)
    return jnp.concatenate([values, received], axis=2)


def upper_rim(values):
    return upper_along_y(upper_along_x(values))


def spill_along_x(values):
    received = shifted(values[:, -1:, :], "zx", 1)
    return jnp.concatenate([values[:, 0:1, :] + received, values[:, 1:-1, :]], axis=1)


def spill_along_y(values):
    received = shifted(values[:, :, -1:], "zy", 1)
    return jnp.concatenate([values[:, :, 0:1] + received, values[:, :, 1:-1]], axis=2)


def spill_rim(values):
    return spill_along_y(spill_along_x(values))


def slice_corners(extended):
    return (extended[:, :-1, :-1], extended[:, 1:, :-1], extended[:, 1:, 1:], extended[:, :-1, 1:])


SUB = 8
LANES = 128
QUAD = 4


def lower_half(shape):
    return lax.broadcasted_iota(jnp.int32, shape, len(shape) - 2) % SUB < QUAD


def zones_first(field):
    return jnp.concatenate([field[:, :LANES], field[:, LANES:]], axis=0).T


def pair_to_pieces(first, second, low):
    even = jnp.where(low, first, pltpu.roll(second, QUAD, 0))
    odd = jnp.where(low, pltpu.roll(first, QUAD, 0), second)
    return even, odd


def store_pairs(values, out_ref, row):
    low = lower_half((SUB, LANES))
    for pair in range(len(values) // 2):
        first, second = zones_first(values[2 * pair]), zones_first(values[2 * pair + 1])
        rows = slice(row + SUB * pair, row + SUB * pair + SUB)
        for octet in range(LANES // SUB):
            at = slice(SUB * octet, SUB * octet + SUB)
            even, odd = pair_to_pieces(first[at], second[at], low)
            out_ref[2 * octet, rows, :] = even
            out_ref[2 * octet + 1, rows, :] = odd


def split3(value):
    high = value.astype(jnp.bfloat16)
    left = value - high.astype(jnp.float32)
    middle = left.astype(jnp.bfloat16)
    low = (left - middle.astype(jnp.float32)).astype(jnp.bfloat16)
    return high, middle, low


def table_kernel(target_ref, source_ref, place_ref, weight_ref, keep_ref, out_ref):
    entries = target_ref.shape[1]
    row = target_ref[...].astype(jnp.float32)
    down = lax.broadcasted_iota(jnp.int32, (entries, entries), 0)
    across = lax.broadcasted_iota(jnp.int32, (entries, entries), 1)
    column = jnp.sum(jnp.where(down == across, row, 0.0), axis=1, keepdims=True)
    earlier = (row < column) | ((row == column) & (across < down))
    order = jnp.sum(jnp.where(earlier, 1.0, 0.0), axis=1, keepdims=True)
    hot = jnp.where(across.astype(jnp.float32) == order, 1.0, 0.0)
    source, place = source_ref[...], place_ref[...]
    half = LANES // 2
    source = ((source & 1) * half + (source >> 1)).astype(jnp.float32)
    place = ((place & 1) * half + (place >> 1)).astype(jnp.float32)
    parts = [part.astype(jnp.float32) for part in split3(weight_ref[...])] + [source, place]
    values = jnp.concatenate(parts + [jnp.zeros((SUB - len(parts), entries), jnp.float32)], axis=0)
    tables = jnp.dot(
        values.astype(jnp.bfloat16), hot.astype(jnp.bfloat16), preferred_element_type=jnp.float32
    )
    weights = tables[0:1] + tables[1:2] + tables[2:3]
    for table, value in enumerate((tables[3:4], weights, tables[4:5])):
        for side in range(2):
            at = slice(LANES * side, LANES * side + LANES)
            out_ref[2 * table + side : 2 * table + side + 1, :] = value[:, at]
    device = lax.broadcasted_iota(jnp.int32, (entries, LANES), 1).astype(jnp.float32)
    out_ref[6:7, :] = jnp.sum(jnp.where(column < device, 1.0, 0.0), axis=0, keepdims=True)
    lane = lax.broadcasted_iota(jnp.int32, (SUB, LANES), 1)
    keep = jnp.take_along_axis(
        jnp.broadcast_to(keep_ref[...], (SUB, LANES)),
        2 * (lane % half) + lane // half,
        axis=1,
        mode="promise_in_bounds",
    )
    out_ref[7:8, :] = keep[0:1]


def stiffness(materials):
    gammas = np.float32(1.3) + np.float32(0.05) * np.arange(materials, dtype=np.float32)
    return [float(gamma) for gamma in gammas - np.float32(1.0)]


def sums_kernel(
    frac_ref, density_ref, energy_ref, shift_ref, speed_ref, sums_ref, rim_ref, first_ref, last_ref
):
    materials = frac_ref.shape[0]
    stiff = stiffness(materials)
    mass = pressure = None
    for material in range(materials):
        part = frac_ref[material] * density_ref[material]
        force = part * energy_ref[material] * stiff[material]
        mass = part if mass is None else mass + part
        pressure = force if pressure is None else pressure + force
    sums_ref[0], sums_ref[1] = mass, pressure
    last = mass.shape[0] - 1
    for field in range(2):
        for at, ref in ((0, shift_ref), (4, speed_ref)):
            rim_ref[at + 2 * field : at + 2 * field + 2, :] = ref[field, 0:2, :]
            for copy in range(2):
                row = 16 + at + 2 * field + copy
                rim_ref[row : row + 1, :] = ref[field, last : last + 1, :]
    for field, value in enumerate((mass, pressure)):
        rim_ref[8 + field : 9 + field, :] = value[0:1]
        rim_ref[24 + field : 25 + field, :] = value[last : last + 1]
    height, width = mass.shape
    lane = lax.broadcasted_iota(jnp.int32, (height, LANES), 1)
    wanted = jnp.zeros((height, LANES), jnp.float32)
    values = [shift_ref[0], shift_ref[1], speed_ref[0], speed_ref[1], mass, pressure]
    for field, value in enumerate(values):
        row = 2 * field if field < 4 else 4 + field
        moved = value[:, :LANES]
        moved = pltpu.roll(moved, row, 1) if row else moved
        ends = (lane == row) | (lane == row + 1) if field < 4 else lane == row
        wanted = jnp.where(ends, moved, wanted)
        moved = pltpu.roll(value[:, width - LANES :], 17 + row, 1)
        wanted = jnp.where(lane == 16 + row, moved, wanted)
    wanted = jnp.concatenate([wanted, jnp.zeros((LANES - height, LANES), jnp.float32)], axis=0).T
    first_ref[...], last_ref[...] = wanted[0:16], wanted[16:32]


def lagrange_kernel(
    now_shift_ref,
    now_speed_ref,
    sums_ref,
    left_above_ref,
    left_below_ref,
    left_ref,
    right_ref,
    right_above_ref,
    right_below_ref,
    above_ref,
    below_ref,
    frac_ref,
    density_ref,
    energy_ref,
    tables_ref,
    speed_ref,
    shift_ref,
    out_ref,
):
    height, width = sums_ref.shape[1:]
    shape = (height + SUB, width + LANES)
    lane = lax.broadcasted_iota(jnp.int32, shape, 1)
    line = lax.broadcasted_iota(jnp.int32, (shape[0], width), 0)
    side_lane = lax.broadcasted_iota(jnp.int32, (16, LANES), 1)
    sides = []
    for ref, above, below in (
        (right_ref, right_above_ref, right_below_ref),
        (left_ref, left_above_ref, left_below_ref),
    ):
        beyond = jnp.where(
            side_lane < shape[0] - 1, pltpu.roll(above[...], height, 1), pltpu.roll(below[...], SUB, 1)
        )
        sides.append(jnp.where(side_lane < height, ref[...], beyond))
    sides.append(jnp.zeros((LANES - 32, LANES), jnp.float32))
    sides = jnp.concatenate(sides, axis=0).T[0 : shape[0]]

    def extend(field):
        value = (now_shift_ref, now_speed_ref, sums_ref)[field // 2][field % 2]
        value = jnp.concatenate([value, jnp.zeros((SUB, width), jnp.float32)], axis=0)
        at = 2 * field if field < 4 else 4 + field
        value = jnp.where(line == shape[0] - 1, below_ref[16 + at : 17 + at, :], value)
        value = jnp.where(line == height, above_ref[at : at + 1, :], value)
        if field < 4:
            value = jnp.where(line == height + 1, above_ref[at + 1 : at + 2, :], value)
        value = jnp.concatenate([value, jnp.zeros((shape[0], LANES), jnp.float32)], axis=1)
        value = jnp.where(lane == shape[1] - 1, sides[:, 16 + at : 17 + at], value)
        value = jnp.where(lane == width, sides[:, at : at + 1], value)
        if field < 4:
            value = jnp.where(lane == width + 1, sides[:, at + 1 : at + 2], value)
        return value

    def next_row(value):
        return pltpu.roll(value, shape[0] - 1, 0)

    def next_column(value):
        return pltpu.roll(value, shape[1] - 1, 1)

    def before_row(value):
        return pltpu.roll(value, 1, 0)

    def before_column(value):
        return pltpu.roll(value, 1, 1)

    def diagonals(value):
        across = next_column(value)
        down = next_row(value)
        return next_row(across) - value, across - down

    def geometry(shift_x, shift_y):
        rise_x, cross_x = diagonals(shift_x)
        rise_y, cross_y = diagonals(shift_y)
        return 1.0 + rise_x, 1.0 + rise_y, -1.0 + cross_x, 1.0 + cross_y

    shift_x, shift_y, speed_x, speed_y, density, pressure = [extend(field) for field in range(6)]
    rise_x, rise_y, cross_x, cross_y = geometry(shift_x, shift_y)
    area = 0.5 * (rise_x * cross_y - cross_x * rise_y)
    up_x, over_x = diagonals(speed_x)
    up_y, over_y = diagonals(speed_y)
    rate = 0.5 * (up_x * cross_y + rise_x * over_y - over_x * rise_y - cross_x * up_y)
    squeeze = jnp.minimum(rate / area, 0.0)
    viscous = VISC_COEF * density * area * squeeze * squeeze
    half = 0.5 * (pressure + viscous)
    quarter = 0.25 * density * area

    def corners(one, two, sign):
        upper = before_row(two - before_column(one))
        return sign * (one - before_column(two) + upper)

    force_x = corners(-half * cross_y, half * rise_y, 1.0)
    force_y = corners(half * cross_x, -half * rise_x, 1.0)
    both = quarter + before_column(quarter)
    mass = both + before_row(both)
    speed_x = speed_x + TIME_STEP * (force_x / mass)
    speed_y = speed_y + TIME_STEP * (force_y / mass)
    shift_x = shift_x + TIME_STEP * speed_x
    shift_y = shift_y + TIME_STEP * speed_y
    rise_x, rise_y, cross_x, cross_y = geometry(shift_x, shift_y)
    after = 0.5 * (rise_x * cross_y - cross_x * rise_y)

    def own(value):
        return value[0:height, 0:width]

    speed_ref[0], speed_ref[1] = own(speed_x), own(speed_y)
    shift_ref[0], shift_ref[1] = own(shift_x), own(shift_y)

    area, after, viscous = own(area), own(after), own(viscous)
    change = after - area
    materials = frac_ref.shape[0]
    volumes, masses, energies = [], [], []
    for material, stiff in enumerate(stiffness(materials)):
        frac, density, energy = frac_ref[material], density_ref[material], energy_ref[material]
        force = stiff * density * energy + viscous
        volumes.append(frac * after)
        masses.append(frac * density * area)
        energies.append(masses[-1] * energy - frac * force * change)
    for third, values in enumerate((volumes, masses, energies)):
        store_pairs(values, out_ref, third * materials * QUAD)
    rows = 3 * materials * QUAD
    for piece in range(out_ref.shape[0]):
        out_ref[piece, rows : rows + SUB] = tables_ref[...]


def crossing_kernel(
    state_ref, out_ref, even_ref, odd_ref, places_ref, sources_ref, weights_ref
):
    devices, rows = out_ref.shape[0], out_ref.shape[1]
    tiles = rows // SUB
    groups = devices // SUB
    capacity = LANES // SUB
    slots_ref = (even_ref, odd_ref)
    spread = (SUB, LANES)
    lane = lax.broadcasted_iota(jnp.int32, spread, 1)
    source_of = lax.broadcasted_iota(jnp.int32, spread, 0)
    piece = lane // capacity
    odd = [(piece >> bit) & 1 == 1 for bit in range(3)]

    def take(values, index):
        return jnp.take_along_axis(values, index, axis=1, mode="promise_in_bounds")

    def regroup(values):
        for bit in range(3):
            values = [
                jnp.where(odd[bit], values[i | (1 << bit)], values[i & ~(1 << bit)])
                if not (i >> bit) & 1
                else jnp.where(odd[bit], values[i & ~(1 << bit)], values[i | (1 << bit)])
                for i in range(SUB)
            ]
        return values

    for a in range(groups):
        table = [state_ref[a * SUB : a * SUB + SUB, rows + i, :] for i in range(7)]
        starts = table[6].astype(jnp.int32)
        for octet in range(groups):
            target = SUB * octet + (piece ^ source_of)
            at = take(starts, target) + lane % capacity
            valid = at < take(starts, target + 1)
            later, at = at >= LANES, at & (LANES - 1)
            source, weight, place = [
                jnp.where(later, take(table[2 * i + 1], at), take(table[2 * i], at)) for i in range(3)
            ]
            sources_ref[octet, a] = source
            weights_ref[octet, a] = jnp.where(valid, weight, 0.0)
            places = [jnp.broadcast_to(place[i : i + 1], spread) for i in range(SUB)]
            for delta, value in enumerate(regroup(places)):
                twice = jnp.concatenate([value, value], axis=0)
                places_ref[SUB * octet + delta, a] = twice.astype(jnp.bfloat16)

    def gather(octet, a):
        sources, weights = sources_ref[octet, a].astype(jnp.int32), weights_ref[octet, a]
        index = [jnp.broadcast_to(sources[i : i + 1], spread) for i in range(SUB)]
        weight = [jnp.broadcast_to(weights[i : i + 1], spread) for i in range(SUB)]
        at = [slice(SUB * tile, SUB * tile + SUB) for tile in range(tiles)]
        values = [
            [take(state_ref[a * SUB + i, rows_of], index[i]) * weight[i] for rows_of in at]
            for i in range(SUB)
        ]
        for tile, rows_of in enumerate(at):
            for delta, value in enumerate(regroup([value[tile] for value in values])):
                slots_ref[octet % 2][delta, a, rows_of] = value

    packed = (2 * SUB, LANES)
    block = lax.broadcasted_iota(jnp.int32, packed, 0).astype(jnp.float32).astype(jnp.bfloat16)
    one, zero = jnp.ones(packed, jnp.bfloat16), jnp.zeros(packed, jnp.bfloat16)

    def scatter(octet, delta):
        target = SUB * octet + delta
        slots = slots_ref[octet % 2]
        value = jnp.concatenate([slots[delta, a] for a in range(groups)], axis=1)
        parts = jnp.concatenate(split3(value), axis=0)
        place = [places_ref[target, a] for a in range(groups)]
        hot = [
            [
                jnp.where(place[a] == block + jnp.bfloat16(2 * SUB * tile), one, zero)
                for tile in range(LANES // SUB // 2)
            ]
            for a in range(groups)
        ]
        hot = jnp.concatenate([jnp.concatenate(column, axis=0) for column in hot], axis=1)
        total = lax.dot_general(
            parts,
            hot,
            (((1,), (1,)), ((), ())),
            preferred_element_type=jnp.float32,
        )
        keep = jnp.broadcast_to(state_ref[target, rows + 7 : rows + 8], (rows, LANES))
        stay = keep * state_ref[target, 0:rows]
        out_ref[target] = stay + total[0:rows] + total[rows : 2 * rows] + total[2 * rows : 3 * rows]

    lax.fori_loop(0, groups, lambda a, carry: (gather(0, a), carry)[1], 0)
    for octet in range(groups):

        def step(a, carry):
            if octet + 1 < groups:
                gather(octet + 1, a)
            for i in range(SUB // groups):
                scatter(octet, SUB // groups * a + i)
            return carry

        lax.fori_loop(0, groups, step, 0, unroll=True)


UNPACK_PARTS = 4


def unpack_kernel(sums_ref, out_ref, rows_ref, sems):
    low = lower_half((SUB, LANES))
    half = LANES // 2
    fields = out_ref.shape[0] // UNPACK_PARTS
    copies = []
    for pair in range(sums_ref.shape[1] // SUB):
        at = slice(SUB * pair, SUB * pair + SUB)
        first, second = [], []
        for octet in range(LANES // SUB):
            even, odd = pair_to_pieces(sums_ref[2 * octet, at], sums_ref[2 * octet + 1, at], low)
            first.append(even)
            second.append(odd)
        for field, tiles in ((2 * pair, first), (2 * pair + 1, second)):
            blocks = jnp.concatenate(tiles, axis=0).T
            rows_ref[field, :, :LANES] = blocks[:half]
            rows_ref[field, :, LANES:] = blocks[half:]
        if (2 * pair + 2) % fields == 0:
            part = pl.ds(2 * pair + 2 - fields, fields)
            sem = sems.at[len(copies)]
            copies.append(pltpu.make_async_copy(rows_ref.at[part], out_ref.at[part], sem))
            copies[-1].start()
    for copy in copies:
        copy.wait()


def unpack(sums, shape):
    return pl.pallas_call(
        unpack_kernel,
        out_shape=jax.ShapeDtypeStruct(shape, jnp.float32),
        in_specs=whole(1),
        out_specs=pl.BlockSpec(memory_space=pl.ANY),
        scratch_shapes=[pltpu.VMEM(shape, jnp.float32), pltpu.SemaphoreType.DMA((UNPACK_PARTS,))],
        name="unpack",
    )(near(sums))


def whole(count):
    return [pl.BlockSpec(memory_space=pltpu.VMEM)] * count


def near(value):
    return pltpu.with_memory_space_constraint(value, pltpu.VMEM)


def call(kernel, name, outs, inputs, scratch=(), near_ins=(), near_outs=()):
    inputs = [
        near(value) if i in near_ins else value for i, value in enumerate(inputs)
    ]
    shapes = [
        pltpu.VMEM(shape, jnp.float32) if i in near_outs else jax.ShapeDtypeStruct(shape, jnp.float32)
        for i, shape in enumerate(outs)
    ]
    return pl.pallas_call(
        kernel,
        out_shape=shapes if len(shapes) > 1 else shapes[0],
        in_specs=whole(len(inputs)),
        out_specs=whole(len(shapes)) if len(shapes) > 1 else whole(1)[0],
        scratch_shapes=scratch,
        name=name,
    )(*inputs)


def exchange(value):
    return lax.all_to_all(value, ("zx", "zy"), 0, 0, tiled=True)


def diagonal(value, by_x, by_y):
    size_x, size_y = lax.axis_size("zx"), lax.axis_size("zy")
    route = [
        (a * size_y + b, (a + by_x) % size_x * size_y + (b + by_y) % size_y)
        for a in range(size_x)
        for b in range(size_y)
    ]
    return lax.ppermute(value, ("zx", "zy"), route)


def local(*arguments):
    materials, rows_x, rows_y = arguments[0].shape
    devices = lax.axis_size("zx") * lax.axis_size("zy")
    entries, nblocks = arguments[6].shape[2], arguments[9].shape[2]
    fits = (rows_x, rows_y, nblocks) == (64, 256, LANES) and materials == 8
    if fits and devices == LANES // QUAD and entries == 2 * LANES:
        return local_by_zones(*arguments)
    return local_by_entries(*arguments)


def local_by_zones(
    frac, density, energy, node_shift, node_speed, dest_tile, src_block, dest_block, crossing, keep
):
    materials, rows_x, rows_y = frac.shape
    devices = lax.axis_size("zx") * lax.axis_size("zy")
    fields = 3 * materials
    rows = fields * QUAD
    plane = (2, rows_x, rows_y)
    sums, rim, first, last = call(
        sums_kernel,
        "sums",
        [plane, (32, rows_y), (16, LANES), (16, LANES)],
        (frac, density, energy, node_shift, node_speed),
        near_outs=(0, 1, 2, 3),
    )
    right_above, left_above = diagonal(first, -1, -1), diagonal(last, -1, 1)
    right, left = shifted(first, "zy", -1), shifted(last, "zy", 1)
    above = shifted(rim, "zx", -1)
    if lax.axis_size("zx") == 2:
        below, right_below, left_below = above, right_above, left_above
    else:
        below = shifted(rim, "zx", 1)
        right_below, left_below = diagonal(first, 1, -1), diagonal(last, 1, 1)
    tables = call(
        table_kernel,
        "tables",
        [(SUB, LANES)],
        (dest_tile.reshape(1, -1), src_block[0], dest_block[0], crossing[0], keep[0]),
        near_outs=(0,),
    )
    speed_after, shift_after, state = call(
        lagrange_kernel,
        "lagrange",
        [plane, plane, (devices, rows + SUB, LANES)],
        (
            node_shift,
            node_speed,
            sums,
            left_above,
            left_below,
            left,
            right,
            right_above,
            right_below,
            above,
            below,
            frac,
            density,
            energy,
            tables,
        ),
        near_ins=(2, 3, 4, 5, 6, 7, 8, 9, 10, 14),
        near_outs=(2,),
    )
    state = exchange(state)
    groups = devices // SUB
    totals = call(
        crossing_kernel,
        "crossings",
        [(devices, rows, LANES)],
        (state,),
        scratch=[pltpu.VMEM((SUB, groups, rows, LANES), jnp.float32)] * 2
        + [pltpu.VMEM((devices, groups, 2 * SUB, LANES), jnp.bfloat16)]
        + [pltpu.VMEM((groups, groups, SUB, LANES), jnp.float32)] * 2,
        near_ins=(0,),
        near_outs=(0,),
    )
    totals = exchange(totals)
    remapped = unpack(totals, (fields, rows_x, rows_y))
    return (remapped.reshape(3, materials, rows_x, rows_y), speed_after, shift_after)


def local_by_entries(
    frac, density, energy, node_shift, node_speed, dest_tile, src_block, dest_block, crossing, keep
):
    materials, rows_x, rows_y = frac.shape
    node_fields = jnp.concatenate([node_shift, node_speed], axis=0)
    extended = upper_rim(node_fields)
    area_now, mat_pressure, viscous, terms = zone_phase(
        frac, density, energy, slice_corners(extended[0:2]), slice_corners(extended[2:4])
    )
    term_one, term_two, term_three, term_four = terms
    gathered = (
        jnp.pad(term_one, ((0, 0), (0, 1), (0, 1)))
        + jnp.pad(term_two, ((0, 0), (1, 0), (0, 1)))
        + jnp.pad(term_three, ((0, 0), (1, 0), (1, 0)))
        + jnp.pad(term_four, ((0, 0), (0, 1), (1, 0)))
    )
    totals = spill_rim(gathered)
    speed_after, shift_after = node_update(totals, node_shift, node_speed)
    moved_rim = upper_rim(shift_after)
    area_after = zone_area(slice_corners(moved_rim))
    conserved = material_state(frac, density, energy, area_now, area_after, mat_pressure, viscous)
    nblocks = keep.shape[2]
    block_len = rows_x * rows_y // nblocks
    fields = 3 * materials
    blocks = conserved.reshape(fields, nblocks, block_len)
    size_x = lax.axis_size("zx")
    size_y = lax.axis_size("zy")
    devices = size_x * size_y
    targets = dest_tile[0, 0, :, 0]
    sources = src_block[0, 0]
    places = dest_block[0, 0]
    weights = crossing[0, 0]
    entry_count = targets.shape[0]
    capacity = max(2, 2 * entry_count // devices)
    member = (targets[:, None] == jnp.arange(devices, dtype=jnp.int32)[None, :]).astype(jnp.int32)
    before = jnp.cumsum(member, axis=0) - member
    slot_rank = jnp.sum(before * member, axis=1)
    slot_index = targets * capacity + slot_rank
    slot_total = devices * capacity
    matches = slot_index[:, None] == jnp.arange(slot_total, dtype=jnp.int32)[None, :]
    filled = jnp.any(matches, axis=0)
    owners = jnp.sum(
        jnp.where(matches, jnp.arange(entry_count, dtype=jnp.int32)[:, None], 0), axis=0
    )
    slot_weight = jnp.where(filled, weights[owners], 0.0)
    slot_place = jnp.where(filled, places[owners], nblocks)
    payload = blocks[:, sources[owners], :] * slot_weight[None, :, None]
    payload = payload.reshape(fields, size_x, size_y, capacity, block_len)
    place_ids = slot_place.reshape(1, size_x, size_y, capacity)
    arrived, arrived_ids = (
        lax.all_to_all(
            lax.all_to_all(payload, "zx", split_axis=1, concat_axis=1, tiled=True),
            "zy",
            split_axis=2,
            concat_axis=2,
            tiled=True,
        ),
        lax.all_to_all(
            lax.all_to_all(place_ids, "zx", split_axis=1, concat_axis=1, tiled=True),
            "zy",
            split_axis=2,
            concat_axis=2,
            tiled=True,
        ),
    )
    arrived = arrived.reshape(fields, slot_total, block_len)
    arrived_ids = arrived_ids.reshape(slot_total)
    landed = (
        jnp.zeros((fields, nblocks + 1, block_len), jnp.float32).at[:, arrived_ids, :].add(arrived)
    )
    result = blocks * keep[0, 0][None, :, None] + landed[:, :nblocks, :]
    remapped = result.reshape(3, materials, rows_x, rows_y)
    return (remapped, speed_after, shift_after)


def solution(mesh):
    in_specs = (
        P(None, "zx", "zy"),
        P(None, "zx", "zy"),
        P(None, "zx", "zy"),
        P(None, "zx", "zy"),
        P(None, "zx", "zy"),
        P("zx", "zy", None, None),
        P("zx", "zy", None),
        P("zx", "zy", None),
        P("zx", "zy", None),
        P("zx", "zy", None),
    )
    out_specs = (P(None, None, "zx", "zy"), P(None, "zx", "zy"), P(None, "zx", "zy"))
    return jax.shard_map(local, mesh=mesh, in_specs=in_specs, out_specs=out_specs, check_vma=False)
```

```python
import jax
import jax.numpy as jnp
import numpy as np
from jax import lax
from jax.experimental import pallas as pl
from jax.experimental.pallas import tpu as pltpu
from jax.sharding import PartitionSpec as P

TIME_STEP = 0.02
VISC_COEF = 0.25


def shifted(value, axis, by):
    peers = lax.axis_size(axis)
    return lax.ppermute(value, axis, [(i, (i + by) % peers) for i in range(peers)])


def corner_geometry(corners):
    corner_one, corner_two, corner_three, corner_four = corners
    rise_x = 1.0 + corner_three[0] - corner_one[0]
    rise_y = 1.0 + corner_three[1] - corner_one[1]
    cross_x = -1.0 + corner_four[0] - corner_two[0]
    cross_y = 1.0 + corner_four[1] - corner_two[1]
    return (rise_x, rise_y, cross_x, cross_y)


def zone_area(corners):
    rise_x, rise_y, cross_x, cross_y = corner_geometry(corners)
    return 0.5 * (rise_x * cross_y - cross_x * rise_y)


def zone_phase(frac, density, energy, shifts, speeds):
    rise_x, rise_y, cross_x, cross_y = corner_geometry(shifts)
    area_now = 0.5 * (rise_x * cross_y - cross_x * rise_y)
    speed_one, speed_two, speed_three, speed_four = speeds
    area_rate = 0.5 * (
        (speed_three[0] - speed_one[0]) * cross_y
        + rise_x * (speed_four[1] - speed_two[1])
        - (speed_four[0] - speed_two[0]) * rise_y
        - cross_x * (speed_three[1] - speed_one[1])
    )
    squeeze = jnp.minimum(area_rate / area_now, 0.0)
    gammas = (1.3 + 0.05 * jnp.arange(frac.shape[0], dtype=jnp.int32).astype(jnp.float32))[
        :, None, None
    ]
    mat_pressure = (gammas - 1.0) * density * energy
    zone_density = jnp.sum(frac * density, axis=0)
    viscous = VISC_COEF * zone_density * area_now * squeeze * squeeze
    total_pressure = jnp.sum(frac * mat_pressure, axis=0) + viscous
    half_press = 0.5 * total_pressure
    quarter_mass = 0.25 * zone_density * area_now
    term_one = jnp.stack([-half_press * cross_y, half_press * cross_x, quarter_mass])
    term_two = jnp.stack([half_press * rise_y, -half_press * rise_x, quarter_mass])
    term_three = jnp.stack([half_press * cross_y, -half_press * cross_x, quarter_mass])
    term_four = jnp.stack([-half_press * rise_y, half_press * rise_x, quarter_mass])
    return (area_now, mat_pressure, viscous, (term_one, term_two, term_three, term_four))


def node_update(totals, node_shift, node_speed):
    accel_xy = totals[0:2] / totals[2:3]
    speed_after = node_speed + TIME_STEP * accel_xy
    shift_after = node_shift + TIME_STEP * speed_after
    return (speed_after, shift_after)


def material_state(frac, density, energy, area_now, area_after, mat_pressure, viscous):
    energy_after = energy - (mat_pressure + viscous) * (area_after - area_now) / (
        density * area_now
    )
    volume = frac * area_after
    mass_now = frac * density * area_now
    return jnp.stack([volume, mass_now, mass_now * energy_after])


def upper_along_x(values):
    received = shifted(values[:, 0:1, :], "zx", -1)
    return jnp.concatenate([values, received], axis=1)


def upper_along_y(values):
    received = shifted(values[:, :, 0:1], "zy", -1)
    return jnp.concatenate([values, received], axis=2)


def upper_rim(values):
    return upper_along_y(upper_along_x(values))


def spill_along_x(values):
    received = shifted(values[:, -1:, :], "zx", 1)
    return jnp.concatenate([values[:, 0:1, :] + received, values[:, 1:-1, :]], axis=1)


def spill_along_y(values):
    received = shifted(values[:, :, -1:], "zy", 1)
    return jnp.concatenate([values[:, :, 0:1] + received, values[:, :, 1:-1]], axis=2)


def spill_rim(values):
    return spill_along_y(spill_along_x(values))


def slice_corners(extended):
    return (extended[:, :-1, :-1], extended[:, 1:, :-1], extended[:, 1:, 1:], extended[:, :-1, 1:])


SUB = 8
LANES = 128
QUAD = 4


def lower_half(shape):
    return lax.broadcasted_iota(jnp.int32, shape, len(shape) - 2) % SUB < QUAD


def zones_first(field):
    return jnp.concatenate([field[:, :LANES], field[:, LANES:]], axis=0).T


def pair_to_pieces(first, second, low):
    even = jnp.where(low, first, pltpu.roll(second, QUAD, 0))
    odd = jnp.where(low, pltpu.roll(first, QUAD, 0), second)
    return even, odd


def store_pairs(values, out_ref, row):
    low = lower_half((SUB, LANES))
    for pair in range(len(values) // 2):
        first, second = zones_first(values[2 * pair]), zones_first(values[2 * pair + 1])
        rows = slice(row + SUB * pair, row + SUB * pair + SUB)
        for octet in range(LANES // SUB):
            at = slice(SUB * octet, SUB * octet + SUB)
            even, odd = pair_to_pieces(first[at], second[at], low)
            out_ref[2 * octet, rows, :] = even
            out_ref[2 * octet + 1, rows, :] = odd


def split3(value):
    high = value.astype(jnp.bfloat16)
    left = value - high.astype(jnp.float32)
    middle = left.astype(jnp.bfloat16)
    low = (left - middle.astype(jnp.float32)).astype(jnp.bfloat16)
    return high, middle, low


def table_kernel(target_ref, source_ref, place_ref, weight_ref, keep_ref, out_ref):
    entries = target_ref.shape[1]
    row = target_ref[...].astype(jnp.float32)
    down = lax.broadcasted_iota(jnp.int32, (entries, entries), 0)
    across = lax.broadcasted_iota(jnp.int32, (entries, entries), 1)
    column = jnp.sum(jnp.where(down == across, row, 0.0), axis=1, keepdims=True)
    earlier = (row < column) | ((row == column) & (across < down))
    order = jnp.sum(jnp.where(earlier, 1.0, 0.0), axis=1, keepdims=True)
    hot = jnp.where(across.astype(jnp.float32) == order, 1.0, 0.0)
    source, place = source_ref[...], place_ref[...]
    half = LANES // 2
    source = ((source & 1) * half + (source >> 1)).astype(jnp.float32)
    place = ((place & 1) * half + (place >> 1)).astype(jnp.float32)
    parts = [part.astype(jnp.float32) for part in split3(weight_ref[...])] + [source, place]
    values = jnp.concatenate(parts + [jnp.zeros((SUB - len(parts), entries), jnp.float32)], axis=0)
    tables = jnp.dot(
        values.astype(jnp.bfloat16), hot.astype(jnp.bfloat16), preferred_element_type=jnp.float32
    )
    weights = tables[0:1] + tables[1:2] + tables[2:3]
    for table, value in enumerate((tables[3:4], weights, tables[4:5])):
        for side in range(2):
            at = slice(LANES * side, LANES * side + LANES)
            out_ref[2 * table + side : 2 * table + side + 1, :] = value[:, at]
    device = lax.broadcasted_iota(jnp.int32, (entries, LANES), 1).astype(jnp.float32)
    out_ref[6:7, :] = jnp.sum(jnp.where(column < device, 1.0, 0.0), axis=0, keepdims=True)
    lane = lax.broadcasted_iota(jnp.int32, (SUB, LANES), 1)
    keep = jnp.take_along_axis(
        jnp.broadcast_to(keep_ref[...], (SUB, LANES)),
        2 * (lane % half) + lane // half,
        axis=1,
        mode="promise_in_bounds",
    )
    out_ref[7:8, :] = keep[0:1]


def stiffness(materials):
    gammas = np.float32(1.3) + np.float32(0.05) * np.arange(materials, dtype=np.float32)
    return [float(gamma) for gamma in gammas - np.float32(1.0)]


def sums_kernel(
    frac_ref, density_ref, energy_ref, shift_ref, speed_ref, sums_ref, rim_ref, first_ref, last_ref
):
    materials = frac_ref.shape[0]
    stiff = stiffness(materials)
    mass = pressure = None
    for material in range(materials):
        part = frac_ref[material] * density_ref[material]
        force = part * energy_ref[material] * stiff[material]
        mass = part if mass is None else mass + part
        pressure = force if pressure is None else pressure + force
    sums_ref[0], sums_ref[1] = mass, pressure
    last = mass.shape[0] - 1
    for field in range(2):
        for at, ref in ((0, shift_ref), (4, speed_ref)):
            rim_ref[at + 2 * field : at + 2 * field + 2, :] = ref[field, 0:2, :]
            for copy in range(2):
                row = 16 + at + 2 * field + copy
                rim_ref[row : row + 1, :] = ref[field, last : last + 1, :]
    for field, value in enumerate((mass, pressure)):
        rim_ref[8 + field : 9 + field, :] = value[0:1]
        rim_ref[24 + field : 25 + field, :] = value[last : last + 1]
    height, width = mass.shape
    lane = lax.broadcasted_iota(jnp.int32, (height, LANES), 1)
    wanted = jnp.zeros((height, LANES), jnp.float32)
    values = [shift_ref[0], shift_ref[1], speed_ref[0], speed_ref[1], mass, pressure]
    for field, value in enumerate(values):
        row = 2 * field if field < 4 else 4 + field
        moved = value[:, :LANES]
        moved = pltpu.roll(moved, row, 1) if row else moved
        ends = (lane == row) | (lane == row + 1) if field < 4 else lane == row
        wanted = jnp.where(ends, moved, wanted)
        moved = pltpu.roll(value[:, width - LANES :], 17 + row, 1)
        wanted = jnp.where(lane == 16 + row, moved, wanted)
    wanted = jnp.concatenate([wanted, jnp.zeros((LANES - height, LANES), jnp.float32)], axis=0).T
    first_ref[...], last_ref[...] = wanted[0:16], wanted[16:32]


def lagrange_kernel(
    now_shift_ref,
    now_speed_ref,
    sums_ref,
    left_above_ref,
    left_below_ref,
    left_ref,
    right_ref,
    right_above_ref,
    right_below_ref,
    above_ref,
    below_ref,
    frac_ref,
    density_ref,
    energy_ref,
    tables_ref,
    speed_ref,
    shift_ref,
    out_ref,
):
    height, width = sums_ref.shape[1:]
    shape = (height + SUB, width + LANES)
    lane = lax.broadcasted_iota(jnp.int32, (shape[0], LANES), 1)
    line = lax.broadcasted_iota(jnp.int32, (SUB, width), 0)
    side_lane = lax.broadcasted_iota(jnp.int32, (16, LANES), 1)
    sides = []
    for ref, above, below in (
        (right_ref, right_above_ref, right_below_ref),
        (left_ref, left_above_ref, left_below_ref),
    ):
        beyond = jnp.where(
            side_lane < shape[0] - 1, pltpu.roll(above[...], height, 1), pltpu.roll(below[...], SUB, 1)
        )
        sides.append(jnp.where(side_lane < height, ref[...], beyond))
    sides.append(jnp.zeros((LANES - 32, LANES), jnp.float32))
    sides = jnp.concatenate(sides, axis=0).T[0 : shape[0]]

    def extend(field):
        value = (now_shift_ref, now_speed_ref, sums_ref)[field // 2][field % 2]
        at = 2 * field if field < 4 else 4 + field
        edge = jnp.where(line == SUB - 1, below_ref[16 + at : 17 + at, :], above_ref[at : at + 1, :])
        if field < 4:
            edge = jnp.where(line == 1, above_ref[at + 1 : at + 2, :], edge)
        value = jnp.concatenate([value, edge], axis=0)
        edge = jnp.where(lane == LANES - 1, sides[:, 16 + at : 17 + at], sides[:, at : at + 1])
        if field < 4:
            edge = jnp.where(lane == 1, sides[:, at + 1 : at + 2], edge)
        value = jnp.concatenate([value, edge], axis=1)
        return value

    def next_row(value):
        return pltpu.roll(value, shape[0] - 1, 0)

    def next_column(value):
        return pltpu.roll(value, shape[1] - 1, 1)

    def before_row(value):
        return pltpu.roll(value, 1, 0)

    def before_column(value):
        return pltpu.roll(value, 1, 1)

    def diagonals(value):
        across = next_column(value)
        down = next_row(value)
        return next_row(across) - value, across - down

    def geometry(shift_x, shift_y):
        rise_x, cross_x = diagonals(shift_x)
        rise_y, cross_y = diagonals(shift_y)
        return 1.0 + rise_x, 1.0 + rise_y, -1.0 + cross_x, 1.0 + cross_y

    shift_x, shift_y, speed_x, speed_y, density, pressure = [extend(field) for field in range(6)]
    rise_x, rise_y, cross_x, cross_y = geometry(shift_x, shift_y)
    area = 0.5 * (rise_x * cross_y - cross_x * rise_y)
    up_x, over_x = diagonals(speed_x)
    up_y, over_y = diagonals(speed_y)
    rate = 0.5 * (up_x * cross_y + rise_x * over_y - over_x * rise_y - cross_x * up_y)
    squeeze = jnp.minimum(rate / area, 0.0)
    viscous = VISC_COEF * density * area * squeeze * squeeze
    half = 0.5 * (pressure + viscous)
    quarter = 0.25 * density * area

    def corners(one, two, sign):
        upper = before_row(two - before_column(one))
        return sign * (one - before_column(two) + upper)

    force_x = corners(-half * cross_y, half * rise_y, 1.0)
    force_y = corners(half * cross_x, -half * rise_x, 1.0)
    both = quarter + before_column(quarter)
    mass = both + before_row(both)
    speed_x = speed_x + TIME_STEP * (force_x / mass)
    speed_y = speed_y + TIME_STEP * (force_y / mass)
    shift_x = shift_x + TIME_STEP * speed_x
    shift_y = shift_y + TIME_STEP * speed_y
    rise_x, rise_y, cross_x, cross_y = geometry(shift_x, shift_y)
    after = 0.5 * (rise_x * cross_y - cross_x * rise_y)

    def own(value):
        return value[0:height, 0:width]

    speed_ref[0], speed_ref[1] = own(speed_x), own(speed_y)
    shift_ref[0], shift_ref[1] = own(shift_x), own(shift_y)

    area, after, viscous = own(area), own(after), own(viscous)
    change = after - area
    materials = frac_ref.shape[0]
    volumes, masses, energies = [], [], []
    for material, stiff in enumerate(stiffness(materials)):
        frac, density, energy = frac_ref[material], density_ref[material], energy_ref[material]
        force = stiff * density * energy + viscous
        volumes.append(frac * after)
        masses.append(frac * density * area)
        energies.append(masses[-1] * energy - frac * force * change)
    for third, values in enumerate((volumes, masses, energies)):
        store_pairs(values, out_ref, third * materials * QUAD)
    rows = 3 * materials * QUAD
    for piece in range(out_ref.shape[0]):
        out_ref[piece, rows : rows + SUB] = tables_ref[...]


def crossing_kernel(
    state_ref, out_ref, even_ref, odd_ref, places_ref, sources_ref, weights_ref
):
    devices, rows = out_ref.shape[0], out_ref.shape[1]
    tiles = rows // SUB
    groups = devices // SUB
    capacity = LANES // SUB
    slots_ref = (even_ref, odd_ref)
    spread = (SUB, LANES)
    lane = lax.broadcasted_iota(jnp.int32, spread, 1)
    source_of = lax.broadcasted_iota(jnp.int32, spread, 0)
    piece = lane // capacity
    odd = [(piece >> bit) & 1 == 1 for bit in range(3)]

    def take(values, index):
        return jnp.take_along_axis(values, index, axis=1, mode="promise_in_bounds")

    def regroup(values):
        for bit in range(3):
            values = [
                jnp.where(odd[bit], values[i | (1 << bit)], values[i & ~(1 << bit)])
                if not (i >> bit) & 1
                else jnp.where(odd[bit], values[i & ~(1 << bit)], values[i | (1 << bit)])
                for i in range(SUB)
            ]
        return values

    for a in range(groups):
        table = [state_ref[a * SUB : a * SUB + SUB, rows + i, :] for i in range(7)]
        starts = table[6].astype(jnp.int32)
        for octet in range(groups):
            target = SUB * octet + (piece ^ source_of)
            at = take(starts, target) + lane % capacity
            valid = at < take(starts, target + 1)
            later, at = at >= LANES, at & (LANES - 1)
            source, weight, place = [
                jnp.where(later, take(table[2 * i + 1], at), take(table[2 * i], at)) for i in range(3)
            ]
            sources_ref[octet, a] = source
            weights_ref[octet, a] = jnp.where(valid, weight, 0.0)
            places = [jnp.broadcast_to(place[i : i + 1], spread) for i in range(SUB)]
            for delta, value in enumerate(regroup(places)):
                twice = jnp.concatenate([value, value], axis=0)
                places_ref[SUB * octet + delta, a] = twice.astype(jnp.bfloat16)

    def gather(octet, a):
        sources, weights = sources_ref[octet, a].astype(jnp.int32), weights_ref[octet, a]
        index = [jnp.broadcast_to(sources[i : i + 1], spread) for i in range(SUB)]
        weight = [jnp.broadcast_to(weights[i : i + 1], spread) for i in range(SUB)]
        at = [slice(SUB * tile, SUB * tile + SUB) for tile in range(tiles)]
        values = [
            [take(state_ref[a * SUB + i, rows_of], index[i]) * weight[i] for rows_of in at]
            for i in range(SUB)
        ]
        for tile, rows_of in enumerate(at):
            for delta, value in enumerate(regroup([value[tile] for value in values])):
                slots_ref[octet % 2][delta, a, rows_of] = value

    packed = (2 * SUB, LANES)
    block = lax.broadcasted_iota(jnp.int32, packed, 0).astype(jnp.float32).astype(jnp.bfloat16)
    one, zero = jnp.ones(packed, jnp.bfloat16), jnp.zeros(packed, jnp.bfloat16)

    def scatter(octet, delta):
        target = SUB * octet + delta
        slots = slots_ref[octet % 2]
        value = jnp.concatenate([slots[delta, a] for a in range(groups)], axis=1)
        parts = jnp.concatenate(split3(value), axis=0)
        place = [places_ref[target, a] for a in range(groups)]
        hot = [
            [
                jnp.where(place[a] == block + jnp.bfloat16(2 * SUB * tile), one, zero)
                for tile in range(LANES // SUB // 2)
            ]
            for a in range(groups)
        ]
        hot = jnp.concatenate([jnp.concatenate(column, axis=0) for column in hot], axis=1)
        total = lax.dot_general(
            parts,
            hot,
            (((1,), (1,)), ((), ())),
            preferred_element_type=jnp.float32,
        )
        keep = jnp.broadcast_to(state_ref[target, rows + 7 : rows + 8], (rows, LANES))
        stay = keep * state_ref[target, 0:rows]
        out_ref[target] = stay + total[0:rows] + total[rows : 2 * rows] + total[2 * rows : 3 * rows]

    lax.fori_loop(0, groups, lambda a, carry: (gather(0, a), carry)[1], 0)
    for octet in range(groups):

        def step(a, carry):
            if octet + 1 < groups:
                gather(octet + 1, a)
            for i in range(SUB // groups):
                scatter(octet, SUB // groups * a + i)
            return carry

        lax.fori_loop(0, groups, step, 0, unroll=True)


UNPACK_PARTS = 4


def unpack_kernel(sums_ref, out_ref, rows_ref, sems):
    low = lower_half((SUB, LANES))
    half = LANES // 2
    fields = out_ref.shape[0] // UNPACK_PARTS
    copies = []
    for pair in range(sums_ref.shape[1] // SUB):
        at = slice(SUB * pair, SUB * pair + SUB)
        first, second = [], []
        for octet in range(LANES // SUB):
            even, odd = pair_to_pieces(sums_ref[2 * octet, at], sums_ref[2 * octet + 1, at], low)
            first.append(even)
            second.append(odd)
        for field, tiles in ((2 * pair, first), (2 * pair + 1, second)):
            blocks = jnp.concatenate(tiles, axis=0).T
            rows_ref[field, :, :LANES] = blocks[:half]
            rows_ref[field, :, LANES:] = blocks[half:]
        if (2 * pair + 2) % fields == 0:
            part = pl.ds(2 * pair + 2 - fields, fields)
            sem = sems.at[len(copies)]
            copies.append(pltpu.make_async_copy(rows_ref.at[part], out_ref.at[part], sem))
            copies[-1].start()
    for copy in copies:
        copy.wait()


def unpack(sums, shape):
    return pl.pallas_call(
        unpack_kernel,
        out_shape=jax.ShapeDtypeStruct(shape, jnp.float32),
        in_specs=whole(1),
        out_specs=pl.BlockSpec(memory_space=pl.ANY),
        scratch_shapes=[pltpu.VMEM(shape, jnp.float32), pltpu.SemaphoreType.DMA((UNPACK_PARTS,))],
        name="unpack",
    )(near(sums))


def whole(count):
    return [pl.BlockSpec(memory_space=pltpu.VMEM)] * count


def near(value):
    return pltpu.with_memory_space_constraint(value, pltpu.VMEM)


def call(kernel, name, outs, inputs, scratch=(), near_ins=(), near_outs=()):
    inputs = [
        near(value) if i in near_ins else value for i, value in enumerate(inputs)
    ]
    shapes = [
        pltpu.VMEM(shape, jnp.float32) if i in near_outs else jax.ShapeDtypeStruct(shape, jnp.float32)
        for i, shape in enumerate(outs)
    ]
    return pl.pallas_call(
        kernel,
        out_shape=shapes if len(shapes) > 1 else shapes[0],
        in_specs=whole(len(inputs)),
        out_specs=whole(len(shapes)) if len(shapes) > 1 else whole(1)[0],
        scratch_shapes=scratch,
        name=name,
    )(*inputs)


def exchange(value):
    return lax.all_to_all(value, ("zx", "zy"), 0, 0, tiled=True)


def diagonal(value, by_x, by_y):
    size_x, size_y = lax.axis_size("zx"), lax.axis_size("zy")
    route = [
        (a * size_y + b, (a + by_x) % size_x * size_y + (b + by_y) % size_y)
        for a in range(size_x)
        for b in range(size_y)
    ]
    return lax.ppermute(value, ("zx", "zy"), route)


def local(*arguments):
    materials, rows_x, rows_y = arguments[0].shape
    devices = lax.axis_size("zx") * lax.axis_size("zy")
    entries, nblocks = arguments[6].shape[2], arguments[9].shape[2]
    fits = (rows_x, rows_y, nblocks) == (64, 256, LANES) and materials == 8
    if fits and devices == LANES // QUAD and entries == 2 * LANES:
        return local_by_zones(*arguments)
    return local_by_entries(*arguments)


def local_by_zones(
    frac, density, energy, node_shift, node_speed, dest_tile, src_block, dest_block, crossing, keep
):
    materials, rows_x, rows_y = frac.shape
    devices = lax.axis_size("zx") * lax.axis_size("zy")
    fields = 3 * materials
    rows = fields * QUAD
    plane = (2, rows_x, rows_y)
    sums, rim, first, last = call(
        sums_kernel,
        "sums",
        [plane, (32, rows_y), (16, LANES), (16, LANES)],
        (frac, density, energy, node_shift, node_speed),
        near_outs=(0, 1, 2, 3),
    )
    right_above, left_above = diagonal(first, -1, -1), diagonal(last, -1, 1)
    right, left = shifted(first, "zy", -1), shifted(last, "zy", 1)
    above = shifted(rim, "zx", -1)
    if lax.axis_size("zx") == 2:
        below, right_below, left_below = above, right_above, left_above
    else:
        below = shifted(rim, "zx", 1)
        right_below, left_below = diagonal(first, 1, -1), diagonal(last, 1, 1)
    tables = call(
        table_kernel,
        "tables",
        [(SUB, LANES)],
        (dest_tile.reshape(1, -1), src_block[0], dest_block[0], crossing[0], keep[0]),
        near_outs=(0,),
    )
    speed_after, shift_after, state = call(
        lagrange_kernel,
        "lagrange",
        [plane, plane, (devices, rows + SUB, LANES)],
        (
            node_shift,
            node_speed,
            sums,
            left_above,
            left_below,
            left,
            right,
            right_above,
            right_below,
            above,
            below,
            frac,
            density,
            energy,
            tables,
        ),
        near_ins=(2, 3, 4, 5, 6, 7, 8, 9, 10, 14),
        near_outs=(2,),
    )
    state = exchange(state)
    groups = devices // SUB
    totals = call(
        crossing_kernel,
        "crossings",
        [(devices, rows, LANES)],
        (state,),
        scratch=[pltpu.VMEM((SUB, groups, rows, LANES), jnp.float32)] * 2
        + [pltpu.VMEM((devices, groups, 2 * SUB, LANES), jnp.bfloat16)]
        + [pltpu.VMEM((groups, groups, SUB, LANES), jnp.float32)] * 2,
        near_ins=(0,),
        near_outs=(0,),
    )
    totals = exchange(totals)
    remapped = unpack(totals, (fields, rows_x, rows_y))
    return (remapped.reshape(3, materials, rows_x, rows_y), speed_after, shift_after)


def local_by_entries(
    frac, density, energy, node_shift, node_speed, dest_tile, src_block, dest_block, crossing, keep
):
    materials, rows_x, rows_y = frac.shape
    node_fields = jnp.concatenate([node_shift, node_speed], axis=0)
    extended = upper_rim(node_fields)
    area_now, mat_pressure, viscous, terms = zone_phase(
        frac, density, energy, slice_corners(extended[0:2]), slice_corners(extended[2:4])
    )
    term_one, term_two, term_three, term_four = terms
    gathered = (
        jnp.pad(term_one, ((0, 0), (0, 1), (0, 1)))
        + jnp.pad(term_two, ((0, 0), (1, 0), (0, 1)))
        + jnp.pad(term_three, ((0, 0), (1, 0), (1, 0)))
        + jnp.pad(term_four, ((0, 0), (0, 1), (1, 0)))
    )
    totals = spill_rim(gathered)
    speed_after, shift_after = node_update(totals, node_shift, node_speed)
    moved_rim = upper_rim(shift_after)
    area_after = zone_area(slice_corners(moved_rim))
    conserved = material_state(frac, density, energy, area_now, area_after, mat_pressure, viscous)
    nblocks = keep.shape[2]
    block_len = rows_x * rows_y // nblocks
    fields = 3 * materials
    blocks = conserved.reshape(fields, nblocks, block_len)
    size_x = lax.axis_size("zx")
    size_y = lax.axis_size("zy")
    devices = size_x * size_y
    targets = dest_tile[0, 0, :, 0]
    sources = src_block[0, 0]
    places = dest_block[0, 0]
    weights = crossing[0, 0]
    entry_count = targets.shape[0]
    capacity = max(2, 2 * entry_count // devices)
    member = (targets[:, None] == jnp.arange(devices, dtype=jnp.int32)[None, :]).astype(jnp.int32)
    before = jnp.cumsum(member, axis=0) - member
    slot_rank = jnp.sum(before * member, axis=1)
    slot_index = targets * capacity + slot_rank
    slot_total = devices * capacity
    matches = slot_index[:, None] == jnp.arange(slot_total, dtype=jnp.int32)[None, :]
    filled = jnp.any(matches, axis=0)
    owners = jnp.sum(
        jnp.where(matches, jnp.arange(entry_count, dtype=jnp.int32)[:, None], 0), axis=0
    )
    slot_weight = jnp.where(filled, weights[owners], 0.0)
    slot_place = jnp.where(filled, places[owners], nblocks)
    payload = blocks[:, sources[owners], :] * slot_weight[None, :, None]
    payload = payload.reshape(fields, size_x, size_y, capacity, block_len)
    place_ids = slot_place.reshape(1, size_x, size_y, capacity)
    arrived, arrived_ids = (
        lax.all_to_all(
            lax.all_to_all(payload, "zx", split_axis=1, concat_axis=1, tiled=True),
            "zy",
            split_axis=2,
            concat_axis=2,
            tiled=True,
        ),
        lax.all_to_all(
            lax.all_to_all(place_ids, "zx", split_axis=1, concat_axis=1, tiled=True),
            "zy",
            split_axis=2,
            concat_axis=2,
            tiled=True,
        ),
    )
    arrived = arrived.reshape(fields, slot_total, block_len)
    arrived_ids = arrived_ids.reshape(slot_total)
    landed = (
        jnp.zeros((fields, nblocks + 1, block_len), jnp.float32).at[:, arrived_ids, :].add(arrived)
    )
    result = blocks * keep[0, 0][None, :, None] + landed[:, :nblocks, :]
    remapped = result.reshape(3, materials, rows_x, rows_y)
    return (remapped, speed_after, shift_after)


def solution(mesh):
    in_specs = (
        P(None, "zx", "zy"),
        P(None, "zx", "zy"),
        P(None, "zx", "zy"),
        P(None, "zx", "zy"),
        P(None, "zx", "zy"),
        P("zx", "zy", None, None),
        P("zx", "zy", None),
        P("zx", "zy", None),
        P("zx", "zy", None),
        P("zx", "zy", None),
    )
    out_specs = (P(None, None, "zx", "zy"), P(None, "zx", "zy"), P(None, "zx", "zy"))
    return jax.shard_map(local, mesh=mesh, in_specs=in_specs, out_specs=out_specs, check_vma=False)
```
